128 devices in a mesh: gx: 16 (over y, z), gy: 8 (over x, core).
Axes of the slice: x: 4, y: 4, z: 4, core: 2. Of those that a mesh axis runs over, the one named last changes fastest.
Arguments:
- pressure: float32 [12, 512, 1024], P(None, 'gx', 'gy'), may hold values from 0.5 to 1.5
- saturation: float32 [2, 12, 512, 1024], P(None, None, 'gx', 'gy'), may hold values from 0.05 to 0.35
- permeability: float32 [3, 12, 512, 1024], P(None, None, 'gx', 'gy'), may hold values from 0.25 to 8
- pore_volume: float32 [12, 512, 1024], P(None, 'gx', 'gy'), may hold values from 0.5 to 8
- cell_depth: float32 [12, 512, 1024], P(None, 'gx', 'gy'), may hold values from -4 to 4
- residual: float32 [3, 12, 512, 1024], P(None, None, 'gx', 'gy'), may hold values from -12 to 12
- upstream_flags: int32 [12, 512, 1024], P(None, 'gx', 'gy'), may hold values from 0 to 7
- perf_cell: int32 [128, 1024], P(('gx', 'gy')), may hold values from 0 to 49151
- perf_well: int32 [128, 1024], P(('gx', 'gy')), may hold values from -1 to 4095, as said below
- perf_index: float32 [128, 1024], P(('gx', 'gy')), may hold values from 0.5 to 4
- well_mode: int32 [4096], P(('gx', 'gy')), may hold values from 0 to 1
- well_target: float32 [4096], P(('gx', 'gy')), may hold values from 0.2 to 1.2
Outputs:
- new_pressure: float32 [12, 512, 1024], P(None, 'gx', 'gy')
- well_bhp: float32 [4096], P(('gx', 'gy'))
The draws below stay inside these ranges and needn't reach their ends.
Inputs may be any that keep to these rules, and one draw needn't show every extreme that they name: `upstream_flags`: bit 1 set: the cell is upstream on its face towards the next cell along x; bit 2: along y; bit 4: along z. `perf_cell`: the local cell number, within its row's block of columns, of the perforated cell. `perf_well`: -1 marks an empty slot; in each row the live slots come first; every well has at least one live slot; in every draw some row has all 1024 slots live. `well_mode`: 0: the well holds its bottom-hole pressure at well_target; 1: it produces well_target.
All inputs are finite; a program needn't handle non-finite values.
Results may differ from the reference program's by a relative error of at most 0.0003.
Values sent between devices are 32-bit elements; how exact they have to be, the bound alone decides.
A program may use at most 64 MiB of HBM per device.

```python
import math
import jax
import jax.numpy as jnp
from jax import lax

NZ = 12
CX = 32
CY = 128
W_DEV = 32
PERF_DEV = 1024
SWEEPS = 2
NX = 512
NY = 1024
WELLS = 4096
N_GX = 16
N_GY = 8
DEVICES = 128


def draw_perf_well(key, part):
    subkeys = jax.random.split(jax.random.fold_in(key, 7), 5)
    device_row = jnp.arange(DEVICES, dtype=jnp.int32)[:, None]
    slot_index = jnp.arange(PERF_DEV, dtype=jnp.int32)[None, :]
    drawn_count = jax.random.randint(subkeys[0], (DEVICES, 1), PERF_DEV // 8, PERF_DEV // 4 + 1)
    crowded = jax.random.randint(subkeys[1], (DEVICES, 1), 0, 8)
    fullest = jax.random.randint(subkeys[2], (), 0, DEVICES)
    live_count = jnp.where((crowded == 0) | (device_row == fullest), PERF_DEV, drawn_count)
    well_order = jax.random.permutation(subkeys[3], WELLS).astype(jnp.int32)
    home_well = well_order[device_row * W_DEV + jnp.minimum(slot_index, W_DEV - 1)]
    others = jax.random.randint(subkeys[4], (DEVICES, PERF_DEV), 0, WELLS)
    chosen = jnp.where(slot_index < W_DEV, home_well, others)
    return jnp.where(slot_index < live_count, chosen, -1).astype(jnp.int32)


def with_ends(array, key, smallest, top_value):
    longest = array.shape.index(max(array.shape))
    spots = []
    for shift in (0, 1):
        where = [jax.random.randint(jax.random.fold_in(key, axis), (), 0, length) for axis, length in enumerate(array.shape)]
        where[longest] = (where[longest] + shift) % array.shape[longest]
        spots.append(tuple(where))
    return array.at[spots[0]].set(smallest).at[spots[1]].set(top_value)


def levels(stream_key, dims, cuts, smallest, largest):
    gain, own = 1.0, jax.random.fold_in(stream_key, 6)
    for dim, shards_of in cuts:
        heights = jnp.exp(jax.random.uniform(jax.random.fold_in(own, dim), (shards_of,), jnp.float32, smallest / len(cuts), largest / len(cuts)))
        gain = gain * jnp.repeat(heights, dims[dim] // shards_of).reshape([-1 if axis == dim else 1 for axis in range(len(dims))])
    return gain


def normal_values(own_key, dims, scale, limit, shards=(), held_as=jnp.bfloat16):
    array = scale * jax.random.normal(own_key, dims, jnp.float32)
    if shards:
        array = array * levels(own_key, dims, shards, -0.22, 0.18)
    return jnp.clip(array, -limit, limit).astype(held_as)


def setup_inputs(seed: int = 0) -> dict:
    seeds = jax.random.split(jax.random.key(seed), 13)
    pressure = jnp.clip(0.5 + 1.0 * jax.random.uniform(seeds[0], (NZ, NX, NY), jnp.float32) ** levels(seeds[0], (NZ, NX, NY), ((1, 16), (2, 8)), -0.2, 0.2), 0.5, 1.5)
    saturation = jnp.clip(0.05 + 0.29999999 * jax.random.uniform(seeds[1], (2, NZ, NX, NY), jnp.float32) ** levels(seeds[1], (2, NZ, NX, NY), ((2, 16), (3, 8)), -0.2, 0.2), 0.05, 0.35)
    permeability = jnp.clip(jnp.exp(math.log(8.0) - 3.465736 * jax.random.uniform(seeds[2], (3, NZ, NX, NY), jnp.float32) ** levels(seeds[2], (3, NZ, NX, NY), ((2, 16), (3, 8)), -0.2, 0.2)), 0.25, 8.0)
    pore_volume = jnp.clip(jnp.exp(math.log(8.0) - 2.7725887 * jax.random.uniform(seeds[3], (NZ, NX, NY), jnp.float32) ** levels(seeds[3], (NZ, NX, NY), ((1, 16), (2, 8)), -0.2, 0.2)), 0.5, 8.0)
    cell_depth = normal_values(seeds[4], (NZ, NX, NY), 1.0, 4.0, ((1, 16), (2, 8)), jnp.float32)
    residual = normal_values(seeds[5], (3, NZ, NX, NY), 2.0, 12.0, ((2, 16), (3, 8)), jnp.float32)
    upstream_flags = with_ends(jax.random.randint(seeds[6], (NZ, NX, NY), 0, 8), jax.random.fold_in(seeds[6], 1), 0, 7).astype(jnp.int32)
    perf_cell = with_ends(jax.random.randint(seeds[7], (DEVICES, PERF_DEV), 0, NZ * CX * CY), jax.random.fold_in(seeds[7], 1), 0, (NZ * CX * CY) - 1).astype(jnp.int32)
    perf_well = draw_perf_well(jax.random.fold_in(seeds[12], 71), 0)
    perf_index = jnp.clip(jnp.exp(math.log(4.0) - 2.0794415 * jax.random.uniform(seeds[9], (DEVICES, PERF_DEV), jnp.float32) ** levels(seeds[9], (DEVICES, PERF_DEV), ((0, 128),), -0.2, 0.2)), 0.5, 4.0)
    well_mode = with_ends(jax.random.randint(seeds[10], (WELLS,), 0, 2), jax.random.fold_in(seeds[10], 1), 0, 1).astype(jnp.int32)
    well_target = jnp.clip(0.2 + 1 * jax.random.uniform(seeds[11], (WELLS,), jnp.float32) ** levels(seeds[11], (WELLS,), ((0, 128),), -0.2, 0.2), 0.2, 1.2)
    return {"pressure": pressure, "saturation": saturation, "permeability": permeability, "pore_volume": pore_volume, "cell_depth": cell_depth, "residual": residual, "upstream_flags": upstream_flags, "perf_cell": perf_cell, "perf_well": perf_well, "perf_index": perf_index, "well_mode": well_mode, "well_target": well_target}


MU_OIL = 2.0
MU_WATER = 1.0
MU_GAS = 0.2
COMP_OIL = 0.2
COMP_WATER = 0.05
GRAV_OIL = 0.4
GRAV_WATER = 0.5
GRAV_GAS = 0.08
RELAXATION = 0.8


def phase_weights(pressure):
    b_oil = 1.0 + COMP_OIL * (pressure - 1.0)
    b_water = 1.0 + COMP_WATER * (pressure - 1.0)
    return (1.0 / b_oil, 1.0 / b_water, 1.0 / pressure)


def phase_mobility(pressure, sat_water, sat_gas):
    sat_oil = 1.0 - sat_water - sat_gas
    b_oil = 1.0 + COMP_OIL * (pressure - 1.0)
    b_water = 1.0 + COMP_WATER * (pressure - 1.0)
    return (sat_oil * sat_oil * b_oil / MU_OIL, sat_water * sat_water * b_water / MU_WATER, sat_gas * sat_gas * pressure / MU_GAS)


def storage_term(weights, sat_water, sat_gas):
    sat_oil = 1.0 - sat_water - sat_gas
    return sat_oil * COMP_OIL * weights[0] + sat_water * COMP_WATER * weights[1] + sat_gas * weights[2]


def flag_bits(flag_code):
    bit_x = jnp.mod(flag_code, 2.0)
    remainder = (flag_code - bit_x) * 0.5
    bit_y = jnp.mod(remainder, 2.0)
    return bit_x, bit_y, (remainder - bit_y) * 0.5


def face_terms(weights, mob_center, mob_beside, perm_center, perm_beside, center_up, depth_drop):
    transmit = 2.0 * perm_center * perm_beside / (perm_center + perm_beside)
    coupling = jnp.zeros_like(transmit)
    gravity = jnp.zeros_like(transmit)
    for weight, center, beside, lift_rate in zip(weights, mob_center, mob_beside, (GRAV_OIL, GRAV_WATER, GRAV_GAS)):
        flux_term = weight * (transmit * jnp.where(center_up, center, beside))
        coupling = coupling + flux_term
        gravity = gravity + flux_term * lift_rate
    return coupling, gravity * depth_drop


def direction_terms(weights, center, plus_side, minus_side, bit_center, bit_minus):
    coup_plus, grav_plus = face_terms(weights, center[0], plus_side[0], center[1], plus_side[1], bit_center > 0.5, center[2] - plus_side[2])
    coup_minus, grav_minus = face_terms(weights, center[0], minus_side[0], center[1], minus_side[1], bit_minus < 0.5, center[2] - minus_side[2])
    return (coup_plus, coup_minus), grav_plus + grav_minus


def neighbour(grid_field, axis_dim, offset):
    padding = [(0, 0)] * grid_field.ndim
    padding[axis_dim] = (1, 1)
    padded = jnp.pad(grid_field, padding)
    return lax.slice_in_dim(padded, 1 + offset, 1 + offset + grid_field.shape[axis_dim], axis=axis_dim)


def coupled_sum(couplings, besides):
    running = couplings[0] * besides[0]
    for coupling, beside in zip(couplings[1:], besides[1:]):
        running = running + coupling * beside
    return running


def reference(pressure, saturation, permeability, pore_volume, cell_depth, residual, upstream_flags, perf_cell, perf_well, perf_index, well_mode, well_target):
    sat_water, sat_gas = saturation[0], saturation[1]
    weights = phase_weights(pressure)
    mobility = phase_mobility(pressure, sat_water, sat_gas)
    storage = pore_volume * storage_term(weights, sat_water, sat_gas)
    flag_parts = flag_bits(upstream_flags.astype(jnp.float32))
    couplings = ()
    gravity = jnp.zeros_like(pressure)
    for direction, axis_dim in ((0, 1), (1, 2), (2, 0)):
        center = (mobility, permeability[direction], cell_depth)
        plus_side = (tuple(neighbour(phase_field, axis_dim, 1) for phase_field in mobility), neighbour(permeability[direction], axis_dim, 1), neighbour(cell_depth, axis_dim, 1))
        minus_side = (tuple(neighbour(phase_field, axis_dim, -1) for phase_field in mobility), neighbour(permeability[direction], axis_dim, -1), neighbour(cell_depth, axis_dim, -1))
        coupled, grav_part = direction_terms(weights, center, plus_side, minus_side, flag_parts[direction], neighbour(flag_parts[direction], axis_dim, -1))
        couplings = couplings + coupled
        gravity = gravity + grav_part
    faces_total = couplings[0] + couplings[1] + couplings[2] + couplings[3] + couplings[4] + couplings[5]
    combined = weights[0] * residual[0] + weights[1] * residual[1] + weights[2] * residual[2]
    rhs_base = (storage * pressure - combined) + gravity
    total_mob = weights[0] * mobility[0] + weights[1] * mobility[1] + weights[2] * mobility[2]
    devices_row = jnp.arange(N_GX * N_GY, dtype=jnp.int32)[:, None]
    perf_layer = perf_cell // (CX * CY)
    cell_x = (devices_row // N_GY) * CX + (perf_cell // CY) % CX
    cell_y = (devices_row % N_GY) * CY + perf_cell % CY
    is_live = perf_well >= 0
    well_ids = jnp.where(is_live, perf_well, 0).reshape(-1)
    perf_factor = jnp.where(is_live, perf_index * total_mob[perf_layer, cell_x, cell_y], 0.0)
    well_base = jax.ops.segment_sum(perf_factor.reshape(-1), well_ids, num_segments=WELLS)
    well_diag = jnp.zeros_like(pressure).at[perf_layer, cell_x, cell_y].add(perf_factor)
    total_diag = (storage + faces_total) + well_diag
    current = pressure
    well_bhp = well_target
    for sweep_index in range(SWEEPS):
        at_perf = current[perf_layer, cell_x, cell_y]
        well_part = jax.ops.segment_sum((perf_factor * at_perf).reshape(-1), well_ids, num_segments=WELLS)
        well_bhp = jnp.where(well_mode == 0, well_target, (well_part - well_target) / well_base)
        perf_bhp = perf_factor * well_bhp[well_ids].reshape(perf_factor.shape)
        well_rhs = jnp.zeros_like(pressure).at[perf_layer, cell_x, cell_y].add(perf_bhp)
        besides = (neighbour(current, 1, 1), neighbour(current, 1, -1), neighbour(current, 2, 1), neighbour(current, 2, -1), neighbour(current, 0, 1), neighbour(current, 0, -1))
        current = current + RELAXATION * (((rhs_base + well_rhs) - total_diag * current) + coupled_sum(couplings, besides)) / total_diag
    return current, well_bhp
```

```python
import jax
import jax.numpy as jnp
from jax import lax
from jax.experimental import pallas as pl
from jax.experimental.pallas import tpu as pltpu
from jax.sharding import PartitionSpec as P

MESH = pl.DeviceIdType.MESH
NZ, CX, CY = 12, 32, 128
ROWS = NZ * CX
SLOTS = 1024
NGX, NGY = 16, 8
GAMMA = (0.4, 0.5, 0.08)
F32, BF16 = jnp.float32, jnp.bfloat16
CONTRACT_LAST = (((1,), (1,)), ((), ()))
CONTRACT_FIRST = (((0,), (0,)), ((), ()))


def split(x):
    high = x.astype(BF16)
    return high, (x - high.astype(F32)).astype(BF16)


def phase_state(p, sw, sg):
    so = 1.0 - sw - sg
    bo = 1.0 + 0.2 * (p - 1.0)
    bw = 1.0 + 0.05 * (p - 1.0)
    return so, bo, bw


def kernel(
    p_ref, sat_ref, perm_ref, pv_ref, dep_ref, res_ref, flag_ref, pc_ref, pw_ref, pi_ref, wm_ref, wt_ref,
    out_ref, bhp_ref,
    mob, onehot, fields, spread, wrow, coup, pre, inv, rhs, cur, wacc, slotv,
    table, rs_recv, xs_src, xs_recv, tm_src, tm_recv, ball,
    hx_send, hx_recv, hy_send, hy_recv, halo_y, hx2_send, hx2_recv, hy2_send, hy2_recv,
    rs_ss, rs_rs, xs_ss, xs_rs, tm_ss, tm_rs, bh_ss, bh_rs, h_ss, h_rs,
):
    ix, iy = lax.axis_index("gx"), lax.axis_index("gy")

    def gx_peer(k):
        return (lax.rem(ix + k, NGX), iy)

    def gy_peer(k):
        return (ix, lax.rem(iy + k, NGY))

    barrier = pltpu.get_barrier_semaphore()

    @pl.loop(1, NGX)
    def _(k):
        pl.semaphore_signal(barrier, inc=1, device_id=gx_peer(k), device_id_type=MESH)

    @pl.loop(1, NGY)
    def _(k):
        pl.semaphore_signal(barrier, inc=1, device_id=gy_peer(k), device_id_type=MESH)

    lane = lax.broadcasted_iota(jnp.int32, (CX, CY), 1)
    row = lax.broadcasted_iota(jnp.int32, (CX, CY), 0)

    def rs_copy(t, k):
        return pltpu.make_async_remote_copy(
            src_ref=table.at[t, lax.rem(iy + k, NGY)], dst_ref=rs_recv.at[t, k - 1],
            send_sem=rs_ss.at[t, k - 1], recv_sem=rs_rs.at[t, k - 1],
            device_id=gy_peer(k), device_id_type=MESH)

    def xs_copy(t, k):
        return pltpu.make_async_remote_copy(
            src_ref=xs_src.at[t], dst_ref=xs_recv.at[t, k - 1],
            send_sem=xs_ss.at[t, k - 1], recv_sem=xs_rs.at[t, k - 1],
            device_id=gx_peer(k), device_id_type=MESH)

    def tm_copy(k):
        return pltpu.make_async_remote_copy(
            src_ref=tm_src, dst_ref=tm_recv.at[k - 1],
            send_sem=tm_ss.at[k - 1], recv_sem=tm_rs.at[k - 1],
            device_id=gx_peer(k), device_id_type=MESH)

    def bh_send(t, k):
        return pltpu.make_async_remote_copy(
            src_ref=ball.at[t, iy], dst_ref=ball.at[t, iy],
            send_sem=bh_ss.at[t, k - 1], recv_sem=bh_rs.at[t, k - 1],
            device_id=gy_peer(k), device_id_type=MESH)

    def bh_recv(t, k):
        other = lax.rem(iy + NGY - k, NGY)
        return pltpu.make_async_remote_copy(
            src_ref=ball.at[t, other], dst_ref=ball.at[t, other],
            send_sem=bh_ss.at[t, k - 1], recv_sem=bh_rs.at[t, k - 1],
            device_id=gy_peer(k), device_id_type=MESH)

    def halo_copies(xs, xr, ys, yr, base):
        def one(src, dst, n, dev):
            return pltpu.make_async_remote_copy(
                src_ref=src, dst_ref=dst, send_sem=h_ss.at[base + n], recv_sem=h_rs.at[base + n],
                device_id=dev, device_id_type=MESH)
        return (
            one(xs.at[1], xr.at[0], 0, gx_peer(1)),
            one(xs.at[0], xr.at[1], 1, gx_peer(NGX - 1)),
            one(ys.at[1], yr.at[0], 2, gy_peer(1)),
            one(ys.at[0], yr.at[1], 3, gy_peer(NGY - 1)),
        )

    halo1 = halo_copies(hx_send, hx_recv, hy_send, hy_recv, 0)
    halo2 = halo_copies(hx2_send, hx2_recv, hy2_send, hy2_recv, 4)

    @pl.loop(0, NZ)
    def _(z):
        p, sw, sg = p_ref[z], sat_ref[0, z], sat_ref[1, z]
        so, bo, bw = phase_state(p, sw, sg)
        so2, sw2, sg2 = so * so * 0.5, sw * sw, sg * sg * 5.0
        m = (so2 * bo, sw2 * bw, sg2 * p)
        for c in range(3):
            mob[c, z] = m[c]
        total = so2 + sw2 + sg2
        rows = pl.ds(pl.multiple_of(z * CX, CX), CX)
        for n, part in enumerate(split(total) + split(p)):
            fields[rows, n * CY:(n + 1) * CY] = part
        flags = flag_ref[z]
        bit_x = (flags & 1).astype(F32)
        bit_y = ((flags >> 1) & 1).astype(F32)
        dep = dep_ref[z]
        xf = m + (perm_ref[0, z], dep, bit_x, p)
        yf = m + (perm_ref[1, z], dep, bit_y, p)
        for n, f in enumerate(xf):
            hx_send[0, z, n:n + 1, :] = f[0:1, :]
            hx_send[1, z, n:n + 1, :] = f[CX - 1:CX, :]
        hx_send[0, z, 7:8, :] = jnp.zeros((1, CY), F32)
        hx_send[1, z, 7:8, :] = jnp.zeros((1, CY), F32)
        packed = jnp.zeros((CX, CY), F32)
        for n, f in enumerate(yf):
            packed = jnp.where(lane == n, pltpu.roll(f, (n + 1) % CY, 1), packed)
            packed = jnp.where(lane == 8 + n, pltpu.roll(f, 8 + n, 1), packed)
        halo_y[z] = packed

    cell = pc_ref[...]
    cell_row, cell_lane = cell >> 7, cell & 127
    live = pw_ref[...] >= 0
    well = jnp.where(live, pw_ref[...], 0)
    well_row = ((well >> 5) & 7) * 8 + (well >> 10)
    well_lane = ((well >> 8) & 3) * 32 + (well & 31)
    slotv[0:1, :] = jnp.where(live, pi_ref[...], 0.0)

    @pl.loop(0, NZ)
    def _(z):
        ids = lax.broadcasted_iota(jnp.int32, (CX, SLOTS), 0) + z * CX
        onehot[pl.ds(pl.multiple_of(z * CX, CX), CX), :] = jnp.where(ids == cell_row, 1.0, 0.0).astype(BF16)

    well_ids = lax.broadcasted_iota(jnp.int32, (64, SLOTS), 0)
    wrow[0:64, :] = jnp.where(well_ids == well_row, 1.0, 0.0).astype(BF16)
    wrow[64:128, :] = jnp.where(well_ids == well_row + 4, 1.0, 0.0).astype(BF16)

    sub256 = lax.broadcasted_iota(jnp.int32, (CY, 256), 0)

    def lane_rows(ref_row, chunk):
        if ref_row == 0:
            ids = pc_ref[0:1, chunk] & 127
        else:
            w = jnp.maximum(pw_ref[0:1, chunk], 0)
            ids = ((w >> 8) & 3) * 32 + (w & 31)
        return ids

    def picked(operand, rows_ref, which, count, dst):
        @pl.loop(0, SLOTS // 256)
        def _(j):
            chunk = pl.ds(pl.multiple_of(j * 256, 256), 256)
            g = lax.dot_general(operand, rows_ref[0:operand.shape[0], chunk], CONTRACT_FIRST, preferred_element_type=F32)
            mask = sub256 == lane_rows(which, chunk)
            for n in range(count):
                both = g[2 * n * CY:(2 * n + 1) * CY] + g[(2 * n + 1) * CY:(2 * n + 2) * CY]
                slotv[dst + n:dst + n + 1, chunk] = jnp.sum(jnp.where(mask, both, 0.0), axis=0, keepdims=True)

    def spread_lanes(value_row, which, base):
        @pl.loop(0, SLOTS // 256)
        def _(j):
            chunk = pl.ds(pl.multiple_of(j * 256, 256), 256)
            v = jnp.where(sub256 == lane_rows(which, chunk), slotv[value_row:value_row + 1, chunk], 0.0)
            high, low = split(v)
            spread[base:base + CY, chunk] = high
            spread[base + CY:base + 2 * CY, chunk] = low

    def scatter_cells(value_row):
        spread_lanes(value_row, 0, 0)
        both = lax.dot_general(onehot[...], spread[0:256, :], CONTRACT_LAST, preferred_element_type=F32)
        wacc[...] = both[:, 0:CY] + both[:, CY:2 * CY]

    def well_sums(value_row, with_base):
        spread_lanes(value_row, 1, 0)
        both = lax.dot_general(wrow[0:64, :], spread[0:256, :], CONTRACT_LAST, preferred_element_type=F32)
        if with_base:
            spread_lanes(1, 1, 256)
            both = both + lax.dot_general(wrow[64:128, :], spread[256:512, :], CONTRACT_LAST, preferred_element_type=F32)
        sums = both[:, 0:CY] + both[:, CY:2 * CY]
        return sums.reshape(NGY, 8, CY)

    picked(fields[...], onehot, 0, 2, 4)
    factor = slotv[0:1, :] * slotv[4:5, :]
    slotv[1:2, :] = factor
    slotv[2:3, :] = factor * slotv[5:6, :]
    table[0] = well_sums(2, True)

    quarter = lax.broadcasted_iota(jnp.int32, (8, CY), 1) // 32
    line = lax.broadcasted_iota(jnp.int32, (8, CY), 0)
    own = (quarter == lax.rem(ix, 4)) & (line % 4 == ix // 4)
    target4 = jnp.concatenate([wt_ref[...]] * 4, axis=1)
    mode4 = jnp.concatenate([wm_ref[...].astype(F32)] * 4, axis=1)
    controls = jnp.where(line < 4, jnp.broadcast_to(target4, (8, CY)), jnp.broadcast_to(mode4, (8, CY)))
    tm_src[...] = jnp.where(own, controls, 0.0)

    pl.semaphore_wait(barrier, NGX + NGY - 2)

    def send_table(t):
        @pl.loop(1, NGY)
        def _(k):
            rs_copy(t, k).start()

    def exchange(t):
        @pl.loop(1, NGY)
        def _(k):
            rs_copy(t, k).wait_recv()
        part = table[t, iy]
        for k in range(NGY - 1):
            part = part + rs_recv[t, k]
        xs_src[t] = part

        @pl.loop(1, NGX)
        def _(k):
            xs_copy(t, k).start()

    def finish_sums(t):
        @pl.loop(1, NGX)
        def _(k):
            xs_copy(t, k).wait_recv()
        total = xs_src[t]
        for k in range(NGX - 1):
            total = total + xs_recv[t, k]
        return total

    def share_bhp(t, value):
        ball[t, iy] = value

        @pl.loop(1, NGY)
        def _(k):
            bh_send(t, k).start()

        @pl.loop(1, NGY)
        def _(k):
            bh_recv(t, k).wait_recv()

    send_table(0)

    @pl.loop(1, NGX)
    def _(k):
        tm_copy(k).start()

    turned = halo_y[...].reshape(ROWS, CY).T
    hy_send[1] = turned[0:8, :]
    hy_send[0] = turned[8:16, :]
    for copy in halo1:
        copy.start()

    exchange(0)

    scatter_cells(1)
    for copy in halo1:
        copy.wait_recv()
    stacked = jnp.concatenate([hy_recv[0], hy_recv[1], jnp.zeros((CY - 16, ROWS), F32)], axis=0)
    halo_y[...] = stacked.T.reshape(NZ, CX, CY)

    def face(w, m, n, k, kn, up, drop):
        trans = 2.0 * k * kn / (k + kn)
        c = jnp.zeros((CX, CY), F32)
        g = jnp.zeros((CX, CY), F32)
        for i in range(3):
            flux = w[i] * jnp.where(up, m[i], n[i])
            c = c + flux
            g = g + GAMMA[i] * flux
        c = c * trans
        return c, g * (trans * drop)

    @pl.loop(0, NZ)
    def _(z):
        p, sw, sg = p_ref[z], sat_ref[0, z], sat_ref[1, z]
        so, bo, bw = phase_state(p, sw, sg)
        w = (1.0 / bo, 1.0 / bw, 1.0 / p)
        m = (mob[0, z], mob[1, z], mob[2, z])
        dep = dep_ref[z]
        flags = flag_ref[z]
        storage = pv_ref[z] * (so * 0.2 * w[0] + sw * 0.05 * w[1] + sg * w[2])
        lift = jnp.zeros((CX, CY), F32)
        faces = jnp.zeros((CX, CY), F32)
        beside = jnp.zeros((CX, CY), F32)

        def add(n, lift, faces, beside, c, g, pn):
            coup[n, z] = c
            return lift + g, faces + c, beside + c * pn

        for side in range(2):
            halo = hx_recv[side, z]
            edge = 0 if side == 0 else CX - 1
            inside = (ix > 0) if side == 0 else (ix < NGX - 1)

            def shifted(f, n):
                return jnp.where(row == edge, jnp.broadcast_to(halo[n:n + 1, :], (CX, CY)), pltpu.roll(f, 1 if side == 0 else CX - 1, 0))
            k = perm_ref[0, z]
            kn = shifted(k, 3)
            kn = jnp.where((row == edge) & jnp.logical_not(inside), 0.0, kn)
            if side == 0:
                up = shifted((flags & 1).astype(F32), 5) < 0.5
            else:
                up = (flags & 1) == 1
            c, g = face(w, m, tuple(shifted(m[i], i) for i in range(3)), k, kn, up, dep - shifted(dep, 4))
            lift, faces, beside = add(side, lift, faces, beside, c, g, shifted(p, 6))

        pack = halo_y[z]
        for side in range(2):
            edge = 0 if side == 0 else CY - 1
            inside = (iy > 0) if side == 0 else (iy < NGY - 1)

            def shifted(f, n):
                moved = pltpu.roll(pack, (CY - n) % CY if side == 0 else CY - 1 - 8 - n, 1)
                return jnp.where(lane == edge, moved, pltpu.roll(f, 1 if side == 0 else CY - 1, 1))
            k = perm_ref[1, z]
            kn = shifted(k, 3)
            kn = jnp.where((lane == edge) & jnp.logical_not(inside), 0.0, kn)
            if side == 0:
                up = shifted(((flags >> 1) & 1).astype(F32), 5) < 0.5
            else:
                up = ((flags >> 1) & 1) == 1
            c, g = face(w, m, tuple(shifted(m[i], i) for i in range(3)), k, kn, up, dep - shifted(dep, 4))
            lift, faces, beside = add(2 + side, lift, faces, beside, c, g, shifted(p, 6))

        for side in range(2):
            zn = jnp.maximum(z - 1, 0) if side == 0 else jnp.minimum(z + 1, NZ - 1)
            inside = (z > 0) if side == 0 else (z < NZ - 1)
            k = perm_ref[2, z]
            kn = jnp.where(inside, perm_ref[2, zn], 0.0)
            if side == 0:
                up = (flag_ref[zn] >> 2) == 0
            else:
                up = (flags >> 2) == 1
            c, g = face(w, m, (mob[0, zn], mob[1, zn], mob[2, zn]), k, kn, up, dep - dep_ref[zn])
            lift, faces, beside = add(4 + side, lift, faces, beside, c, g, p_ref[zn])

        combined = w[0] * res_ref[0, z] + w[1] * res_ref[1, z] + w[2] * res_ref[2, z]
        b = storage * p - combined + lift
        rows = pl.ds(pl.multiple_of(z * CX, CX), CX)
        damp = 0.8 / (storage + faces + wacc[rows, :])
        rhs[z] = b
        inv[z] = damp
        pre[z] = 0.2 * p + damp * (b + beside)

    @pl.loop(1, NGX)
    def _(k):
        tm_copy(k).wait_recv()
    controls = tm_src[...]
    for k in range(NGX - 1):
        controls = controls + tm_recv[k]
    mode = pltpu.roll(controls, 4, 0)

    def bhp_of(sums, base):
        value = jnp.where(mode < 0.5, controls, (sums - controls) / base)
        return jnp.where(line < 4, value, 0.0)

    def apply_bhp(t):
        wells = ball[t].reshape(64, CY)
        high, low = split(wells)
        picked(jnp.concatenate([high, low], axis=1), wrow, 1, 1, 3)
        slotv[2:3, :] = slotv[1:2, :] * slotv[3:4, :]
        scatter_cells(2)

    sums = finish_sums(0)
    base = pltpu.roll(sums, 4, 0)
    share_bhp(0, bhp_of(sums, base))
    apply_bhp(0)

    @pl.loop(0, NZ)
    def _(z):
        rows = pl.ds(pl.multiple_of(z * CX, CX), CX)
        c = pre[z] + inv[z] * wacc[rows, :]
        cur[z] = c
        for n, part in enumerate(split(c)):
            fields[rows, n * CY:(n + 1) * CY] = part
        hx2_send[0, z] = c[0:1, :]
        hx2_send[1, z] = c[CX - 1:CX, :]
        packed = jnp.where(lane == 0, pltpu.roll(c, 1, 1), 0.0)
        halo_y[z] = jnp.where(lane == 8, pltpu.roll(c, 8, 1), packed)

    picked(fields[:, 0:256], onehot, 0, 1, 5)
    slotv[2:3, :] = slotv[1:2, :] * slotv[5:6, :]
    table[1] = well_sums(2, False)
    send_table(1)
    turned = halo_y[...].reshape(ROWS, CY).T
    hy2_send[1] = turned[0:8, :]
    hy2_send[0] = turned[8:16, :]
    for copy in halo2:
        copy.start()
    exchange(1)

    for copy in halo2:
        copy.wait_recv()
    stacked = jnp.concatenate([hy2_recv[0], hy2_recv[1], jnp.zeros((CY - 16, ROWS), F32)], axis=0)
    halo_y[...] = stacked.T.reshape(NZ, CX, CY)

    @pl.loop(0, NZ)
    def _(z):
        c = cur[z]
        pack = halo_y[z]
        up_x = jnp.where(row == 0, jnp.broadcast_to(hx2_recv[0, z], (CX, CY)), pltpu.roll(c, 1, 0))
        down_x = jnp.where(row == CX - 1, jnp.broadcast_to(hx2_recv[1, z], (CX, CY)), pltpu.roll(c, CX - 1, 0))
        up_y = jnp.where(lane == 0, pack, pltpu.roll(c, 1, 1))
        down_y = jnp.where(lane == CY - 1, pltpu.roll(pack, CY - 9, 1), pltpu.roll(c, CY - 1, 1))
        up_z, down_z = cur[jnp.maximum(z - 1, 0)], cur[jnp.minimum(z + 1, NZ - 1)]
        total = rhs[z]
        for n, value in enumerate((up_x, down_x, up_y, down_y, up_z, down_z)):
            total = total + coup[n, z] * value
        pre[z] = 0.2 * c + inv[z] * total

    value = bhp_of(finish_sums(1), base)
    share_bhp(1, value)
    apply_bhp(1)

    @pl.loop(0, NZ)
    def _(z):
        rows = pl.ds(pl.multiple_of(z * CX, CX), CX)
        out_ref[z] = pre[z] + inv[z] * wacc[rows, :]

    mine = jnp.sum(jnp.where(own & (line < 4), value, 0.0), axis=0, keepdims=True)
    mine = jnp.broadcast_to(mine, (8, CY))
    mine = mine + pltpu.roll(mine, 32, 1) + pltpu.roll(mine, 64, 1) + pltpu.roll(mine, 96, 1)
    bhp_ref[...] = mine[0:1, 0:32]

    for t in range(2):
        @pl.loop(1, NGY)
        def _(k):
            rs_copy(t, k).wait_send()
            bh_send(t, k).wait_send()

        @pl.loop(1, NGX)
        def _(k):
            xs_copy(t, k).wait_send()

    @pl.loop(1, NGX)
    def _(k):
        tm_copy(k).wait_send()
    for copy in halo1 + halo2:
        copy.wait_send()


def body(pressure, saturation, permeability, pore_volume, cell_depth, residual, upstream_flags,
         perf_cell, perf_well, perf_index, well_mode, well_target):
    grid = (NZ, CX, CY)
    vmem = pl.BlockSpec(memory_space=pltpu.VMEM)
    dma = pltpu.SemaphoreType.DMA
    new_pressure, well_bhp = pl.pallas_call(
        kernel,
        out_shape=(jax.ShapeDtypeStruct(grid, F32), jax.ShapeDtypeStruct((1, 32), F32)),
        in_specs=[vmem] * 12,
        out_specs=(vmem, vmem),
        scratch_shapes=[
            pltpu.VMEM((3,) + grid, F32),
            pltpu.VMEM((ROWS, SLOTS), BF16),
            pltpu.VMEM((ROWS, 4 * CY), BF16),
            pltpu.VMEM((4 * CY, SLOTS), BF16),
            pltpu.VMEM((128, SLOTS), BF16),
            pltpu.VMEM((6,) + grid, F32),
            pltpu.VMEM(grid, F32),
            pltpu.VMEM(grid, F32),
            pltpu.VMEM(grid, F32),
            pltpu.VMEM(grid, F32),
            pltpu.VMEM((ROWS, CY), F32),
            pltpu.VMEM((8, SLOTS), F32),
            pltpu.VMEM((2, NGY, 8, CY), F32),
            pltpu.VMEM((2, NGY - 1, 8, CY), F32),
            pltpu.VMEM((2, 8, CY), F32),
            pltpu.VMEM((2, NGX - 1, 8, CY), F32),
            pltpu.VMEM((8, CY), F32),
            pltpu.VMEM((NGX - 1, 8, CY), F32),
            pltpu.VMEM((2, NGY, 8, CY), F32),
            pltpu.VMEM((2, NZ, 8, CY), F32),
            pltpu.VMEM((2, NZ, 8, CY), F32),
            pltpu.VMEM((2, 8, ROWS), F32),
            pltpu.VMEM((2, 8, ROWS), F32),
            pltpu.VMEM(grid, F32),
            pltpu.VMEM((2, NZ, 1, CY), F32),
            pltpu.VMEM((2, NZ, 1, CY), F32),
            pltpu.VMEM((2, 8, ROWS), F32),
            pltpu.VMEM((2, 8, ROWS), F32),
            dma((2, NGY - 1)), dma((2, NGY - 1)),
            dma((2, NGX - 1)), dma((2, NGX - 1)),
            dma((NGX - 1,)), dma((NGX - 1,)),
            dma((2, NGY - 1)), dma((2, NGY - 1)),
            dma((8,)), dma((8,)),
        ],
        compiler_params=pltpu.CompilerParams(collective_id=0, has_side_effects=True),
        name="cpr_step",
    )(pressure, saturation, permeability, pore_volume, cell_depth, residual, upstream_flags,
      perf_cell, perf_well, perf_index, well_mode.reshape(1, 32), well_target.reshape(1, 32))
    return new_pressure, well_bhp.reshape(32)


def solution(mesh):
    areal, stacked, owned = P(None, "gx", "gy"), P(None, None, "gx", "gy"), P(("gx", "gy"))
    slots = P(("gx", "gy"), None)
    return jax.shard_map(
        body,
        mesh=mesh,
        in_specs=(areal, stacked, stacked, areal, areal, stacked, areal, slots, slots, slots, owned, owned),
        out_specs=(areal, owned),
        check_vma=False,
    )
```

```python
import jax
import jax.numpy as jnp
from jax import lax
from jax.experimental import pallas as pl
from jax.experimental.pallas import tpu as pltpu
from jax.sharding import PartitionSpec as P

MESH = pl.DeviceIdType.MESH
NZ, CX, CY = 12, 32, 128
ROWS = NZ * CX
SLOTS = 1024
NGX, NGY = 16, 8
GAMMA = (0.4, 0.5, 0.08)
F32, BF16 = jnp.float32, jnp.bfloat16
CONTRACT_LAST = (((1,), (1,)), ((), ()))
CONTRACT_FIRST = (((0,), (0,)), ((), ()))


def split(x):
    high = x.astype(BF16)
    return high, (x - high.astype(F32)).astype(BF16)


def phase_state(p, sw, sg):
    so = 1.0 - sw - sg
    bo = 1.0 + 0.2 * (p - 1.0)
    bw = 1.0 + 0.05 * (p - 1.0)
    return so, bo, bw


def hops(offset, size):
    return min(offset, size - offset)


GX_OFFSETS = sorted(((a, b) for a in range(4) for b in range(4) if a or b), key=lambda o: -hops(o[0], 4) - hops(o[1], 4))
GY_OFFSETS = sorted(((a, b) for a in range(4) for b in range(2) if a or b), key=lambda o: -2 * hops(o[0], 4) - o[1])


def kernel(
    p_hbm, sat_hbm, perm_hbm, pv_hbm, dep_hbm, res_hbm, flag_hbm, pc_hbm, pw_hbm, pi_hbm, wm_hbm, wt_hbm,
    out_ref, bhp_ref,
    p_ref, sat_ref, perm_ref, pv_ref, dep_ref, res_ref, flag_ref, pc_ref, pw_ref, pi_ref, wm_ref, wt_ref,
    mob, onehot, fields, spread, wrow, same, coup, pre, inv, rhs, cur, wacc, slotv,
    table, rs_recv, xs_src, xs_recv, tm_src, tm_recv, ball,
    hx_send, hx_recv, hy_send, hy_recv, halo_y, hx2_send, hx2_recv, hy2_send, hy2_recv,
    in_sem, rs_ss, rs_rs, xs_ss, xs_rs, tm_ss, tm_rs, bh_ss, bh_rs, h_ss, h_rs,
):
    ix, iy = lax.axis_index("gx"), lax.axis_index("gy")
    chip_y, chip_z = ix // 4, lax.rem(ix, 4)
    chip_x, core = iy // 2, lax.rem(iy, 2)

    def gx_of(a, b):
        return lax.rem(chip_y + a, 4) * 4 + lax.rem(chip_z + b, 4)

    def gy_of(a, b):
        return lax.rem(chip_x + a, 4) * 2 + lax.rem(core + b, 2)

    barrier = pltpu.get_barrier_semaphore()
    for a, b in GX_OFFSETS:
        pl.semaphore_signal(barrier, inc=1, device_id=(gx_of(a, b), iy), device_id_type=MESH)
    for a, b in GY_OFFSETS:
        pl.semaphore_signal(barrier, inc=1, device_id=(ix, gy_of(a, b)), device_id_type=MESH)

    loads = {}
    pairs = (("pc", pc_hbm, pc_ref), ("pw", pw_hbm, pw_ref), ("pi", pi_hbm, pi_ref), ("sat", sat_hbm, sat_ref),
             ("p", p_hbm, p_ref), ("perm", perm_hbm, perm_ref), ("dep", dep_hbm, dep_ref), ("flag", flag_hbm, flag_ref),
             ("wm", wm_hbm, wm_ref), ("wt", wt_hbm, wt_ref), ("pv", pv_hbm, pv_ref), ("res", res_hbm, res_ref))
    for n, (name, src, dst) in enumerate(pairs):
        loads[name] = pltpu.make_async_copy(src, dst, in_sem.at[n])
        loads[name].start()

    lane = lax.broadcasted_iota(jnp.int32, (CX, CY), 1)
    row = lax.broadcasted_iota(jnp.int32, (CX, CY), 0)

    def remote(src, dst, ss, rs, dev):
        return pltpu.make_async_remote_copy(src_ref=src, dst_ref=dst, send_sem=ss, recv_sem=rs,
                                            device_id=dev, device_id_type=MESH)

    def rs_copies(t):
        return [remote(table.at[t, gy_of(a, b)], rs_recv.at[t, n], rs_ss.at[t, n], rs_rs.at[t, n], (ix, gy_of(a, b)))
                for n, (a, b) in enumerate(GY_OFFSETS)]

    def xs_copies(t):
        return [remote(xs_src.at[t], xs_recv.at[t, n], xs_ss.at[t, n], xs_rs.at[t, n], (gx_of(a, b), iy))
                for n, (a, b) in enumerate(GX_OFFSETS)]

    tm_copies = [remote(tm_src, tm_recv.at[n], tm_ss.at[n], tm_rs.at[n], (gx_of(a, b), iy))
                 for n, (a, b) in enumerate(GX_OFFSETS)]

    def bh_sends(t):
        return [remote(ball.at[t, iy], ball.at[t, iy], bh_ss.at[t, n], bh_rs.at[t, n], (ix, gy_of(a, b)))
                for n, (a, b) in enumerate(GY_OFFSETS)]

    def bh_recvs(t):
        return [remote(ball.at[t, gy_of((4 - a) % 4, b)], ball.at[t, gy_of((4 - a) % 4, b)], bh_ss.at[t, n], bh_rs.at[t, n],
                       (ix, gy_of(a, b)))
                for n, (a, b) in enumerate(GY_OFFSETS)]

    def halo_copies(xs, xr, ys, yr, base):
        return (
            remote(xs.at[1], xr.at[0], h_ss.at[base], h_rs.at[base], (lax.rem(ix + 1, NGX), iy)),
            remote(xs.at[0], xr.at[1], h_ss.at[base + 1], h_rs.at[base + 1], (lax.rem(ix + NGX - 1, NGX), iy)),
            remote(ys.at[1], yr.at[0], h_ss.at[base + 2], h_rs.at[base + 2], (ix, lax.rem(iy + 1, NGY))),
            remote(ys.at[0], yr.at[1], h_ss.at[base + 3], h_rs.at[base + 3], (ix, lax.rem(iy + NGY - 1, NGY))),
        )

    halo1 = halo_copies(hx_send, hx_recv, hy_send, hy_recv, 0)
    halo2 = halo_copies(hx2_send, hx2_recv, hy2_send, hy2_recv, 4)

    for name in ("pc", "pw", "pi"):
        loads[name].wait()
    cell = pc_ref[...]
    cell_row = cell >> 7
    live = pw_ref[...] >= 0
    well = jnp.where(live, pw_ref[...], 0)
    well_row = ((well >> 5) & 7) * 8 + (well >> 10)
    slotv[0:1, :] = jnp.where(live, pi_ref[...], 0.0)

    @pl.loop(0, NZ)
    def _(z):
        ids = lax.broadcasted_iota(jnp.int32, (CX, SLOTS), 0) + z * CX
        onehot[pl.ds(pl.multiple_of(z * CX, CX), CX), :] = jnp.where(ids == cell_row, 1.0, 0.0).astype(BF16)

    well_ids = lax.broadcasted_iota(jnp.int32, (64, SLOTS), 0)
    wrow[0:64, :] = jnp.where(well_ids == well_row, 1.0, 0.0).astype(BF16)
    wrow[64:128, :] = jnp.where(well_ids == well_row + 4, 1.0, 0.0).astype(BF16)

    loads["sat"].wait()
    loads["p"].wait()

    @pl.loop(0, NZ)
    def _(z):
        sw, sg = sat_ref[0, z], sat_ref[1, z]
        so = 1.0 - sw - sg
        total = so * so * 0.5 + sw * sw + sg * sg * 5.0
        rows = pl.ds(pl.multiple_of(z * CX, CX), CX)
        for n, part in enumerate(split(total) + split(p_ref[z])):
            fields[rows, n * CY:(n + 1) * CY] = part

    sub256 = lax.broadcasted_iota(jnp.int32, (CY, 256), 0)

    def lane_rows(ref_row, chunk):
        if ref_row == 0:
            ids = pc_ref[0:1, chunk] & 127
        else:
            w = jnp.maximum(pw_ref[0:1, chunk], 0)
            ids = ((w >> 8) & 3) * 32 + (w & 31)
        return ids

    def picked(operand, rows_ref, which, count, dst):
        for j in range(SLOTS // 256):
            chunk = slice(j * 256, (j + 1) * 256)
            g = lax.dot_general(operand, rows_ref[0:operand.shape[0], chunk], CONTRACT_FIRST, preferred_element_type=F32)
            mask = sub256 == lane_rows(which, chunk)
            for n in range(count):
                both = g[2 * n * CY:(2 * n + 1) * CY] + g[(2 * n + 1) * CY:(2 * n + 2) * CY]
                slotv[dst + n:dst + n + 1, chunk] = jnp.sum(jnp.where(mask, both, 0.0), axis=0, keepdims=True)

    def spread_lanes(value_row, which, base):
        for j in range(SLOTS // 256):
            chunk = slice(j * 256, (j + 1) * 256)
            v = jnp.where(sub256 == lane_rows(which, chunk), slotv[value_row:value_row + 1, chunk], 0.0)
            high, low = split(v)
            spread[base:base + CY, chunk] = high
            spread[base + CY:base + 2 * CY, chunk] = low

    def scatter_cells(value_row):
        spread_lanes(value_row, 0, 0)
        both = lax.dot_general(onehot[...], spread[0:256, :], CONTRACT_LAST, preferred_element_type=F32)
        wacc[...] = both[:, 0:CY] + both[:, CY:2 * CY]

    def well_sums(value_row, with_base):
        spread_lanes(value_row, 1, 0)
        both = lax.dot_general(wrow[0:64, :], spread[0:256, :], CONTRACT_LAST, preferred_element_type=F32)
        if with_base:
            spread_lanes(1, 1, 256)
            both = both + lax.dot_general(wrow[64:128, :], spread[256:512, :], CONTRACT_LAST, preferred_element_type=F32)
        sums = both[:, 0:CY] + both[:, CY:2 * CY]
        return sums.reshape(NGY, 8, CY)

    picked(fields[...], onehot, 0, 2, 4)
    factor = slotv[0:1, :] * slotv[4:5, :]
    slotv[1:2, :] = factor
    slotv[2:3, :] = factor * slotv[5:6, :]
    table[0] = well_sums(2, True)

    pl.semaphore_wait(barrier, NGX + NGY - 2)

    def send(copies):
        for copy in copies:
            copy.start()

    def arrive(copies):
        for copy in copies:
            copy.wait_recv()

    def exchange(t):
        arrive(rs_copies(t))
        part = table[t, iy]
        for n in range(NGY - 1):
            part = part + rs_recv[t, n]
        xs_src[t] = part
        send(xs_copies(t))

    def finish_sums(t):
        arrive(xs_copies(t))
        total = xs_src[t]
        for n in range(NGX - 1):
            total = total + xs_recv[t, n]
        return total

    send(rs_copies(0))

    for name in ("perm", "dep", "flag", "wm", "wt"):
        loads[name].wait()

    @pl.loop(0, NZ)
    def _(z):
        p, sw, sg = p_ref[z], sat_ref[0, z], sat_ref[1, z]
        so, bo, bw = phase_state(p, sw, sg)
        so2, sw2, sg2 = so * so * 0.5, sw * sw, sg * sg * 5.0
        m = (so2 * bo, sw2 * bw, sg2 * p)
        for c in range(3):
            mob[c, z] = m[c]
        flags = flag_ref[z]
        bit_x = (flags & 1).astype(F32)
        bit_y = ((flags >> 1) & 1).astype(F32)
        dep = dep_ref[z]
        xf = m + (perm_ref[0, z], dep, bit_x, p)
        yf = m + (perm_ref[1, z], dep, bit_y, p)
        for n, f in enumerate(xf):
            hx_send[0, z, n:n + 1, :] = f[0:1, :]
            hx_send[1, z, n:n + 1, :] = f[CX - 1:CX, :]
        hx_send[0, z, 7:8, :] = jnp.zeros((1, CY), F32)
        hx_send[1, z, 7:8, :] = jnp.zeros((1, CY), F32)
        packed = jnp.zeros((CX, CY), F32)
        for n, f in enumerate(yf):
            packed = jnp.where(lane == n, pltpu.roll(f, (n + 1) % CY, 1), packed)
            packed = jnp.where(lane == 8 + n, pltpu.roll(f, 8 + n, 1), packed)
        halo_y[z] = packed

    quarter = lax.broadcasted_iota(jnp.int32, (8, CY), 1) // 32
    line = lax.broadcasted_iota(jnp.int32, (8, CY), 0)
    own = (quarter == lax.rem(ix, 4)) & (line % 4 == ix // 4)
    target4 = jnp.concatenate([wt_ref[...]] * 4, axis=1)
    mode4 = jnp.concatenate([wm_ref[...].astype(F32)] * 4, axis=1)
    controls = jnp.where(line < 4, jnp.broadcast_to(target4, (8, CY)), jnp.broadcast_to(mode4, (8, CY)))
    tm_src[...] = jnp.where(own, controls, 0.0)

    send(tm_copies)
    turned = halo_y[...].reshape(ROWS, CY).T
    hy_send[1] = turned[0:8, :]
    hy_send[0] = turned[8:16, :]
    send(halo1)
    exchange(0)

    scatter_cells(1)
    for name in ("pv", "res"):
        loads[name].wait()
    arrive(halo1)
    stacked = jnp.concatenate([hy_recv[0], hy_recv[1], jnp.zeros((CY - 16, ROWS), F32)], axis=0)
    halo_y[...] = stacked.T.reshape(NZ, CX, CY)

    def face(w, m, n, k, kn, up, drop):
        trans = 2.0 * k * kn / (k + kn)
        c = jnp.zeros((CX, CY), F32)
        g = jnp.zeros((CX, CY), F32)
        for i in range(3):
            flux = w[i] * jnp.where(up, m[i], n[i])
            c = c + flux
            g = g + GAMMA[i] * flux
        c = c * trans
        return c, g * (trans * drop)

    @pl.loop(0, NZ)
    def _(z):
        p, sw, sg = p_ref[z], sat_ref[0, z], sat_ref[1, z]
        so, bo, bw = phase_state(p, sw, sg)
        w = (1.0 / bo, 1.0 / bw, 1.0 / p)
        m = (mob[0, z], mob[1, z], mob[2, z])
        dep = dep_ref[z]
        flags = flag_ref[z]
        storage = pv_ref[z] * (so * 0.2 * w[0] + sw * 0.05 * w[1] + sg * w[2])
        lift = jnp.zeros((CX, CY), F32)
        faces = jnp.zeros((CX, CY), F32)
        beside = jnp.zeros((CX, CY), F32)

        def add(n, lift, faces, beside, c, g, pn):
            coup[n, z] = c
            return lift + g, faces + c, beside + c * pn

        for side in range(2):
            halo = hx_recv[side, z]
            edge = 0 if side == 0 else CX - 1
            inside = (ix > 0) if side == 0 else (ix < NGX - 1)

            def shifted(f, n):
                return jnp.where(row == edge, jnp.broadcast_to(halo[n:n + 1, :], (CX, CY)), pltpu.roll(f, 1 if side == 0 else CX - 1, 0))
            k = perm_ref[0, z]
            kn = shifted(k, 3)
            kn = jnp.where((row == edge) & jnp.logical_not(inside), 0.0, kn)
            if side == 0:
                up = shifted((flags & 1).astype(F32), 5) < 0.5
            else:
                up = (flags & 1) == 1
            c, g = face(w, m, tuple(shifted(m[i], i) for i in range(3)), k, kn, up, dep - shifted(dep, 4))
            lift, faces, beside = add(side, lift, faces, beside, c, g, shifted(p, 6))

        pack = halo_y[z]
        for side in range(2):
            edge = 0 if side == 0 else CY - 1
            inside = (iy > 0) if side == 0 else (iy < NGY - 1)

            def shifted(f, n):
                moved = pltpu.roll(pack, (CY - n) % CY if side == 0 else CY - 1 - 8 - n, 1)
                return jnp.where(lane == edge, moved, pltpu.roll(f, 1 if side == 0 else CY - 1, 1))
            k = perm_ref[1, z]
            kn = shifted(k, 3)
            kn = jnp.where((lane == edge) & jnp.logical_not(inside), 0.0, kn)
            if side == 0:
                up = shifted(((flags >> 1) & 1).astype(F32), 5) < 0.5
            else:
                up = ((flags >> 1) & 1) == 1
            c, g = face(w, m, tuple(shifted(m[i], i) for i in range(3)), k, kn, up, dep - shifted(dep, 4))
            lift, faces, beside = add(2 + side, lift, faces, beside, c, g, shifted(p, 6))

        for side in range(2):
            zn = jnp.maximum(z - 1, 0) if side == 0 else jnp.minimum(z + 1, NZ - 1)
            inside = (z > 0) if side == 0 else (z < NZ - 1)
            k = perm_ref[2, z]
            kn = jnp.where(inside, perm_ref[2, zn], 0.0)
            if side == 0:
                up = (flag_ref[zn] >> 2) == 0
            else:
                up = (flags >> 2) == 1
            c, g = face(w, m, (mob[0, zn], mob[1, zn], mob[2, zn]), k, kn, up, dep - dep_ref[zn])
            lift, faces, beside = add(4 + side, lift, faces, beside, c, g, p_ref[zn])

        combined = w[0] * res_ref[0, z] + w[1] * res_ref[1, z] + w[2] * res_ref[2, z]
        b = storage * p - combined + lift
        rows = pl.ds(pl.multiple_of(z * CX, CX), CX)
        damp = 0.8 / (storage + faces + wacc[rows, :])
        rhs[z] = b
        inv[z] = damp
        pre[z] = 0.2 * p + damp * (b + beside)

    arrive(tm_copies)
    controls = tm_src[...]
    for n in range(NGX - 1):
        controls = controls + tm_recv[n]
    mode = pltpu.roll(controls, 4, 0)

    def bhp_of(sums, base):
        value = jnp.where(mode < 0.5, controls, (sums - controls) / base)
        return jnp.where(line < 4, value, 0.0)

    def slot_flow(t):
        arrive(bh_recvs(t))
        high, low = split(ball[t].reshape(64, CY))
        picked(jnp.concatenate([high, low], axis=1), wrow, 1, 1, 3)
        slotv[2:3, :] = slotv[1:2, :] * slotv[3:4, :]

    sums = finish_sums(0)
    base = pltpu.roll(sums, 4, 0)
    ball[0, iy] = bhp_of(sums, base)
    send(bh_sends(0))

    cells = jnp.broadcast_to(pc_ref[...].astype(F32), (CY, SLOTS)).T

    for j in range(SLOTS // CY):
        chunk = slice(j * CY, (j + 1) * CY)
        same[:, chunk] = jnp.where(cells == pc_ref[0:1, chunk].astype(F32), 1.0, 0.0).astype(BF16)

    @pl.loop(0, NZ)
    def _(z):
        rows = pl.ds(pl.multiple_of(z * CX, CX), CX)
        for n, part in enumerate(split(pre[z]) + split(inv[z])):
            fields[rows, n * CY:(n + 1) * CY] = part

    picked(fields[...], onehot, 0, 2, 4)
    slot_flow(0)
    high, low = split(slotv[2:3, :])
    flow = jnp.concatenate([jnp.broadcast_to(high, (16, SLOTS)), jnp.broadcast_to(low, (16, SLOTS))], axis=0)
    met = jnp.dot(flow, same[...], preferred_element_type=F32)
    slotv[6:7, :] = slotv[1:2, :] * (slotv[4:5, :] + slotv[5:6, :] * (met[0:1, :] + met[16:17, :]))
    table[1] = well_sums(6, False)
    send(rs_copies(1))

    scatter_cells(2)

    @pl.loop(0, NZ)
    def _(z):
        rows = pl.ds(pl.multiple_of(z * CX, CX), CX)
        c = pre[z] + inv[z] * wacc[rows, :]
        cur[z] = c
        hx2_send[0, z] = c[0:1, :]
        hx2_send[1, z] = c[CX - 1:CX, :]
        packed = jnp.where(lane == 0, pltpu.roll(c, 1, 1), 0.0)
        halo_y[z] = jnp.where(lane == 8, pltpu.roll(c, 8, 1), packed)

    turned = halo_y[...].reshape(ROWS, CY).T
    hy2_send[1] = turned[0:8, :]
    hy2_send[0] = turned[8:16, :]
    send(halo2)
    exchange(1)

    arrive(halo2)
    stacked = jnp.concatenate([hy2_recv[0], hy2_recv[1], jnp.zeros((CY - 16, ROWS), F32)], axis=0)
    halo_y[...] = stacked.T.reshape(NZ, CX, CY)

    @pl.loop(0, NZ)
    def _(z):
        c = cur[z]
        pack = halo_y[z]
        up_x = jnp.where(row == 0, jnp.broadcast_to(hx2_recv[0, z], (CX, CY)), pltpu.roll(c, 1, 0))
        down_x = jnp.where(row == CX - 1, jnp.broadcast_to(hx2_recv[1, z], (CX, CY)), pltpu.roll(c, CX - 1, 0))
        up_y = jnp.where(lane == 0, pack, pltpu.roll(c, 1, 1))
        down_y = jnp.where(lane == CY - 1, pltpu.roll(pack, CY - 9, 1), pltpu.roll(c, CY - 1, 1))
        up_z, down_z = cur[jnp.maximum(z - 1, 0)], cur[jnp.minimum(z + 1, NZ - 1)]
        total = rhs[z]
        for n, value in enumerate((up_x, down_x, up_y, down_y, up_z, down_z)):
            total = total + coup[n, z] * value
        pre[z] = 0.2 * c + inv[z] * total

    value = bhp_of(finish_sums(1), base)
    ball[1, iy] = value
    send(bh_sends(1))
    slot_flow(1)
    scatter_cells(2)

    @pl.loop(0, NZ)
    def _(z):
        rows = pl.ds(pl.multiple_of(z * CX, CX), CX)
        out_ref[z] = pre[z] + inv[z] * wacc[rows, :]

    mine = jnp.sum(jnp.where(own & (line < 4), value, 0.0), axis=0, keepdims=True)
    mine = jnp.broadcast_to(mine, (8, CY))
    mine = mine + pltpu.roll(mine, 32, 1) + pltpu.roll(mine, 64, 1) + pltpu.roll(mine, 96, 1)
    bhp_ref[...] = mine[0:1, 0:32]

    for copy in rs_copies(0) + rs_copies(1) + xs_copies(0) + xs_copies(1) + bh_sends(0) + bh_sends(1) + tm_copies:
        copy.wait_send()
    for copy in halo1 + halo2:
        copy.wait_send()


def body(pressure, saturation, permeability, pore_volume, cell_depth, residual, upstream_flags,
         perf_cell, perf_well, perf_index, well_mode, well_target):
    grid = (NZ, CX, CY)
    vmem = pl.BlockSpec(memory_space=pltpu.VMEM)
    dma = pltpu.SemaphoreType.DMA
    new_pressure, well_bhp = pl.pallas_call(
        kernel,
        out_shape=(pltpu.VMEM(grid, F32), pltpu.VMEM((1, 32), F32)),
        in_specs=[pl.BlockSpec(memory_space=pl.ANY)] * 12,
        out_specs=(vmem, vmem),
        scratch_shapes=[
            pltpu.VMEM(grid, F32),
            pltpu.VMEM((2,) + grid, F32),
            pltpu.VMEM((3,) + grid, F32),
            pltpu.VMEM(grid, F32),
            pltpu.VMEM(grid, F32),
            pltpu.VMEM((3,) + grid, F32),
            pltpu.VMEM(grid, jnp.int32),
            pltpu.VMEM((1, SLOTS), jnp.int32),
            pltpu.VMEM((1, SLOTS), jnp.int32),
            pltpu.VMEM((1, SLOTS), F32),
            pltpu.VMEM((1, 32), jnp.int32),
            pltpu.VMEM((1, 32), F32),
            pltpu.VMEM((3,) + grid, F32),
            pltpu.VMEM((ROWS, SLOTS), BF16),
            pltpu.VMEM((ROWS, 4 * CY), BF16),
            pltpu.VMEM((4 * CY, SLOTS), BF16),
            pltpu.VMEM((128, SLOTS), BF16),
            pltpu.VMEM((SLOTS, SLOTS), BF16),
            pltpu.VMEM((6,) + grid, F32),
            pltpu.VMEM(grid, F32),
            pltpu.VMEM(grid, F32),
            pltpu.VMEM(grid, F32),
            pltpu.VMEM(grid, F32),
            pltpu.VMEM((ROWS, CY), F32),
            pltpu.VMEM((8, SLOTS), F32),
            pltpu.VMEM((2, NGY, 8, CY), F32),
            pltpu.VMEM((2, NGY - 1, 8, CY), F32),
            pltpu.VMEM((2, 8, CY), F32),
            pltpu.VMEM((2, NGX - 1, 8, CY), F32),
            pltpu.VMEM((8, CY), F32),
            pltpu.VMEM((NGX - 1, 8, CY), F32),
            pltpu.VMEM((2, NGY, 8, CY), F32),
            pltpu.VMEM((2, NZ, 8, CY), F32),
            pltpu.VMEM((2, NZ, 8, CY), F32),
            pltpu.VMEM((2, 8, ROWS), F32),
            pltpu.VMEM((2, 8, ROWS), F32),
            pltpu.VMEM(grid, F32),
            pltpu.VMEM((2, NZ, 1, CY), F32),
            pltpu.VMEM((2, NZ, 1, CY), F32),
            pltpu.VMEM((2, 8, ROWS), F32),
            pltpu.VMEM((2, 8, ROWS), F32),
            dma((12,)),
            dma((2, NGY - 1)), dma((2, NGY - 1)),
            dma((2, NGX - 1)), dma((2, NGX - 1)),
            dma((NGX - 1,)), dma((NGX - 1,)),
            dma((2, NGY - 1)), dma((2, NGY - 1)),
            dma((8,)), dma((8,)),
        ],
        compiler_params=pltpu.CompilerParams(collective_id=0, has_side_effects=True),
        name="cpr_step",
    )(pressure, saturation, permeability, pore_volume, cell_depth, residual, upstream_flags,
      perf_cell, perf_well, perf_index, well_mode.reshape(1, 32), well_target.reshape(1, 32))
    return new_pressure, well_bhp.reshape(32)


def solution(mesh):
    areal, stacked, owned = P(None, "gx", "gy"), P(None, None, "gx", "gy"), P(("gx", "gy"))
    slots = P(("gx", "gy"), None)
    return jax.shard_map(
        body,
        mesh=mesh,
        in_specs=(areal, stacked, stacked, areal, areal, stacked, areal, slots, slots, slots, owned, owned),
        out_specs=(areal, owned),
        check_vma=False,
    )
```

```python
import jax
import jax.numpy as jnp
from jax import lax
from jax.experimental import pallas as pl
from jax.experimental.pallas import tpu as pltpu
from jax.sharding import PartitionSpec as P

MESH = pl.DeviceIdType.MESH
NZ, CX, CY = 12, 32, 128
ROWS = NZ * CX
SLOTS = 1024
NGX, NGY = 16, 8
GAMMA = (0.4, 0.5, 0.08)
F32, BF16 = jnp.float32, jnp.bfloat16
CONTRACT_LAST = (((1,), (1,)), ((), ()))
CONTRACT_FIRST = (((0,), (0,)), ((), ()))


def split(x):
    high = x.astype(BF16)
    return high, (x - high.astype(F32)).astype(BF16)


def phase_state(p, sw, sg):
    so = 1.0 - sw - sg
    bo = 1.0 + 0.2 * (p - 1.0)
    bw = 1.0 + 0.05 * (p - 1.0)
    return so, bo, bw


def hops(offset, size):
    return min(offset, size - offset)


GX_OFFSETS = sorted(((a, b) for a in range(4) for b in range(4) if a or b), key=lambda o: -hops(o[0], 4) - hops(o[1], 4))
GY_OFFSETS = sorted(((a, b) for a in range(4) for b in range(2) if a or b), key=lambda o: -2 * hops(o[0], 4) - o[1])


def kernel(
    p_hbm, sat_hbm, perm_hbm, pv_hbm, dep_hbm, res_hbm, flag_hbm, pc_hbm, pw_hbm, pi_hbm, wm_hbm, wt_hbm,
    out_ref, bhp_ref,
    p_ref, sat_ref, perm_ref, pv_ref, dep_ref, res_ref, flag_ref, pc_ref, pw_ref, pi_ref, wm_ref, wt_ref,
    mob, onehot, fields, spread, wlane, wpart, same, coup, pre, inv, rhs, cur, wacc, slotv,
    table0, table1, rs_recv0, rs_recv1, xs_src0, xs_src1, xs_recv0, xs_recv1, pair_src, pair_recv, tm_all, ctl, ball,
    hx_send, hx_recv, hy_send, hy_recv, halo_y, hx2_send, hx2_recv, hy2_send, hy2_recv,
    in_sem, send_sem, recv_sem,
):
    ix, iy = lax.axis_index("gx"), lax.axis_index("gy")
    chip_y, chip_z = ix // 4, lax.rem(ix, 4)
    chip_x, core = iy // 2, lax.rem(iy, 2)

    def gx_of(a, b):
        return lax.rem(chip_y + a, 4) * 4 + lax.rem(chip_z + b, 4)

    def gy_of(a, b):
        return lax.rem(chip_x + a, 4) * 2 + lax.rem(core + b, 2)

    barrier = pltpu.get_barrier_semaphore()
    for a, b in GX_OFFSETS:
        pl.semaphore_signal(barrier, inc=1, device_id=(gx_of(a, b), iy), device_id_type=MESH)
    for a, b in GY_OFFSETS:
        pl.semaphore_signal(barrier, inc=1, device_id=(ix, gy_of(a, b)), device_id_type=MESH)

    loads = {}
    pairs = (("pc", pc_hbm, pc_ref), ("pw", pw_hbm, pw_ref), ("pi", pi_hbm, pi_ref), ("sat", sat_hbm, sat_ref),
             ("p", p_hbm, p_ref), ("perm", perm_hbm, perm_ref), ("dep", dep_hbm, dep_ref), ("flag", flag_hbm, flag_ref),
             ("wm", wm_hbm, wm_ref), ("wt", wt_hbm, wt_ref), ("pv", pv_hbm, pv_ref), ("res", res_hbm, res_ref))
    for n, (name, src, dst) in enumerate(pairs):
        loads[name] = pltpu.make_async_copy(src, dst, in_sem.at[n])
        loads[name].start()

    lane = lax.broadcasted_iota(jnp.int32, (CX, CY), 1)
    row = lax.broadcasted_iota(jnp.int32, (CX, CY), 0)

    def remote(src, dst, ss, rs, dev):
        return pltpu.make_async_remote_copy(src_ref=src, dst_ref=dst, send_sem=ss, recv_sem=rs,
                                            device_id=dev, device_id_type=MESH)

    table, rs_recv = (table0, table1), (rs_recv0, rs_recv1)
    xs_src, xs_recv = (xs_src0, xs_src1), (xs_recv0, xs_recv1)

    def chunk_of(a, b):
        return lax.rem(core + b, 2) * 2 + lax.rem(chip_x + a, 2)

    mine_chunk = chunk_of(0, 0)
    far = (ix, gy_of(2, 0))
    near = [(ix, gy_of(0, 1))] + [(ix, (chip_x + 1 - 2 * lax.rem(chip_x, 2)) * 2 + lax.rem(core + b, 2)) for b in (0, 1)]

    class Group:
        def __init__(self, sem, copies, whole):
            self.copies = [remote(src, dst, send_sem.at[sem], recv_sem.at[sem], dev) for src, dst, dev in copies]
            self.all = remote(whole, whole, send_sem.at[sem], recv_sem.at[sem], copies[0][2])

        def send(self):
            for copy in self.copies:
                copy.start()

        def arrive(self):
            self.all.wait_recv()

        def left(self):
            self.all.wait_send()

    rs = [Group(t, [(table[t].at[chunk_of(a, b)], rs_recv[t].at[n], (ix, gy_of(a, b))) for n, (a, b) in enumerate(GY_OFFSETS)],
                rs_recv[t]) for t in range(2)]
    xs = [Group(2 + t, [(xs_src[t], xs_recv[t].at[n], (gx_of(a, b), iy)) for n, (a, b) in enumerate(GX_OFFSETS)],
                xs_recv[t]) for t in range(2)]
    bh = [Group(4 + t, [(ball.at[t, mine_chunk], ball.at[t, mine_chunk], dev) for dev in near[::-1]], ball.at[t, 0:3])
          for t in range(2)]
    pair = Group(6, [(pair_src, pair_recv, far)], pair_recv)
    tm = Group(7, [(tm_all.at[ix], tm_all.at[ix], (gx_of(a, b), iy)) for a, b in GX_OFFSETS], tm_all.at[0:NGX - 1])

    def halo_group(sem, xs, xr, ys, yr):
        after, before = (lax.rem(ix + 1, NGX), iy), (lax.rem(ix + NGX - 1, NGX), iy)
        right, left = (ix, lax.rem(iy + 1, NGY)), (ix, lax.rem(iy + NGY - 1, NGY))
        return (Group(sem, [(xs.at[1], xr.at[0], after), (xs.at[0], xr.at[1], before)], xr),
                Group(sem + 1, [(ys.at[1], yr.at[0], right), (ys.at[0], yr.at[1], left)], yr))

    halo1 = halo_group(8, hx_send, hx_recv, hy_send, hy_recv)
    halo2 = halo_group(10, hx2_send, hx2_recv, hy2_send, hy2_recv)

    for name in ("pc", "pw", "pi"):
        loads[name].wait()
    cell = pc_ref[...]
    cell_row = cell >> 7
    live = pw_ref[...] >= 0
    well = jnp.where(live, pw_ref[...], 0)
    owner = well >> 5
    well_row = (owner & 1) * 16 + ((owner >> 1) & 1) * 8 + ((owner >> 2) & 1) * 4 + (owner >> 5)
    well_lane = ((owner >> 3) & 3) * 32 + (well & 31)
    well_rows = lax.broadcasted_iota(jnp.int32, (32, SLOTS), 0) == well_row
    slotv[0:1, :] = jnp.where(live, pi_ref[...], 0.0)

    @pl.loop(0, NZ)
    def _(z):
        ids = lax.broadcasted_iota(jnp.int32, (CX, SLOTS), 0) + z * CX
        onehot[pl.ds(pl.multiple_of(z * CX, CX), CX), :] = jnp.where(ids == cell_row, 1.0, 0.0).astype(BF16)

    wlane[...] = jnp.where(lax.broadcasted_iota(jnp.int32, (CY, SLOTS), 0) == well_lane, 1.0, 0.0).astype(BF16)

    loads["sat"].wait()
    loads["p"].wait()

    @pl.loop(0, NZ)
    def _(z):
        sw, sg = sat_ref[0, z], sat_ref[1, z]
        so = 1.0 - sw - sg
        total = so * so * 0.5 + sw * sw + sg * sg * 5.0
        rows = pl.ds(pl.multiple_of(z * CX, CX), CX)
        for n, part in enumerate(split(total) + split(p_ref[z])):
            fields[rows, n * CY:(n + 1) * CY] = part

    sub256 = lax.broadcasted_iota(jnp.int32, (CY, 256), 0)

    def picked(count, dst):
        for j in range(SLOTS // 256):
            chunk = slice(j * 256, (j + 1) * 256)
            g = lax.dot_general(fields[...], onehot[:, chunk], CONTRACT_FIRST, preferred_element_type=F32)
            mask = sub256 == (pc_ref[0:1, chunk] & 127)
            for n in range(count):
                both = g[2 * n * CY:(2 * n + 1) * CY] + g[(2 * n + 1) * CY:(2 * n + 2) * CY]
                slotv[dst + n:dst + n + 1, chunk] = jnp.sum(jnp.where(mask, both, 0.0), axis=0, keepdims=True)

    def scatter_cells(value_row):
        for j in range(SLOTS // 256):
            chunk = slice(j * 256, (j + 1) * 256)
            mask = sub256 == (pc_ref[0:1, chunk] & 127)
            v = slotv[value_row:value_row + 1, chunk]
            high = v.astype(BF16).astype(F32)
            spread[0:CY, chunk] = jnp.where(mask, high, 0.0).astype(BF16)
            spread[CY:2 * CY, chunk] = jnp.where(mask, v - high, 0.0).astype(BF16)
        both = lax.dot_general(onehot[...], spread[...], CONTRACT_LAST, preferred_element_type=F32)
        wacc[...] = both[:, 0:CY] + both[:, CY:2 * CY]

    def well_sums(value_rows):
        for n, value_row in enumerate(value_rows):
            v = slotv[value_row:value_row + 1, :]
            high = v.astype(BF16).astype(F32)
            wpart[64 * n:64 * n + 32, :] = jnp.where(well_rows, high, 0.0).astype(BF16)
            wpart[64 * n + 32:64 * n + 64, :] = jnp.where(well_rows, v - high, 0.0).astype(BF16)
        both = lax.dot_general(wpart[0:64 * len(value_rows), :], wlane[...], CONTRACT_LAST, preferred_element_type=F32)
        return [(both[64 * n:64 * n + 32] + both[64 * n + 32:64 * n + 64]).reshape(4, 8, CY) for n in range(len(value_rows))]

    picked(2, 4)
    factor = slotv[0:1, :] * slotv[4:5, :]
    slotv[1:2, :] = factor
    slotv[2:3, :] = factor * slotv[5:6, :]
    for n, sums in enumerate(well_sums((2, 1))):
        table0[:, 8 * n:8 * n + 8, :] = sums

    pl.semaphore_wait(barrier, NGX + NGY - 2)

    def exchange(t):
        rs[t].arrive()
        part = table[t][mine_chunk]
        for n in range(NGY - 1):
            part = part + rs_recv[t][n]
        xs_src[t][...] = part
        xs[t].send()

    def finish_sums(t):
        xs[t].arrive()
        total = xs_src[t][...]
        for n in range(NGX - 1):
            total = total + xs_recv[t][n]
        return total

    rs[0].send()

    loads["wm"].wait()
    loads["wt"].wait()
    lanes = lax.broadcasted_iota(jnp.int32, (1, CY), 1)
    target4 = jnp.concatenate([wt_ref[...]] * 4, axis=1)
    mode4 = jnp.concatenate([wm_ref[...].astype(F32)] * 4, axis=1)
    both = jnp.where((lanes // 32) % 2 == 0, target4, mode4)
    pair_src[...] = jnp.where(lanes // 64 == chip_x // 2, both, 0.0)
    pair.send()

    for name in ("perm", "dep", "flag"):
        loads[name].wait()

    @pl.loop(0, NZ)
    def _(z):
        p, sw, sg = p_ref[z], sat_ref[0, z], sat_ref[1, z]
        so, bo, bw = phase_state(p, sw, sg)
        so2, sw2, sg2 = so * so * 0.5, sw * sw, sg * sg * 5.0
        m = (so2 * bo, sw2 * bw, sg2 * p)
        for c in range(3):
            mob[c, z] = m[c]
        flags = flag_ref[z]
        bit_x = (flags & 1).astype(F32)
        bit_y = ((flags >> 1) & 1).astype(F32)
        dep = dep_ref[z]
        xf = m + (perm_ref[0, z], dep, bit_x, p)
        yf = m + (perm_ref[1, z], dep, bit_y, p)
        for n, f in enumerate(xf):
            hx_send[0, z, n:n + 1, :] = f[0:1, :]
            hx_send[1, z, n:n + 1, :] = f[CX - 1:CX, :]
        hx_send[0, z, 7:8, :] = jnp.zeros((1, CY), F32)
        hx_send[1, z, 7:8, :] = jnp.zeros((1, CY), F32)
        packed = jnp.zeros((CX, CY), F32)
        for n, f in enumerate(yf):
            packed = jnp.where(lane == n, pltpu.roll(f, (n + 1) % CY, 1), packed)
            packed = jnp.where(lane == 8 + n, pltpu.roll(f, 8 + n, 1), packed)
        halo_y[z] = packed

    turned = halo_y[...].reshape(ROWS, CY).T
    hy_send[1] = turned[0:8, :]
    hy_send[0] = turned[8:16, :]
    for group in halo1:
        group.send()
    exchange(0)
    pair.arrive()
    tm_all[ix] = pair_src[...] + pair_recv[...]
    tm.send()

    scatter_cells(1)
    cells = jnp.broadcast_to(pc_ref[...].astype(F32), (CY, SLOTS)).T
    for j in range(SLOTS // CY):
        chunk = slice(j * CY, (j + 1) * CY)
        same[:, chunk] = jnp.where(cells == pc_ref[0:1, chunk].astype(F32), 1.0, 0.0).astype(BF16)

    for name in ("pv", "res"):
        loads[name].wait()
    for group in halo1:
        group.arrive()
    stacked = jnp.concatenate([hy_recv[0], hy_recv[1], jnp.zeros((CY - 16, ROWS), F32)], axis=0)
    halo_y[...] = stacked.T.reshape(NZ, CX, CY)

    def face(w, m, n, k, kn, up, drop):
        trans = 2.0 * k * kn / (k + kn)
        c = jnp.zeros((CX, CY), F32)
        g = jnp.zeros((CX, CY), F32)
        for i in range(3):
            flux = w[i] * jnp.where(up, m[i], n[i])
            c = c + flux
            g = g + GAMMA[i] * flux
        c = c * trans
        return c, g * (trans * drop)

    @pl.loop(0, NZ)
    def _(z):
        p, sw, sg = p_ref[z], sat_ref[0, z], sat_ref[1, z]
        so, bo, bw = phase_state(p, sw, sg)
        w = (1.0 / bo, 1.0 / bw, 1.0 / p)
        m = (mob[0, z], mob[1, z], mob[2, z])
        dep = dep_ref[z]
        flags = flag_ref[z]
        storage = pv_ref[z] * (so * 0.2 * w[0] + sw * 0.05 * w[1] + sg * w[2])
        lift = jnp.zeros((CX, CY), F32)
        faces = jnp.zeros((CX, CY), F32)
        beside = jnp.zeros((CX, CY), F32)

        def add(n, lift, faces, beside, c, g, pn):
            coup[n, z] = c
            return lift + g, faces + c, beside + c * pn

        for side in range(2):
            halo = hx_recv[side, z]
            edge = 0 if side == 0 else CX - 1
            inside = (ix > 0) if side == 0 else (ix < NGX - 1)

            def shifted(f, n):
                return jnp.where(row == edge, jnp.broadcast_to(halo[n:n + 1, :], (CX, CY)), pltpu.roll(f, 1 if side == 0 else CX - 1, 0))
            k = perm_ref[0, z]
            kn = shifted(k, 3)
            kn = jnp.where((row == edge) & jnp.logical_not(inside), 0.0, kn)
            if side == 0:
                up = shifted((flags & 1).astype(F32), 5) < 0.5
            else:
                up = (flags & 1) == 1
            c, g = face(w, m, tuple(shifted(m[i], i) for i in range(3)), k, kn, up, dep - shifted(dep, 4))
            lift, faces, beside = add(side, lift, faces, beside, c, g, shifted(p, 6))

        pack = halo_y[z]
        for side in range(2):
            edge = 0 if side == 0 else CY - 1
            inside = (iy > 0) if side == 0 else (iy < NGY - 1)

            def shifted(f, n):
                moved = pltpu.roll(pack, (CY - n) % CY if side == 0 else CY - 1 - 8 - n, 1)
                return jnp.where(lane == edge, moved, pltpu.roll(f, 1 if side == 0 else CY - 1, 1))
            k = perm_ref[1, z]
            kn = shifted(k, 3)
            kn = jnp.where((lane == edge) & jnp.logical_not(inside), 0.0, kn)
            if side == 0:
                up = shifted(((flags >> 1) & 1).astype(F32), 5) < 0.5
            else:
                up = ((flags >> 1) & 1) == 1
            c, g = face(w, m, tuple(shifted(m[i], i) for i in range(3)), k, kn, up, dep - shifted(dep, 4))
            lift, faces, beside = add(2 + side, lift, faces, beside, c, g, shifted(p, 6))

        for side in range(2):
            zn = jnp.maximum(z - 1, 0) if side == 0 else jnp.minimum(z + 1, NZ - 1)
            inside = (z > 0) if side == 0 else (z < NZ - 1)
            k = perm_ref[2, z]
            kn = jnp.where(inside, perm_ref[2, zn], 0.0)
            if side == 0:
                up = (flag_ref[zn] >> 2) == 0
            else:
                up = (flags >> 2) == 1
            c, g = face(w, m, (mob[0, zn], mob[1, zn], mob[2, zn]), k, kn, up, dep - dep_ref[zn])
            lift, faces, beside = add(4 + side, lift, faces, beside, c, g, p_ref[zn])

        combined = w[0] * res_ref[0, z] + w[1] * res_ref[1, z] + w[2] * res_ref[2, z]
        b = storage * p - combined + lift
        rows = pl.ds(pl.multiple_of(z * CX, CX), CX)
        damp = 0.8 / (storage + faces + wacc[rows, :])
        rhs[z] = b
        inv[z] = damp
        first = 0.2 * p + damp * (b + beside)
        pre[z] = first
        for n, part in enumerate(split(first) + split(damp)):
            fields[rows, n * CY:(n + 1) * CY] = part

    picked(2, 4)

    tm.arrive()
    for n in range(NGX):
        ctl[n:n + 1, :] = tm_all[n]
    quarter = lax.broadcasted_iota(jnp.int32, (4, CY), 1) // 32
    quads = [ctl[pl.ds(n, 4, stride=4), :] for n in range(4)]

    def placed(start):
        rows = jnp.zeros((4, CY), F32)
        for n in range(4):
            rows = jnp.where(quarter == n, pltpu.roll(quads[n], (32 * n - start) % CY, 1), rows)
        return rows

    target = jnp.concatenate([placed(0), placed(64)], axis=0)
    mode = jnp.concatenate([placed(32), placed(96)], axis=0)

    def bhp_of(sums, base):
        return jnp.where(mode < 0.5, target, (sums - target) / base)

    def slot_flow(t):
        bh[t].arrive()
        wells = ball[t].reshape(32, CY)
        high, low = split(wells)
        g = jnp.dot(jnp.concatenate([high, low], axis=0), wlane[...], preferred_element_type=F32)
        slot_bhp = jnp.sum(jnp.where(well_rows, g[0:32] + g[32:64], 0.0), axis=0, keepdims=True)
        slotv[2:3, :] = slotv[1:2, :] * slot_bhp

    sums = finish_sums(0)
    base = sums[8:16]
    ball[0, mine_chunk] = bhp_of(sums[0:8], base)
    bh[0].send()
    slot_flow(0)
    high, low = split(slotv[2:3, :])
    flow = jnp.concatenate([jnp.broadcast_to(high, (16, SLOTS)), jnp.broadcast_to(low, (16, SLOTS))], axis=0)
    met = jnp.dot(flow, same[...], preferred_element_type=F32)
    slotv[6:7, :] = slotv[1:2, :] * (slotv[4:5, :] + slotv[5:6, :] * (met[0:1, :] + met[16:17, :]))
    table1[...] = well_sums((6,))[0]
    rs[1].send()

    scatter_cells(2)

    @pl.loop(0, NZ)
    def _(z):
        rows = pl.ds(pl.multiple_of(z * CX, CX), CX)
        c = pre[z] + inv[z] * wacc[rows, :]
        cur[z] = c
        hx2_send[0, z] = c[0:1, :]
        hx2_send[1, z] = c[CX - 1:CX, :]
        packed = jnp.where(lane == 0, pltpu.roll(c, 1, 1), 0.0)
        halo_y[z] = jnp.where(lane == 8, pltpu.roll(c, 8, 1), packed)

    turned = halo_y[...].reshape(ROWS, CY).T
    hy2_send[1] = turned[0:8, :]
    hy2_send[0] = turned[8:16, :]
    for group in halo2:
        group.send()
    exchange(1)

    for group in halo2:
        group.arrive()
    stacked = jnp.concatenate([hy2_recv[0], hy2_recv[1], jnp.zeros((CY - 16, ROWS), F32)], axis=0)
    halo_y[...] = stacked.T.reshape(NZ, CX, CY)

    @pl.loop(0, NZ)
    def _(z):
        c = cur[z]
        pack = halo_y[z]
        up_x = jnp.where(row == 0, jnp.broadcast_to(hx2_recv[0, z], (CX, CY)), pltpu.roll(c, 1, 0))
        down_x = jnp.where(row == CX - 1, jnp.broadcast_to(hx2_recv[1, z], (CX, CY)), pltpu.roll(c, CX - 1, 0))
        up_y = jnp.where(lane == 0, pack, pltpu.roll(c, 1, 1))
        down_y = jnp.where(lane == CY - 1, pltpu.roll(pack, CY - 9, 1), pltpu.roll(c, CY - 1, 1))
        up_z, down_z = cur[jnp.maximum(z - 1, 0)], cur[jnp.minimum(z + 1, NZ - 1)]
        total = rhs[z]
        for n, value in enumerate((up_x, down_x, up_y, down_y, up_z, down_z)):
            total = total + coup[n, z] * value
        pre[z] = 0.2 * c + inv[z] * total

    ball[1, mine_chunk] = bhp_of(finish_sums(1), base)
    bh[1].send()
    slot_flow(1)
    scatter_cells(2)

    @pl.loop(0, NZ)
    def _(z):
        rows = pl.ds(pl.multiple_of(z * CX, CX), CX)
        out_ref[z] = pre[z] + inv[z] * wacc[rows, :]

    line = lax.broadcasted_iota(jnp.int32, (8, CY), 0)
    wide = lax.broadcasted_iota(jnp.int32, (8, CY), 1)
    own = (line == (chip_x // 2) * 4 + chip_y) & (wide // 32 == chip_z)
    mine = jnp.broadcast_to(jnp.sum(jnp.where(own, ball[1, mine_chunk], 0.0), axis=0, keepdims=True), (8, CY))
    mine = mine + pltpu.roll(mine, 32, 1) + pltpu.roll(mine, 64, 1) + pltpu.roll(mine, 96, 1)
    bhp_ref[...] = mine[0:1, 0:32]

    for group in rs + xs + bh + [pair, tm] + list(halo1 + halo2):
        group.left()


def body(pressure, saturation, permeability, pore_volume, cell_depth, residual, upstream_flags,
         perf_cell, perf_well, perf_index, well_mode, well_target):
    grid = (NZ, CX, CY)
    vmem = pl.BlockSpec(memory_space=pltpu.VMEM)
    dma = pltpu.SemaphoreType.DMA
    new_pressure, well_bhp = pl.pallas_call(
        kernel,
        out_shape=(pltpu.VMEM(grid, F32), pltpu.VMEM((1, 32), F32)),
        in_specs=[pl.BlockSpec(memory_space=pl.ANY)] * 12,
        out_specs=(vmem, vmem),
        scratch_shapes=[
            pltpu.VMEM(grid, F32),
            pltpu.VMEM((2,) + grid, F32),
            pltpu.VMEM((3,) + grid, F32),
            pltpu.VMEM(grid, F32),
            pltpu.VMEM(grid, F32),
            pltpu.VMEM((3,) + grid, F32),
            pltpu.VMEM(grid, jnp.int32),
            pltpu.VMEM((1, SLOTS), jnp.int32),
            pltpu.VMEM((1, SLOTS), jnp.int32),
            pltpu.VMEM((1, SLOTS), F32),
            pltpu.VMEM((1, 32), jnp.int32),
            pltpu.VMEM((1, 32), F32),
            pltpu.VMEM((3,) + grid, F32),
            pltpu.VMEM((ROWS, SLOTS), BF16),
            pltpu.VMEM((ROWS, 4 * CY), BF16),
            pltpu.VMEM((2 * CY, SLOTS), BF16),
            pltpu.VMEM((CY, SLOTS), BF16),
            pltpu.VMEM((128, SLOTS), BF16),
            pltpu.VMEM((SLOTS, SLOTS), BF16),
            pltpu.VMEM((6,) + grid, F32),
            pltpu.VMEM(grid, F32),
            pltpu.VMEM(grid, F32),
            pltpu.VMEM(grid, F32),
            pltpu.VMEM(grid, F32),
            pltpu.VMEM((ROWS, CY), F32),
            pltpu.VMEM((8, SLOTS), F32),
            pltpu.VMEM((4, 16, CY), F32),
            pltpu.VMEM((4, 8, CY), F32),
            pltpu.VMEM((NGY - 1, 16, CY), F32),
            pltpu.VMEM((NGY - 1, 8, CY), F32),
            pltpu.VMEM((16, CY), F32),
            pltpu.VMEM((8, CY), F32),
            pltpu.VMEM((NGX - 1, 16, CY), F32),
            pltpu.VMEM((NGX - 1, 8, CY), F32),
            pltpu.VMEM((1, CY), F32),
            pltpu.VMEM((1, CY), F32),
            pltpu.VMEM((NGX, 1, CY), F32),
            pltpu.VMEM((NGX, CY), F32),
            pltpu.VMEM((2, 4, 8, CY), F32),
            pltpu.VMEM((2, NZ, 8, CY), F32),
            pltpu.VMEM((2, NZ, 8, CY), F32),
            pltpu.VMEM((2, 8, ROWS), F32),
            pltpu.VMEM((2, 8, ROWS), F32),
            pltpu.VMEM(grid, F32),
            pltpu.VMEM((2, NZ, 1, CY), F32),
            pltpu.VMEM((2, NZ, 1, CY), F32),
            pltpu.VMEM((2, 8, ROWS), F32),
            pltpu.VMEM((2, 8, ROWS), F32),
            dma((12,)),
            dma((12,)),
            dma((12,)),
        ],
        compiler_params=pltpu.CompilerParams(collective_id=0, has_side_effects=True),
        name="cpr_step",
    )(pressure, saturation, permeability, pore_volume, cell_depth, residual, upstream_flags,
      perf_cell, perf_well, perf_index, well_mode.reshape(1, 32), well_target.reshape(1, 32))
    return new_pressure, well_bhp.reshape(32)


def solution(mesh):
    areal, stacked, owned = P(None, "gx", "gy"), P(None, None, "gx", "gy"), P(("gx", "gy"))
    slots = P(("gx", "gy"), None)
    return jax.shard_map(
        body,
        mesh=mesh,
        in_specs=(areal, stacked, stacked, areal, areal, stacked, areal, slots, slots, slots, owned, owned),
        out_specs=(areal, owned),
        check_vma=False,
    )
```

```python
import jax
import jax.numpy as jnp
from jax import lax
from jax.experimental import pallas as pl
from jax.experimental.pallas import tpu as pltpu
from jax.sharding import PartitionSpec as P

MESH = pl.DeviceIdType.MESH
NZ, CX, CY = 12, 32, 128
ROWS = NZ * CX
SLOTS = 1024
NGX, NGY = 16, 8
GAMMA = (0.4, 0.5, 0.08)
F32, BF16 = jnp.float32, jnp.bfloat16
CONTRACT_LAST = (((1,), (1,)), ((), ()))
CONTRACT_FIRST = (((0,), (0,)), ((), ()))


def split(x):
    high = x.astype(BF16)
    return high, (x - high.astype(F32)).astype(BF16)


def phase_state(p, sw, sg):
    so = 1.0 - sw - sg
    bo = 1.0 + 0.2 * (p - 1.0)
    bw = 1.0 + 0.05 * (p - 1.0)
    return so, bo, bw


def hops(offset, size):
    return min(offset, size - offset)


GX_OFFSETS = sorted(((a, b) for a in range(4) for b in range(4) if a or b), key=lambda o: -hops(o[0], 4) - hops(o[1], 4))
GY_OFFSETS = sorted(((a, b) for a in range(4) for b in range(2) if a or b), key=lambda o: -2 * hops(o[0], 4) - o[1])


def kernel(
    p_hbm, sat_hbm, perm_hbm, pv_hbm, dep_hbm, res_hbm, flag_hbm, pc_hbm, pw_hbm, pi_hbm, wm_hbm, wt_hbm,
    out_ref, bhp_ref,
    p_ref, sat_ref, perm_ref, pv_ref, dep_ref, res_ref, flag_ref, pc_ref, pw_ref, pi_ref, wm_ref, wt_ref,
    mob, onehot, fields, wlane, wpart, same, coup, pre, inv, rhs, cur, wacc, slotv,
    table0, table1, rs_recv0, rs_recv1, xs_src0, xs_src1, xs_recv0, xs_recv1, pair_src, pair_recv, tm_all, ctl, ball,
    hx_send, hx_recv, hy_send, hy_recv, halo_y, hx2_send, hx2_recv, hy2_send, hy2_recv,
    in_sem, send_sem, recv_sem,
):
    ix, iy = lax.axis_index("gx"), lax.axis_index("gy")
    chip_y, chip_z = ix // 4, lax.rem(ix, 4)
    chip_x, core = iy // 2, lax.rem(iy, 2)

    def gx_of(a, b):
        return lax.rem(chip_y + a, 4) * 4 + lax.rem(chip_z + b, 4)

    def gy_of(a, b):
        return lax.rem(chip_x + a, 4) * 2 + lax.rem(core + b, 2)

    barrier = pltpu.get_barrier_semaphore()
    for a, b in GX_OFFSETS:
        pl.semaphore_signal(barrier, inc=1, device_id=(gx_of(a, b), iy), device_id_type=MESH)
    for a, b in GY_OFFSETS:
        pl.semaphore_signal(barrier, inc=1, device_id=(ix, gy_of(a, b)), device_id_type=MESH)

    loads = {}
    pairs = (("pc", pc_hbm, pc_ref), ("pw", pw_hbm, pw_ref), ("pi", pi_hbm, pi_ref), ("sat", sat_hbm, sat_ref),
             ("p", p_hbm, p_ref), ("perm", perm_hbm, perm_ref), ("dep", dep_hbm, dep_ref), ("flag", flag_hbm, flag_ref),
             ("wm", wm_hbm, wm_ref), ("wt", wt_hbm, wt_ref), ("pv", pv_hbm, pv_ref), ("res", res_hbm, res_ref))
    for n, (name, src, dst) in enumerate(pairs):
        loads[name] = pltpu.make_async_copy(src, dst, in_sem.at[n])
        loads[name].start()

    lane = lax.broadcasted_iota(jnp.int32, (CX, CY), 1)
    row = lax.broadcasted_iota(jnp.int32, (CX, CY), 0)

    def remote(src, dst, ss, rs, dev):
        return pltpu.make_async_remote_copy(src_ref=src, dst_ref=dst, send_sem=ss, recv_sem=rs,
                                            device_id=dev, device_id_type=MESH)

    table, rs_recv = (table0, table1), (rs_recv0, rs_recv1)
    xs_src, xs_recv = (xs_src0, xs_src1), (xs_recv0, xs_recv1)

    partner = (ix, gy_of(0, 1))
    x_peers = ((2, 0), (1, 0), (3, 0))

    class Group:
        def __init__(self, sem, copies, whole):
            self.copies = [remote(src, dst, send_sem.at[sem], recv_sem.at[sem], dev) for src, dst, dev in copies]
            self.all = remote(whole, whole, send_sem.at[sem], recv_sem.at[sem], copies[0][2])

        def send(self):
            for copy in self.copies:
                copy.start()

        def arrive(self):
            self.all.wait_recv()

        def left(self):
            self.all.wait_send()

    rs = [Group(t, [(table[t].at[lax.rem(core + b, 2)], rs_recv[t].at[n], (ix, gy_of(a, b))) for n, (a, b) in enumerate(GY_OFFSETS)],
                rs_recv[t]) for t in range(2)]
    xs = [Group(2 + t, [(xs_src[t], xs_recv[t].at[n], (gx_of(a, b), iy)) for n, (a, b) in enumerate(GX_OFFSETS)],
                xs_recv[t]) for t in range(2)]
    bh = [Group(4 + t, [(ball.at[t, core], ball.at[t, core], partner)], ball.at[t, 1 - core])
          for t in range(2)]
    pair = Group(6, [(pair_src, pair_recv.at[n], (ix, gy_of(a, b))) for n, (a, b) in enumerate(x_peers)], pair_recv)
    tm = Group(7, [(tm_all.at[ix], tm_all.at[ix], (gx_of(a, b), iy)) for a, b in GX_OFFSETS], tm_all.at[0:NGX - 1])

    def halo_group(sem, xs, xr, ys, yr):
        after, before = (lax.rem(ix + 1, NGX), iy), (lax.rem(ix + NGX - 1, NGX), iy)
        right, left = (ix, lax.rem(iy + 1, NGY)), (ix, lax.rem(iy + NGY - 1, NGY))
        return (Group(sem, [(xs.at[1], xr.at[0], after), (xs.at[0], xr.at[1], before)], xr),
                Group(sem + 1, [(ys.at[1], yr.at[0], right), (ys.at[0], yr.at[1], left)], yr))

    halo1 = halo_group(8, hx_send, hx_recv, hy_send, hy_recv)
    halo2 = halo_group(10, hx2_send, hx2_recv, hy2_send, hy2_recv)

    for name in ("pc", "pw", "pi"):
        loads[name].wait()
    cell = pc_ref[...]
    cell_row = cell >> 7
    live = pw_ref[...] >= 0
    well = jnp.where(live, pw_ref[...], 0)
    owner = well >> 5
    well_row = (owner & 1) * 16 + ((owner >> 1) & 3) * 4 + (owner >> 5)
    well_lane = ((owner >> 3) & 3) * 32 + (well & 31)
    well_rows = lax.broadcasted_iota(jnp.int32, (32, SLOTS), 0) == well_row
    slotv[0:1, :] = jnp.where(live, pi_ref[...], 0.0)

    @pl.loop(0, NZ)
    def _(z):
        ids = lax.broadcasted_iota(jnp.int32, (CX, SLOTS), 0) + z * CX
        onehot[pl.ds(pl.multiple_of(z * CX, CX), CX), :] = jnp.where(ids == cell_row, 1.0, 0.0).astype(BF16)

    wlane[...] = jnp.where(lax.broadcasted_iota(jnp.int32, (CY, SLOTS), 0) == well_lane, 1.0, 0.0).astype(BF16)

    loads["sat"].wait()
    loads["p"].wait()

    @pl.loop(0, NZ)
    def _(z):
        sw, sg = sat_ref[0, z], sat_ref[1, z]
        so = 1.0 - sw - sg
        total = so * so * 0.5 + sw * sw + sg * sg * 5.0
        rows = pl.ds(pl.multiple_of(z * CX, CX), CX)
        for n, part in enumerate(split(total) + split(p_ref[z])):
            fields[rows, n * CY:(n + 1) * CY] = part

    sub256 = lax.broadcasted_iota(jnp.int32, (CY, 256), 0)

    def picked(count, dst):
        for j in range(SLOTS // 256):
            chunk = slice(j * 256, (j + 1) * 256)
            g = lax.dot_general(fields[...], onehot[:, chunk], CONTRACT_FIRST, preferred_element_type=F32)
            mask = sub256 == (pc_ref[0:1, chunk] & 127)
            for n in range(count):
                both = g[2 * n * CY:(2 * n + 1) * CY] + g[(2 * n + 1) * CY:(2 * n + 2) * CY]
                slotv[dst + n:dst + n + 1, chunk] = jnp.sum(jnp.where(mask, both, 0.0), axis=0, keepdims=True)

    def scattered(value_row):
        total = None
        for j in range(SLOTS // 256):
            chunk = slice(j * 256, (j + 1) * 256)
            mask = sub256 == (pc_ref[0:1, chunk] & 127)
            v = slotv[value_row:value_row + 1, chunk]
            high = v.astype(BF16).astype(F32)
            spread = jnp.concatenate([jnp.where(mask, high, 0.0).astype(BF16), jnp.where(mask, v - high, 0.0).astype(BF16)], axis=0)
            part = lax.dot_general(onehot[:, chunk], spread, CONTRACT_LAST, preferred_element_type=F32)
            total = part if total is None else total + part
        return total[:, 0:CY] + total[:, CY:2 * CY]

    def well_sums(value_rows):
        for n, value_row in enumerate(value_rows):
            v = slotv[value_row:value_row + 1, :]
            high = v.astype(BF16).astype(F32)
            wpart[64 * n:64 * n + 32, :] = jnp.where(well_rows, high, 0.0).astype(BF16)
            wpart[64 * n + 32:64 * n + 64, :] = jnp.where(well_rows, v - high, 0.0).astype(BF16)
        both = lax.dot_general(wpart[0:64 * len(value_rows), :], wlane[...], CONTRACT_LAST, preferred_element_type=F32)
        return [(both[64 * n:64 * n + 32] + both[64 * n + 32:64 * n + 64]).reshape(2, 16, CY) for n in range(len(value_rows))]

    picked(2, 4)
    factor = slotv[0:1, :] * slotv[4:5, :]
    slotv[1:2, :] = factor
    slotv[2:3, :] = factor * slotv[5:6, :]
    for n, sums in enumerate(well_sums((2, 1))):
        table0[:, 16 * n:16 * n + 16, :] = sums

    cells = jnp.broadcast_to(pc_ref[...].astype(F32), (CY, SLOTS)).T
    for j in range(SLOTS // CY):
        chunk = slice(j * CY, (j + 1) * CY)
        same[:, chunk] = jnp.where(cells == pc_ref[0:1, chunk].astype(F32), 1.0, 0.0).astype(BF16)

    loads["wm"].wait()
    loads["wt"].wait()
    pair_lane = lax.broadcasted_iota(jnp.int32, (2, CY), 1)
    pair_row = lax.broadcasted_iota(jnp.int32, (2, CY), 0)
    target4 = jnp.broadcast_to(jnp.concatenate([wt_ref[...]] * 4, axis=1), (2, CY))
    mode4 = jnp.broadcast_to(jnp.concatenate([wm_ref[...].astype(F32)] * 4, axis=1), (2, CY))
    both = jnp.where((pair_lane // 32) % 2 == 0, target4, mode4)
    pair_src[...] = jnp.where((pair_row == chip_x // 2) & (pair_lane // 64 == lax.rem(chip_x, 2)), both, 0.0)

    pl.semaphore_wait(barrier, NGX + NGY - 2)

    def exchange(t):
        rs[t].arrive()
        part = table[t][core]
        for n in range(NGY - 1):
            part = part + rs_recv[t][n]
        xs_src[t][...] = part
        xs[t].send()

    def finish_sums(t):
        xs[t].arrive()
        total = xs_src[t][...]
        for n in range(NGX - 1):
            total = total + xs_recv[t][n]
        return total

    pair.send()
    rs[0].send()

    for name in ("perm", "dep", "flag"):
        loads[name].wait()

    @pl.loop(0, NZ)
    def _(z):
        p, sw, sg = p_ref[z], sat_ref[0, z], sat_ref[1, z]
        so, bo, bw = phase_state(p, sw, sg)
        so2, sw2, sg2 = so * so * 0.5, sw * sw, sg * sg * 5.0
        m = (so2 * bo, sw2 * bw, sg2 * p)
        for c in range(3):
            mob[c, z] = m[c]
        flags = flag_ref[z]
        bit_x = (flags & 1).astype(F32)
        bit_y = ((flags >> 1) & 1).astype(F32)
        dep = dep_ref[z]
        xf = m + (perm_ref[0, z], dep, bit_x, p)
        yf = m + (perm_ref[1, z], dep, bit_y, p)
        for n, f in enumerate(xf):
            hx_send[0, z, n:n + 1, :] = f[0:1, :]
            hx_send[1, z, n:n + 1, :] = f[CX - 1:CX, :]
        hx_send[0, z, 7:8, :] = jnp.zeros((1, CY), F32)
        hx_send[1, z, 7:8, :] = jnp.zeros((1, CY), F32)
        packed = jnp.zeros((CX, CY), F32)
        for n, f in enumerate(yf):
            packed = jnp.where(lane == n, pltpu.roll(f, (n + 1) % CY, 1), packed)
            packed = jnp.where(lane == 8 + n, pltpu.roll(f, 8 + n, 1), packed)
        halo_y[z] = packed

    turned = halo_y[...].reshape(ROWS, CY).T
    hy_send[1] = turned[0:8, :]
    hy_send[0] = turned[8:16, :]
    for group in halo1:
        group.send()
    wacc[...] = scattered(1)
    pair.arrive()
    tm_all[ix] = pair_src[...] + pair_recv[0] + pair_recv[1] + pair_recv[2]
    tm.send()
    exchange(0)

    for name in ("pv", "res"):
        loads[name].wait()
    for group in halo1:
        group.arrive()
    stacked = jnp.concatenate([hy_recv[0], hy_recv[1], jnp.zeros((CY - 16, ROWS), F32)], axis=0)
    halo_y[...] = stacked.T.reshape(NZ, CX, CY)

    def face(w, m, n, k, kn, up, drop):
        trans = 2.0 * k * kn / (k + kn)
        c = jnp.zeros((CX, CY), F32)
        g = jnp.zeros((CX, CY), F32)
        for i in range(3):
            flux = w[i] * jnp.where(up, m[i], n[i])
            c = c + flux
            g = g + GAMMA[i] * flux
        c = c * trans
        return c, g * (trans * drop)

    @pl.loop(0, NZ)
    def _(z):
        p, sw, sg = p_ref[z], sat_ref[0, z], sat_ref[1, z]
        so, bo, bw = phase_state(p, sw, sg)
        w = (1.0 / bo, 1.0 / bw, 1.0 / p)
        m = (mob[0, z], mob[1, z], mob[2, z])
        dep = dep_ref[z]
        flags = flag_ref[z]
        storage = pv_ref[z] * (so * 0.2 * w[0] + sw * 0.05 * w[1] + sg * w[2])
        lift = jnp.zeros((CX, CY), F32)
        faces = jnp.zeros((CX, CY), F32)
        beside = jnp.zeros((CX, CY), F32)

        def add(n, lift, faces, beside, c, g, pn):
            coup[n, z] = c
            return lift + g, faces + c, beside + c * pn

        for side in range(2):
            halo = hx_recv[side, z]
            edge = 0 if side == 0 else CX - 1
            inside = (ix > 0) if side == 0 else (ix < NGX - 1)

            def shifted(f, n):
                return jnp.where(row == edge, jnp.broadcast_to(halo[n:n + 1, :], (CX, CY)), pltpu.roll(f, 1 if side == 0 else CX - 1, 0))
            k = perm_ref[0, z]
            kn = shifted(k, 3)
            kn = jnp.where((row == edge) & jnp.logical_not(inside), 0.0, kn)
            if side == 0:
                up = shifted((flags & 1).astype(F32), 5) < 0.5
            else:
                up = (flags & 1) == 1
            c, g = face(w, m, tuple(shifted(m[i], i) for i in range(3)), k, kn, up, dep - shifted(dep, 4))
            lift, faces, beside = add(side, lift, faces, beside, c, g, shifted(p, 6))

        pack = halo_y[z]
        for side in range(2):
            edge = 0 if side == 0 else CY - 1
            inside = (iy > 0) if side == 0 else (iy < NGY - 1)

            def shifted(f, n):
                moved = pltpu.roll(pack, (CY - n) % CY if side == 0 else CY - 1 - 8 - n, 1)
                return jnp.where(lane == edge, moved, pltpu.roll(f, 1 if side == 0 else CY - 1, 1))
            k = perm_ref[1, z]
            kn = shifted(k, 3)
            kn = jnp.where((lane == edge) & jnp.logical_not(inside), 0.0, kn)
            if side == 0:
                up = shifted(((flags >> 1) & 1).astype(F32), 5) < 0.5
            else:
                up = ((flags >> 1) & 1) == 1
            c, g = face(w, m, tuple(shifted(m[i], i) for i in range(3)), k, kn, up, dep - shifted(dep, 4))
            lift, faces, beside = add(2 + side, lift, faces, beside, c, g, shifted(p, 6))

        for side in range(2):
            zn = jnp.maximum(z - 1, 0) if side == 0 else jnp.minimum(z + 1, NZ - 1)
            inside = (z > 0) if side == 0 else (z < NZ - 1)
            k = perm_ref[2, z]
            kn = jnp.where(inside, perm_ref[2, zn], 0.0)
            if side == 0:
                up = (flag_ref[zn] >> 2) == 0
            else:
                up = (flags >> 2) == 1
            c, g = face(w, m, (mob[0, zn], mob[1, zn], mob[2, zn]), k, kn, up, dep - dep_ref[zn])
            lift, faces, beside = add(4 + side, lift, faces, beside, c, g, p_ref[zn])

        combined = w[0] * res_ref[0, z] + w[1] * res_ref[1, z] + w[2] * res_ref[2, z]
        b = storage * p - combined + lift
        rows = pl.ds(pl.multiple_of(z * CX, CX), CX)
        damp = 0.8 / (storage + faces + wacc[rows, :])
        rhs[z] = b
        inv[z] = damp
        first = 0.2 * p + damp * (b + beside)
        pre[z] = first
        for n, part in enumerate(split(first) + split(damp)):
            fields[rows, n * CY:(n + 1) * CY] = part

    picked(2, 4)

    tm.arrive()
    for n in range(NGX):
        ctl[0, n:n + 1, :] = tm_all[n, 0:1, :]
        ctl[1, n:n + 1, :] = tm_all[n, 1:2, :]
    quarter = lax.broadcasted_iota(jnp.int32, (4, CY), 1) // 32
    quads = [[ctl[h, pl.ds(n, 4, stride=4), :] for n in range(4)] for h in range(2)]

    def placed(start):
        blocks = []
        for x in range(4):
            rows = jnp.zeros((4, CY), F32)
            for n in range(4):
                rows = jnp.where(quarter == n, pltpu.roll(quads[x // 2][n], (32 * n - start - 64 * (x % 2)) % CY, 1), rows)
            blocks.append(rows)
        return jnp.concatenate(blocks, axis=0)

    target, mode = placed(0), placed(32)

    def bhp_of(sums, base):
        return jnp.where(mode < 0.5, target, (sums - target) / base)

    def slot_flow(t):
        bh[t].arrive()
        wells = ball[t].reshape(32, CY)
        high, low = split(wells)
        g = jnp.dot(jnp.concatenate([high, low], axis=0), wlane[...], preferred_element_type=F32)
        slot_bhp = jnp.sum(jnp.where(well_rows, g[0:32] + g[32:64], 0.0), axis=0, keepdims=True)
        slotv[2:3, :] = slotv[1:2, :] * slot_bhp

    sums = finish_sums(0)
    base = sums[16:32]
    ball[0, core] = bhp_of(sums[0:16], base)
    bh[0].send()
    slot_flow(0)
    high, low = split(slotv[2:3, :])
    flow = jnp.concatenate([jnp.broadcast_to(high, (16, SLOTS)), jnp.broadcast_to(low, (16, SLOTS))], axis=0)
    met = jnp.dot(flow, same[...], preferred_element_type=F32)
    slotv[6:7, :] = slotv[1:2, :] * (slotv[4:5, :] + slotv[5:6, :] * (met[0:1, :] + met[16:17, :]))
    table1[...] = well_sums((6,))[0]
    rs[1].send()

    wacc[...] = scattered(2)

    @pl.loop(0, NZ)
    def _(z):
        rows = pl.ds(pl.multiple_of(z * CX, CX), CX)
        c = pre[z] + inv[z] * wacc[rows, :]
        cur[z] = c
        hx2_send[0, z] = c[0:1, :]
        hx2_send[1, z] = c[CX - 1:CX, :]
        packed = jnp.where(lane == 0, pltpu.roll(c, 1, 1), 0.0)
        halo_y[z] = jnp.where(lane == 8, pltpu.roll(c, 8, 1), packed)

    turned = halo_y[...].reshape(ROWS, CY).T
    hy2_send[1] = turned[0:8, :]
    hy2_send[0] = turned[8:16, :]
    for group in halo2:
        group.send()
    exchange(1)

    for group in halo2:
        group.arrive()
    stacked = jnp.concatenate([hy2_recv[0], hy2_recv[1], jnp.zeros((CY - 16, ROWS), F32)], axis=0)
    halo_y[...] = stacked.T.reshape(NZ, CX, CY)

    @pl.loop(0, NZ)
    def _(z):
        c = cur[z]
        pack = halo_y[z]
        up_x = jnp.where(row == 0, jnp.broadcast_to(hx2_recv[0, z], (CX, CY)), pltpu.roll(c, 1, 0))
        down_x = jnp.where(row == CX - 1, jnp.broadcast_to(hx2_recv[1, z], (CX, CY)), pltpu.roll(c, CX - 1, 0))
        up_y = jnp.where(lane == 0, pack, pltpu.roll(c, 1, 1))
        down_y = jnp.where(lane == CY - 1, pltpu.roll(pack, CY - 9, 1), pltpu.roll(c, CY - 1, 1))
        up_z, down_z = cur[jnp.maximum(z - 1, 0)], cur[jnp.minimum(z + 1, NZ - 1)]
        total = rhs[z]
        for n, value in enumerate((up_x, down_x, up_y, down_y, up_z, down_z)):
            total = total + coup[n, z] * value
        pre[z] = 0.2 * c + inv[z] * total

    ball[1, core] = bhp_of(finish_sums(1), base)
    bh[1].send()
    slot_flow(1)
    out_ref[...] = pre[...] + inv[...] * scattered(2).reshape(NZ, CX, CY)

    line = lax.broadcasted_iota(jnp.int32, (16, CY), 0)
    wide = lax.broadcasted_iota(jnp.int32, (16, CY), 1)
    own = (line == chip_x * 4 + chip_y) & (wide // 32 == chip_z)
    mine = jnp.broadcast_to(jnp.sum(jnp.where(own, ball[1, core], 0.0), axis=0, keepdims=True), (8, CY))
    mine = mine + pltpu.roll(mine, 32, 1) + pltpu.roll(mine, 64, 1) + pltpu.roll(mine, 96, 1)
    bhp_ref[...] = mine[0:1, 0:32]

    for group in rs + xs + bh + [pair, tm] + list(halo1 + halo2):
        group.left()


def hand_over(p_src, bhp_src, p_dst, bhp_dst, sem):
    copies = (pltpu.make_async_copy(p_src, p_dst, sem.at[0]), pltpu.make_async_copy(bhp_src, bhp_dst, sem.at[1]))
    for copy in copies:
        copy.start()
    for copy in copies:
        copy.wait()


def body(pressure, saturation, permeability, pore_volume, cell_depth, residual, upstream_flags,
         perf_cell, perf_well, perf_index, well_mode, well_target):
    grid = (NZ, CX, CY)
    vmem = pl.BlockSpec(memory_space=pltpu.VMEM)
    dma = pltpu.SemaphoreType.DMA
    new_pressure, well_bhp = pl.pallas_call(
        kernel,
        out_shape=(pltpu.VMEM(grid, F32), pltpu.VMEM((1, 32), F32)),
        in_specs=[pl.BlockSpec(memory_space=pl.ANY)] * 12,
        out_specs=(vmem, vmem),
        scratch_shapes=[
            pltpu.VMEM(grid, F32),
            pltpu.VMEM((2,) + grid, F32),
            pltpu.VMEM((3,) + grid, F32),
            pltpu.VMEM(grid, F32),
            pltpu.VMEM(grid, F32),
            pltpu.VMEM((3,) + grid, F32),
            pltpu.VMEM(grid, jnp.int32),
            pltpu.VMEM((1, SLOTS), jnp.int32),
            pltpu.VMEM((1, SLOTS), jnp.int32),
            pltpu.VMEM((1, SLOTS), F32),
            pltpu.VMEM((1, 32), jnp.int32),
            pltpu.VMEM((1, 32), F32),
            pltpu.VMEM((3,) + grid, F32),
            pltpu.VMEM((ROWS, SLOTS), BF16),
            pltpu.VMEM((ROWS, 4 * CY), BF16),
            pltpu.VMEM((CY, SLOTS), BF16),
            pltpu.VMEM((128, SLOTS), BF16),
            pltpu.VMEM((SLOTS, SLOTS), BF16),
            pltpu.VMEM((6,) + grid, F32),
            pltpu.VMEM(grid, F32),
            pltpu.VMEM(grid, F32),
            pltpu.VMEM(grid, F32),
            pltpu.VMEM(grid, F32),
            pltpu.VMEM((ROWS, CY), F32),
            pltpu.VMEM((8, SLOTS), F32),
            pltpu.VMEM((2, 32, CY), F32),
            pltpu.VMEM((2, 16, CY), F32),
            pltpu.VMEM((NGY - 1, 32, CY), F32),
            pltpu.VMEM((NGY - 1, 16, CY), F32),
            pltpu.VMEM((32, CY), F32),
            pltpu.VMEM((16, CY), F32),
            pltpu.VMEM((NGX - 1, 32, CY), F32),
            pltpu.VMEM((NGX - 1, 16, CY), F32),
            pltpu.VMEM((2, CY), F32),
            pltpu.VMEM((3, 2, CY), F32),
            pltpu.VMEM((NGX, 2, CY), F32),
            pltpu.VMEM((2, NGX, CY), F32),
            pltpu.VMEM((2, 2, 16, CY), F32),
            pltpu.VMEM((2, NZ, 8, CY), F32),
            pltpu.VMEM((2, NZ, 8, CY), F32),
            pltpu.VMEM((2, 8, ROWS), F32),
            pltpu.VMEM((2, 8, ROWS), F32),
            pltpu.VMEM(grid, F32),
            pltpu.VMEM((2, NZ, 1, CY), F32),
            pltpu.VMEM((2, NZ, 1, CY), F32),
            pltpu.VMEM((2, 8, ROWS), F32),
            pltpu.VMEM((2, 8, ROWS), F32),
            dma((12,)),
            dma((12,)),
            dma((12,)),
        ],
        compiler_params=pltpu.CompilerParams(collective_id=0, has_side_effects=True),
        name="cpr_step",
    )(pressure, saturation, permeability, pore_volume, cell_depth, residual, upstream_flags,
      perf_cell, perf_well, perf_index, well_mode.reshape(1, 32), well_target.reshape(1, 32))
    anywhere = pl.BlockSpec(memory_space=pl.ANY)
    new_pressure, well_bhp = pl.pallas_call(
        hand_over,
        out_shape=(jax.ShapeDtypeStruct(grid, F32), jax.ShapeDtypeStruct((1, 32), F32)),
        in_specs=[vmem] * 2,
        out_specs=(anywhere, anywhere),
        scratch_shapes=[dma((2,))],
        name="hand_over",
    )(pltpu.with_memory_space_constraint(new_pressure, pltpu.VMEM), pltpu.with_memory_space_constraint(well_bhp, pltpu.VMEM))
    return new_pressure, well_bhp.reshape(32)


def solution(mesh):
    areal, stacked, owned = P(None, "gx", "gy"), P(None, None, "gx", "gy"), P(("gx", "gy"))
    slots = P(("gx", "gy"), None)
    return jax.shard_map(
        body,
        mesh=mesh,
        in_specs=(areal, stacked, stacked, areal, areal, stacked, areal, slots, slots, slots, owned, owned),
        out_specs=(areal, owned),
        check_vma=False,
    )
```

```python
import jax
import jax.numpy as jnp
from jax import lax
from jax.experimental import pallas as pl
from jax.experimental.pallas import tpu as pltpu
from jax.sharding import PartitionSpec as P

MESH = pl.DeviceIdType.MESH
NZ, CX, CY = 12, 32, 128
ROWS = NZ * CX
SLOTS = 1024
NGX, NGY = 16, 8
GAMMA = (0.4, 0.5, 0.08)
F32, BF16 = jnp.float32, jnp.bfloat16
CONTRACT_LAST = (((1,), (1,)), ((), ()))
CONTRACT_FIRST = (((0,), (0,)), ((), ()))


def split(x):
    high = x.astype(BF16)
    return high, (x - high.astype(F32)).astype(BF16)


def phase_state(p, sw, sg):
    so = 1.0 - sw - sg
    bo = 1.0 + 0.2 * (p - 1.0)
    bw = 1.0 + 0.05 * (p - 1.0)
    return so, bo, bw


def phase_mobility(p, sw, sg):
    so, bo, bw = phase_state(p, sw, sg)
    return so * so * 0.5 * bo, sw * sw * bw, sg * sg * 5.0 * p


def hops(offset, size):
    return min(offset, size - offset)


GX_OFFSETS = sorted(((a, b) for a in range(4) for b in range(4) if a or b), key=lambda o: -hops(o[0], 4) - hops(o[1], 4))
GY_OFFSETS = sorted(((a, b) for a in range(4) for b in range(2) if a or b), key=lambda o: -2 * hops(o[0], 4) - o[1])


def kernel(
    p_hbm, sat_hbm, perm_hbm, pv_hbm, dep_hbm, res_hbm, flag_hbm, pc_hbm, pw_hbm, pi_hbm, wm_hbm, wt_hbm,
    out_ref, bhp_ref,
    p_ref, sat_ref, perm_ref, pv_ref, dep_ref, res_ref, flag_ref, pc_ref, pw_ref, pi_ref, wm_ref, wt_ref,
    mob, onehot, fields, wlane, clane, wrow, wpart, same, coup, pre, inv, rhs, cur, wacc, slotv,
    table0, table1, rs_recv0, rs_recv1, xs_src0, xs_src1, xs_recv0, xs_recv1, pair_src, pair_recv, tm_all, ctl, ball,
    hx_send, hx_recv, hx_mob, hy_send, hy_recv, hy_rows, halo_y, hx2_send, hx2_recv, hy2_send, hy2_recv,
    in_sem, send_sem, recv_sem,
):
    ix, iy = lax.axis_index("gx"), lax.axis_index("gy")
    chip_y, chip_z = ix // 4, lax.rem(ix, 4)
    chip_x, core = iy // 2, lax.rem(iy, 2)

    def gx_of(a, b):
        return lax.rem(chip_y + a, 4) * 4 + lax.rem(chip_z + b, 4)

    def gy_of(a, b):
        return lax.rem(chip_x + a, 4) * 2 + lax.rem(core + b, 2)

    loads = {}
    pairs = (("pc", pc_hbm, pc_ref), ("pw", pw_hbm, pw_ref), ("pi", pi_hbm, pi_ref), ("sw", sat_hbm.at[0], sat_ref.at[0]),
             ("sg", sat_hbm.at[1], sat_ref.at[1]), ("p", p_hbm, p_ref), ("wm", wm_hbm, wm_ref), ("wt", wt_hbm, wt_ref),
             ("perm", perm_hbm, perm_ref), ("dep", dep_hbm, dep_ref), ("flag", flag_hbm, flag_ref),
             ("pv", pv_hbm, pv_ref), ("res", res_hbm, res_ref))
    for n, (name, src, dst) in enumerate(pairs):
        loads[name] = pltpu.make_async_copy(src, dst, in_sem.at[n])
    for name in ("pc", "pw", "pi", "sw", "sg", "p"):
        loads[name].start()

    barrier = pltpu.get_barrier_semaphore()
    for a, b in GX_OFFSETS:
        pl.semaphore_signal(barrier, inc=1, device_id=(gx_of(a, b), iy), device_id_type=MESH)
    for a, b in GY_OFFSETS:
        pl.semaphore_signal(barrier, inc=1, device_id=(ix, gy_of(a, b)), device_id_type=MESH)

    for name in ("wm", "wt", "perm", "dep", "flag", "pv", "res"):
        loads[name].start()

    lane = lax.broadcasted_iota(jnp.int32, (CX, CY), 1)
    row = lax.broadcasted_iota(jnp.int32, (CX, CY), 0)

    def remote(src, dst, ss, rs, dev):
        return pltpu.make_async_remote_copy(src_ref=src, dst_ref=dst, send_sem=ss, recv_sem=rs,
                                            device_id=dev, device_id_type=MESH)

    table, rs_recv = (table0, table1), (rs_recv0, rs_recv1)
    xs_src, xs_recv = (xs_src0, xs_src1), (xs_recv0, xs_recv1)

    partner = (ix, gy_of(0, 1))
    x_peers = ((2, 0), (1, 0), (3, 0))

    class Group:
        def __init__(self, sem, copies, whole):
            self.copies = [remote(src, dst, send_sem.at[sem], recv_sem.at[sem], dev) for src, dst, dev in copies]
            self.all = remote(whole, whole, send_sem.at[sem], recv_sem.at[sem], copies[0][2])

        def send(self):
            for copy in self.copies:
                copy.start()

        def arrive(self):
            self.all.wait_recv()

        def left(self):
            self.all.wait_send()

    rs = [Group(t, [(table[t].at[lax.rem(core + b, 2)], rs_recv[t].at[n], (ix, gy_of(a, b))) for n, (a, b) in enumerate(GY_OFFSETS)],
                rs_recv[t]) for t in range(2)]
    xs = [Group(2 + t, [(xs_src[t], xs_recv[t].at[n], (gx_of(a, b), iy)) for n, (a, b) in enumerate(GX_OFFSETS)],
                xs_recv[t]) for t in range(2)]
    bh = [Group(4 + t, [(ball.at[t, core], ball.at[t, core], partner)], ball.at[t, 1 - core])
          for t in range(2)]
    pair = Group(6, [(pair_src, pair_recv.at[n], (ix, gy_of(a, b))) for n, (a, b) in enumerate(x_peers)], pair_recv)
    tm = Group(7, [(tm_all.at[ix], tm_all.at[ix], (gx_of(a, b), iy)) for a, b in GX_OFFSETS], tm_all.at[0:NGX - 1])

    def halo_group(sem, xs, xr, ys, yr):
        after, before = (lax.rem(ix + 1, NGX), iy), (lax.rem(ix + NGX - 1, NGX), iy)
        right, left = (ix, lax.rem(iy + 1, NGY)), (ix, lax.rem(iy + NGY - 1, NGY))
        return (Group(sem, [(xs.at[1], xr.at[0], after), (xs.at[0], xr.at[1], before)], xr),
                Group(sem + 1, [(ys.at[1], yr.at[0], right), (ys.at[0], yr.at[1], left)], yr))

    halo1 = halo_group(8, hx_send, hx_recv, hy_send, hy_recv)
    halo2 = halo_group(10, hx2_send, hx2_recv, hy2_send, hy2_recv)

    for name in ("pc", "pw", "pi"):
        loads[name].wait()
    cell = pc_ref[...]
    cell_row = cell >> 7
    live = pw_ref[...] >= 0
    well = jnp.where(live, pw_ref[...], 0)
    owner = well >> 5
    well_row = (owner & 1) * 16 + ((owner >> 1) & 3) * 4 + (owner >> 5)
    well_lane = ((owner >> 3) & 3) * 32 + (well & 31)
    well_rows = lax.broadcasted_iota(jnp.int32, (32, SLOTS), 0) == well_row
    wrow[...] = jnp.where(well_rows, 1.0, 0.0).astype(BF16)
    slotv[0:1, :] = jnp.where(live, pi_ref[...], 0.0)

    @pl.loop(0, NZ)
    def _(z):
        ids = lax.broadcasted_iota(jnp.int32, (CX, SLOTS), 0) + z * CX
        onehot[pl.ds(pl.multiple_of(z * CX, CX), CX), :] = jnp.where(ids == cell_row, 1.0, 0.0).astype(BF16)

    wlane[...] = jnp.where(lax.broadcasted_iota(jnp.int32, (CY, SLOTS), 0) == well_lane, 1.0, 0.0).astype(BF16)

    clane[...] = jnp.where(lax.broadcasted_iota(jnp.int32, (CY, SLOTS), 0) == (cell & 127), 1.0, 0.0).astype(BF16)

    for name in ("sw", "sg", "p"):
        loads[name].wait()

    @pl.loop(0, NZ)
    def _(z):
        sw, sg = sat_ref[0, z], sat_ref[1, z]
        so = 1.0 - sw - sg
        total = so * so * 0.5 + sw * sw + sg * sg * 5.0
        rows = pl.ds(pl.multiple_of(z * CX, CX), CX)
        for n, part in enumerate(split(total) + split(p_ref[z])):
            fields[rows, n * CY:(n + 1) * CY] = part

    sub256 = lax.broadcasted_iota(jnp.int32, (CY, 256), 0)

    def picked(count, dst):
        for j in range(SLOTS // 256):
            chunk = slice(j * 256, (j + 1) * 256)
            g = lax.dot_general(fields[...], onehot[:, chunk], CONTRACT_FIRST, preferred_element_type=F32)
            mask = sub256 == (pc_ref[0:1, chunk] & 127)
            for n in range(count):
                both = g[2 * n * CY:(2 * n + 1) * CY] + g[(2 * n + 1) * CY:(2 * n + 2) * CY]
                slotv[dst + n:dst + n + 1, chunk] = jnp.sum(jnp.where(mask, both, 0.0), axis=0, keepdims=True)

    def scattered(value_row):
        total = None
        for j in range(SLOTS // 256):
            chunk = slice(j * 256, (j + 1) * 256)
            high, low = split(slotv[value_row:value_row + 1, chunk])
            spread = jnp.concatenate([clane[:, chunk] * high, clane[:, chunk] * low], axis=0)
            part = lax.dot_general(onehot[:, chunk], spread, CONTRACT_LAST, preferred_element_type=F32)
            total = part if total is None else total + part
        return total[:, 0:CY] + total[:, CY:2 * CY]

    def well_sums(value_rows):
        for n, value_row in enumerate(value_rows):
            high, low = split(slotv[value_row:value_row + 1, :])
            wpart[64 * n:64 * n + 32, :] = wrow[...] * high
            wpart[64 * n + 32:64 * n + 64, :] = wrow[...] * low
        both = lax.dot_general(wpart[0:64 * len(value_rows), :], wlane[...], CONTRACT_LAST, preferred_element_type=F32)
        return [(both[64 * n:64 * n + 32] + both[64 * n + 32:64 * n + 64]).reshape(2, 16, CY) for n in range(len(value_rows))]

    picked(2, 4)
    factor = slotv[0:1, :] * slotv[4:5, :]
    slotv[1:2, :] = factor
    slotv[2:3, :] = factor * slotv[5:6, :]
    for n, sums in enumerate(well_sums((2, 1))):
        table0[:, 16 * n:16 * n + 16, :] = sums

    loads["wm"].wait()
    loads["wt"].wait()
    pair_lane = lax.broadcasted_iota(jnp.int32, (2, CY), 1)
    pair_row = lax.broadcasted_iota(jnp.int32, (2, CY), 0)
    target4 = jnp.broadcast_to(jnp.concatenate([wt_ref[...]] * 4, axis=1), (2, CY))
    mode4 = jnp.broadcast_to(jnp.concatenate([wm_ref[...].astype(F32)] * 4, axis=1), (2, CY))
    both = jnp.where((pair_lane // 32) % 2 == 0, target4, mode4)
    pair_src[...] = jnp.where((pair_row == chip_x // 2) & (pair_lane // 64 == lax.rem(chip_x, 2)), both, 0.0)

    pl.semaphore_wait(barrier, NGX + NGY - 2)

    def exchange(t):
        rs[t].arrive()
        part = table[t][core]
        for n in range(NGY - 1):
            part = part + rs_recv[t][n]
        xs_src[t][...] = part
        xs[t].send()

    def finish_sums(t):
        xs[t].arrive()
        total = xs_src[t][...]
        for n in range(NGX - 1):
            total = total + xs_recv[t][n]
        return total

    pair.send()
    rs[0].send()

    for name in ("perm", "dep", "flag"):
        loads[name].wait()
    for z in range(NZ):
        for side, edge in enumerate((0, CX - 1)):
            at = slice(edge, edge + 1)
            rim = (p_ref[z, at, :], sat_ref[0, z, at, :], sat_ref[1, z, at, :], perm_ref[0, z, at, :], dep_ref[z, at, :],
                   (flag_ref[z, at, :] & 1).astype(F32))
            for n, f in enumerate(rim):
                hx_send[side, n, z:z + 1, :] = f
    halo1[0].send()

    @pl.loop(0, NZ)
    def _(z):
        rim = (p_ref[z], sat_ref[0, z], sat_ref[1, z], perm_ref[1, z], dep_ref[z], ((flag_ref[z] >> 1) & 1).astype(F32))
        packed = jnp.zeros((CX, CY), F32)
        for n, f in enumerate(rim):
            packed = jnp.where(lane == n, pltpu.roll(f, (n + 1) % CY, 1), packed)
            packed = jnp.where(lane == 8 + n, pltpu.roll(f, 8 + n, 1), packed)
        halo_y[z] = packed

    turned = halo_y[...].reshape(ROWS, CY).T
    hy_send[1] = turned[0:8, :]
    hy_send[0] = turned[8:16, :]
    halo1[1].send()

    @pl.loop(0, NZ)
    def _(z):
        p, sw, sg = p_ref[z], sat_ref[0, z], sat_ref[1, z]
        for c, m in enumerate(phase_mobility(p, sw, sg)):
            mob[c, z] = m

    cells = jnp.broadcast_to(pc_ref[...].astype(F32), (CY, SLOTS)).T
    for j in range(SLOTS // CY):
        chunk = slice(j * CY, (j + 1) * CY)
        same[:, chunk] = jnp.where(cells == pc_ref[0:1, chunk].astype(F32), 1.0, 0.0).astype(BF16)

    wacc[...] = scattered(1)
    pair.arrive()
    tm_all[ix] = pair_src[...] + pair_recv[0] + pair_recv[1] + pair_recv[2]
    tm.send()
    exchange(0)

    for name in ("pv", "res"):
        loads[name].wait()
    for group in halo1:
        group.arrive()
    for side in range(2):
        for c, m in enumerate(phase_mobility(hx_recv[side, 0], hx_recv[side, 1], hx_recv[side, 2])):
            hx_mob[side, c] = m
        got = hy_recv[side]
        beside = phase_mobility(got[0:1], got[1:2], got[2:3]) + (got[3:4], got[4:5], got[5:6], got[0:1], got[7:8])
        for n, f in enumerate(beside):
            hy_rows[8 * side + n:8 * side + n + 1, :] = f
    stacked = jnp.concatenate([hy_rows[...], jnp.zeros((CY - 16, ROWS), F32)], axis=0)
    halo_y[...] = stacked.T.reshape(NZ, CX, CY)

    def face(w, m, n, k, kn, up, drop):
        trans = 2.0 * k * kn / (k + kn)
        c = jnp.zeros((CX, CY), F32)
        g = jnp.zeros((CX, CY), F32)
        for i in range(3):
            flux = w[i] * jnp.where(up, m[i], n[i])
            c = c + flux
            g = g + GAMMA[i] * flux
        c = c * trans
        return c, g * (trans * drop)

    @pl.loop(0, NZ)
    def _(z):
        p, sw, sg = p_ref[z], sat_ref[0, z], sat_ref[1, z]
        so, bo, bw = phase_state(p, sw, sg)
        w = (1.0 / bo, 1.0 / bw, 1.0 / p)
        m = (mob[0, z], mob[1, z], mob[2, z])
        dep = dep_ref[z]
        flags = flag_ref[z]
        storage = pv_ref[z] * (so * 0.2 * w[0] + sw * 0.05 * w[1] + sg * w[2])
        lift = jnp.zeros((CX, CY), F32)
        faces = jnp.zeros((CX, CY), F32)
        beside = jnp.zeros((CX, CY), F32)

        def add(n, lift, faces, beside, c, g, pn):
            coup[n, z] = c
            return lift + g, faces + c, beside + c * pn

        for side in range(2):
            here = pl.ds(z, 1)
            halo = [hx_mob[side, c, here, :] for c in range(3)] + [hx_recv[side, n, here, :] for n in (3, 4, 5, 0)]
            edge = 0 if side == 0 else CX - 1
            inside = (ix > 0) if side == 0 else (ix < NGX - 1)

            def shifted(f, n):
                return jnp.where(row == edge, jnp.broadcast_to(halo[n], (CX, CY)), pltpu.roll(f, 1 if side == 0 else CX - 1, 0))
            k = perm_ref[0, z]
            kn = shifted(k, 3)
            kn = jnp.where((row == edge) & jnp.logical_not(inside), 0.0, kn)
            if side == 0:
                up = shifted((flags & 1).astype(F32), 5) < 0.5
            else:
                up = (flags & 1) == 1
            c, g = face(w, m, tuple(shifted(m[i], i) for i in range(3)), k, kn, up, dep - shifted(dep, 4))
            lift, faces, beside = add(side, lift, faces, beside, c, g, shifted(p, 6))

        pack = halo_y[z]
        for side in range(2):
            edge = 0 if side == 0 else CY - 1
            inside = (iy > 0) if side == 0 else (iy < NGY - 1)

            def shifted(f, n):
                moved = pltpu.roll(pack, (CY - n) % CY if side == 0 else CY - 1 - 8 - n, 1)
                return jnp.where(lane == edge, moved, pltpu.roll(f, 1 if side == 0 else CY - 1, 1))
            k = perm_ref[1, z]
            kn = shifted(k, 3)
            kn = jnp.where((lane == edge) & jnp.logical_not(inside), 0.0, kn)
            if side == 0:
                up = shifted(((flags >> 1) & 1).astype(F32), 5) < 0.5
            else:
                up = ((flags >> 1) & 1) == 1
            c, g = face(w, m, tuple(shifted(m[i], i) for i in range(3)), k, kn, up, dep - shifted(dep, 4))
            lift, faces, beside = add(2 + side, lift, faces, beside, c, g, shifted(p, 6))

        for side in range(2):
            zn = jnp.maximum(z - 1, 0) if side == 0 else jnp.minimum(z + 1, NZ - 1)
            inside = (z > 0) if side == 0 else (z < NZ - 1)
            k = perm_ref[2, z]
            kn = jnp.where(inside, perm_ref[2, zn], 0.0)
            if side == 0:
                up = (flag_ref[zn] >> 2) == 0
            else:
                up = (flags >> 2) == 1
            c, g = face(w, m, (mob[0, zn], mob[1, zn], mob[2, zn]), k, kn, up, dep - dep_ref[zn])
            lift, faces, beside = add(4 + side, lift, faces, beside, c, g, p_ref[zn])

        combined = w[0] * res_ref[0, z] + w[1] * res_ref[1, z] + w[2] * res_ref[2, z]
        b = storage * p - combined + lift
        rows = pl.ds(pl.multiple_of(z * CX, CX), CX)
        damp = 0.8 / (storage + faces + wacc[rows, :])
        rhs[z] = b
        inv[z] = damp
        first = 0.2 * p + damp * (b + beside)
        pre[z] = first
        for n, part in enumerate(split(first) + split(damp)):
            fields[rows, n * CY:(n + 1) * CY] = part

    picked(2, 4)

    tm.arrive()
    for n in range(NGX):
        ctl[0, n:n + 1, :] = tm_all[n, 0:1, :]
        ctl[1, n:n + 1, :] = tm_all[n, 1:2, :]
    quarter = lax.broadcasted_iota(jnp.int32, (4, CY), 1) // 32
    quads = [[ctl[h, pl.ds(n, 4, stride=4), :] for n in range(4)] for h in range(2)]

    def placed(start):
        blocks = []
        for x in range(4):
            rows = jnp.zeros((4, CY), F32)
            for n in range(4):
                rows = jnp.where(quarter == n, pltpu.roll(quads[x // 2][n], (32 * n - start - 64 * (x % 2)) % CY, 1), rows)
            blocks.append(rows)
        return jnp.concatenate(blocks, axis=0)

    target, mode = placed(0), placed(32)

    def bhp_of(sums, base):
        return jnp.where(mode < 0.5, target, (sums - target) / base)

    def slot_flow(t):
        bh[t].arrive()
        wells = ball[t].reshape(32, CY)
        high, low = split(wells)
        g = jnp.dot(jnp.concatenate([high, low], axis=0), wlane[...], preferred_element_type=F32)
        slot_bhp = jnp.sum(jnp.where(well_rows, g[0:32] + g[32:64], 0.0), axis=0, keepdims=True)
        slotv[2:3, :] = slotv[1:2, :] * slot_bhp

    sums = finish_sums(0)
    base = sums[16:32]
    ball[0, core] = bhp_of(sums[0:16], base)
    bh[0].send()
    slot_flow(0)
    high, low = split(slotv[2:3, :])
    flow = jnp.concatenate([jnp.broadcast_to(high, (16, SLOTS)), jnp.broadcast_to(low, (16, SLOTS))], axis=0)
    met = jnp.dot(flow, same[...], preferred_element_type=F32)
    slotv[6:7, :] = slotv[1:2, :] * (slotv[4:5, :] + slotv[5:6, :] * (met[0:1, :] + met[16:17, :]))
    table1[...] = well_sums((6,))[0]
    rs[1].send()

    wacc[...] = scattered(2)

    @pl.loop(0, NZ)
    def _(z):
        rows = pl.ds(pl.multiple_of(z * CX, CX), CX)
        c = pre[z] + inv[z] * wacc[rows, :]
        cur[z] = c
        hx2_send[0, z] = c[0:1, :]
        hx2_send[1, z] = c[CX - 1:CX, :]
        packed = jnp.where(lane == 0, pltpu.roll(c, 1, 1), 0.0)
        halo_y[z] = jnp.where(lane == 8, pltpu.roll(c, 8, 1), packed)

    turned = halo_y[...].reshape(ROWS, CY).T
    hy2_send[1] = turned[0:8, :]
    hy2_send[0] = turned[8:16, :]
    for group in halo2:
        group.send()
    exchange(1)

    for group in halo2:
        group.arrive()
    stacked = jnp.concatenate([hy2_recv[0], hy2_recv[1], jnp.zeros((CY - 16, ROWS), F32)], axis=0)
    halo_y[...] = stacked.T.reshape(NZ, CX, CY)

    @pl.loop(0, NZ)
    def _(z):
        c = cur[z]
        pack = halo_y[z]
        up_x = jnp.where(row == 0, jnp.broadcast_to(hx2_recv[0, z], (CX, CY)), pltpu.roll(c, 1, 0))
        down_x = jnp.where(row == CX - 1, jnp.broadcast_to(hx2_recv[1, z], (CX, CY)), pltpu.roll(c, CX - 1, 0))
        up_y = jnp.where(lane == 0, pack, pltpu.roll(c, 1, 1))
        down_y = jnp.where(lane == CY - 1, pltpu.roll(pack, CY - 9, 1), pltpu.roll(c, CY - 1, 1))
        up_z, down_z = cur[jnp.maximum(z - 1, 0)], cur[jnp.minimum(z + 1, NZ - 1)]
        total = rhs[z]
        for n, value in enumerate((up_x, down_x, up_y, down_y, up_z, down_z)):
            total = total + coup[n, z] * value
        pre[z] = 0.2 * c + inv[z] * total

    ball[1, core] = bhp_of(finish_sums(1), base)
    bh[1].send()
    slot_flow(1)
    out_ref[...] = pre[...] + inv[...] * scattered(2).reshape(NZ, CX, CY)

    line = lax.broadcasted_iota(jnp.int32, (16, CY), 0)
    wide = lax.broadcasted_iota(jnp.int32, (16, CY), 1)
    own = (line == chip_x * 4 + chip_y) & (wide // 32 == chip_z)
    mine = jnp.broadcast_to(jnp.sum(jnp.where(own, ball[1, core], 0.0), axis=0, keepdims=True), (8, CY))
    mine = mine + pltpu.roll(mine, 32, 1) + pltpu.roll(mine, 64, 1) + pltpu.roll(mine, 96, 1)
    bhp_ref[...] = mine[0:1, 0:32]

    for group in rs + xs + bh + [pair, tm] + list(halo1 + halo2):
        group.left()


def hand_over(p_src, bhp_src, p_dst, bhp_dst, sem):
    copies = [pltpu.make_async_copy(bhp_src, bhp_dst, sem.at[4])]
    copies += [pltpu.make_async_copy(p_src.at[3 * n:3 * n + 3], p_dst.at[3 * n:3 * n + 3], sem.at[n]) for n in range(4)]
    for copy in copies:
        copy.start()
    for copy in copies:
        copy.wait()


def body(pressure, saturation, permeability, pore_volume, cell_depth, residual, upstream_flags,
         perf_cell, perf_well, perf_index, well_mode, well_target):
    grid = (NZ, CX, CY)
    vmem = pl.BlockSpec(memory_space=pltpu.VMEM)
    dma = pltpu.SemaphoreType.DMA
    new_pressure, well_bhp = pl.pallas_call(
        kernel,
        out_shape=(pltpu.VMEM(grid, F32), pltpu.VMEM((1, 32), F32)),
        in_specs=[pl.BlockSpec(memory_space=pl.ANY)] * 12,
        out_specs=(vmem, vmem),
        scratch_shapes=[
            pltpu.VMEM(grid, F32),
            pltpu.VMEM((2,) + grid, F32),
            pltpu.VMEM((3,) + grid, F32),
            pltpu.VMEM(grid, F32),
            pltpu.VMEM(grid, F32),
            pltpu.VMEM((3,) + grid, F32),
            pltpu.VMEM(grid, jnp.int32),
            pltpu.VMEM((1, SLOTS), jnp.int32),
            pltpu.VMEM((1, SLOTS), jnp.int32),
            pltpu.VMEM((1, SLOTS), F32),
            pltpu.VMEM((1, 32), jnp.int32),
            pltpu.VMEM((1, 32), F32),
            pltpu.VMEM((3,) + grid, F32),
            pltpu.VMEM((ROWS, SLOTS), BF16),
            pltpu.VMEM((ROWS, 4 * CY), BF16),
            pltpu.VMEM((CY, SLOTS), BF16),
            pltpu.VMEM((CY, SLOTS), BF16),
            pltpu.VMEM((32, SLOTS), BF16),
            pltpu.VMEM((128, SLOTS), BF16),
            pltpu.VMEM((SLOTS, SLOTS), BF16),
            pltpu.VMEM((6,) + grid, F32),
            pltpu.VMEM(grid, F32),
            pltpu.VMEM(grid, F32),
            pltpu.VMEM(grid, F32),
            pltpu.VMEM(grid, F32),
            pltpu.VMEM((ROWS, CY), F32),
            pltpu.VMEM((8, SLOTS), F32),
            pltpu.VMEM((2, 32, CY), F32),
            pltpu.VMEM((2, 16, CY), F32),
            pltpu.VMEM((NGY - 1, 32, CY), F32),
            pltpu.VMEM((NGY - 1, 16, CY), F32),
            pltpu.VMEM((32, CY), F32),
            pltpu.VMEM((16, CY), F32),
            pltpu.VMEM((NGX - 1, 32, CY), F32),
            pltpu.VMEM((NGX - 1, 16, CY), F32),
            pltpu.VMEM((2, CY), F32),
            pltpu.VMEM((3, 2, CY), F32),
            pltpu.VMEM((NGX, 2, CY), F32),
            pltpu.VMEM((2, NGX, CY), F32),
            pltpu.VMEM((2, 2, 16, CY), F32),
            pltpu.VMEM((2, 6, NZ, CY), F32),
            pltpu.VMEM((2, 6, NZ, CY), F32),
            pltpu.VMEM((2, 3, NZ, CY), F32),
            pltpu.VMEM((2, 8, ROWS), F32),
            pltpu.VMEM((2, 8, ROWS), F32),
            pltpu.VMEM((16, ROWS), F32),
            pltpu.VMEM(grid, F32),
            pltpu.VMEM((2, NZ, 1, CY), F32),
            pltpu.VMEM((2, NZ, 1, CY), F32),
            pltpu.VMEM((2, 8, ROWS), F32),
            pltpu.VMEM((2, 8, ROWS), F32),
            dma((13,)),
            dma((12,)),
            dma((12,)),
        ],
        compiler_params=pltpu.CompilerParams(collective_id=0, has_side_effects=True),
        name="cpr_step",
    )(pressure, saturation, permeability, pore_volume, cell_depth, residual, upstream_flags,
      perf_cell, perf_well, perf_index, well_mode.reshape(1, 32), well_target.reshape(1, 32))
    anywhere = pl.BlockSpec(memory_space=pl.ANY)
    new_pressure, well_bhp = pl.pallas_call(
        hand_over,
        out_shape=(jax.ShapeDtypeStruct(grid, F32), jax.ShapeDtypeStruct((1, 32), F32)),
        in_specs=[vmem] * 2,
        out_specs=(anywhere, anywhere),
        scratch_shapes=[dma((5,))],
        name="hand_over",
    )(pltpu.with_memory_space_constraint(new_pressure, pltpu.VMEM), pltpu.with_memory_space_constraint(well_bhp, pltpu.VMEM))
    return new_pressure, well_bhp.reshape(32)


def solution(mesh):
    areal, stacked, owned = P(None, "gx", "gy"), P(None, None, "gx", "gy"), P(("gx", "gy"))
    slots = P(("gx", "gy"), None)
    return jax.shard_map(
        body,
        mesh=mesh,
        in_specs=(areal, stacked, stacked, areal, areal, stacked, areal, slots, slots, slots, owned, owned),
        out_specs=(areal, owned),
        check_vma=False,
    )
```

```python
import jax
import jax.numpy as jnp
from jax import lax
from jax.experimental import pallas as pl
from jax.experimental.pallas import tpu as pltpu
from jax.sharding import PartitionSpec as P

MESH = pl.DeviceIdType.MESH
NZ, CX, CY = 12, 32, 128
ROWS = NZ * CX
SENT_ROWS = 7 * (32 + 16) + 15 * (32 + 16) + 2 * 16 + (3 + 15) * 2 + 2 * (6 * NZ + 24) + 2 * (NZ + 24)
SLOTS = 1024
NGX, NGY = 16, 8
GAMMA = (0.4, 0.5, 0.08)
F32, BF16 = jnp.float32, jnp.bfloat16
CONTRACT_LAST = (((1,), (1,)), ((), ()))
CONTRACT_FIRST = (((0,), (0,)), ((), ()))


def split(x):
    high = x.astype(BF16)
    return high, (x - high.astype(F32)).astype(BF16)


def phase_state(p, sw, sg):
    so = 1.0 - sw - sg
    bo = 1.0 + 0.2 * (p - 1.0)
    bw = 1.0 + 0.05 * (p - 1.0)
    return so, bo, bw


def phase_mobility(p, sw, sg):
    so, bo, bw = phase_state(p, sw, sg)
    return so * so * 0.5 * bo, sw * sw * bw, sg * sg * 5.0 * p


def hops(offset, size):
    return min(offset, size - offset)


GX_OFFSETS = sorted(((a, b) for a in range(4) for b in range(4) if a or b), key=lambda o: -hops(o[0], 4) - hops(o[1], 4))
GY_OFFSETS = sorted(((a, b) for a in range(4) for b in range(2) if a or b), key=lambda o: -2 * hops(o[0], 4) - o[1])


def kernel(
    p_hbm, sat_hbm, perm_hbm, pv_hbm, dep_hbm, res_hbm, flag_hbm, pc_hbm, pw_hbm, pi_hbm, wm_hbm, wt_hbm,
    out_ref, bhp_ref,
    p_ref, sat_ref, perm_ref, pv_ref, dep_ref, res_ref, flag_ref, pc_ref, pw_ref, pi_ref, wm_ref, wt_ref,
    mob, onehot, fields, wlane, clane, wrow, wpart, same, coup, pre, inv, rhs, cur, wacc, slotv,
    table0, table1, rs_recv0, rs_recv1, xs_src0, xs_src1, xs_recv0, xs_recv1, pair_src, pair_recv, tm_all, ctl, ball,
    hx_send, hx_recv, hx_mob, hy_send, hy_recv, hy_rows, halo_y, hx2_send, hx2_recv, hy2_send, hy2_recv, sent,
    in_sem, send_sem, recv_sem,
):
    ix, iy = lax.axis_index("gx"), lax.axis_index("gy")
    chip_y, chip_z = ix // 4, lax.rem(ix, 4)
    chip_x, core = iy // 2, lax.rem(iy, 2)

    def gx_of(a, b):
        return lax.rem(chip_y + a, 4) * 4 + lax.rem(chip_z + b, 4)

    def gy_of(a, b):
        return lax.rem(chip_x + a, 4) * 2 + lax.rem(core + b, 2)

    loads = (
        ((pc_hbm, pc_ref), (pw_hbm, pw_ref), (pi_hbm, pi_ref)),
        ((sat_hbm.at[0], sat_ref.at[0]), (sat_hbm.at[1], sat_ref.at[1]), (p_hbm, p_ref)),
        ((wm_hbm, wm_ref),),
        ((perm_hbm, perm_ref), (dep_hbm, dep_ref), (flag_hbm, flag_ref)),
        ((pv_hbm, pv_ref), (res_hbm, res_ref)),
        ((wt_hbm, wt_ref),),
    )
    sizes = (slotv.at[0:3], perm_ref, wm_ref, coup.at[0:5], coup.at[0:4], wt_ref)

    def load(n):
        for src, dst in loads[n]:
            pltpu.make_async_copy(src, dst, in_sem.at[n]).start()

    def loaded(n):
        pltpu.make_async_copy(sizes[n], sizes[n], in_sem.at[n]).wait()

    load(0)
    load(1)

    barrier = pltpu.get_barrier_semaphore()
    for a, b in GX_OFFSETS:
        pl.semaphore_signal(barrier, inc=1, device_id=(gx_of(a, b), iy), device_id_type=MESH)
    for a, b in GY_OFFSETS:
        pl.semaphore_signal(barrier, inc=1, device_id=(ix, gy_of(a, b)), device_id_type=MESH)

    for n in (2, 5, 3, 4):
        load(n)

    lane = lax.broadcasted_iota(jnp.int32, (CX, CY), 1)
    row = lax.broadcasted_iota(jnp.int32, (CX, CY), 0)

    def remote(src, dst, ss, rs, dev):
        return pltpu.make_async_remote_copy(src_ref=src, dst_ref=dst, send_sem=ss, recv_sem=rs,
                                            device_id=dev, device_id_type=MESH)

    table, rs_recv = (table0, table1), (rs_recv0, rs_recv1)
    xs_src, xs_recv = (xs_src0, xs_src1), (xs_recv0, xs_recv1)

    partner = (ix, gy_of(0, 1))
    x_peers = ((2, 0), (1, 0), (3, 0))

    class Group:
        def __init__(self, sem, copies, whole):
            self.copies = [remote(src, dst, send_sem, recv_sem.at[sem], dev) for src, dst, dev in copies]
            self.whole = (whole, whole, send_sem, recv_sem.at[sem], copies[0][2])

        def send(self):
            for copy in self.copies:
                copy.start()

        def arrive(self):
            remote(*self.whole).wait_recv()

    rs = [Group(t, [(table[t].at[lax.rem(core + b, 2)], rs_recv[t].at[n], (ix, gy_of(a, b))) for n, (a, b) in enumerate(GY_OFFSETS)],
                rs_recv[t]) for t in range(2)]
    xs = [Group(2 + t, [(xs_src[t], xs_recv[t].at[n], (gx_of(a, b), iy)) for n, (a, b) in enumerate(GX_OFFSETS)],
                xs_recv[t]) for t in range(2)]
    bh = [Group(4 + t, [(ball.at[t, core], ball.at[t, core], partner)], ball.at[t, 1 - core])
          for t in range(2)]
    pair = Group(6, [(pair_src, pair_recv.at[n], (ix, gy_of(a, b))) for n, (a, b) in enumerate(x_peers)], pair_recv)
    tm = Group(7, [(tm_all.at[ix], tm_all.at[ix], (gx_of(a, b), iy)) for a, b in GX_OFFSETS], tm_all.at[0:NGX - 1])

    def halo_groups(sem, xs, xr, ys, yr, size):
        after, before = (lax.rem(ix + 1, NGX), iy), (lax.rem(ix + NGX - 1, NGX), iy)
        right, left = (ix, lax.rem(iy + 1, NGY)), (ix, lax.rem(iy + NGY - 1, NGY))
        return (Group(sem, [(xs.at[1], xr.at[0], after), (xs.at[0], xr.at[1], before)], size),
                Group(sem, [(ys.at[1], yr.at[0], right), (ys.at[0], yr.at[1], left)], size))

    halo1 = halo_groups(8, hx_send, hx_recv, hy_send, hy_recv, coup.at[0, 0:6])
    halo2 = halo_groups(9, hx2_send, hx2_recv, hy2_send, hy2_recv, hx_mob)

    loaded(0)
    cell = pc_ref[...]
    cell_row = cell >> 7
    live = pw_ref[...] >= 0
    well = jnp.where(live, pw_ref[...], 0)
    owner = well >> 5
    well_row = (owner & 1) * 16 + ((owner >> 1) & 3) * 4 + (owner >> 5)
    well_lane = ((owner >> 3) & 3) * 32 + (well & 31)
    well_rows = lax.broadcasted_iota(jnp.int32, (32, SLOTS), 0) == well_row
    wrow[...] = jnp.where(well_rows, 1.0, 0.0).astype(BF16)
    slotv[0:1, :] = jnp.where(live, pi_ref[...], 0.0)

    @pl.loop(0, NZ)
    def _(z):
        ids = lax.broadcasted_iota(jnp.int32, (CX, SLOTS), 0) + z * CX
        onehot[pl.ds(pl.multiple_of(z * CX, CX), CX), :] = jnp.where(ids == cell_row, 1.0, 0.0).astype(BF16)

    wlane[...] = jnp.where(lax.broadcasted_iota(jnp.int32, (CY, SLOTS), 0) == well_lane, 1.0, 0.0).astype(BF16)

    clane[...] = jnp.where(lax.broadcasted_iota(jnp.int32, (CY, SLOTS), 0) == (cell & 127), 1.0, 0.0).astype(BF16)

    loaded(1)

    @pl.loop(0, NZ)
    def _(z):
        sw, sg = sat_ref[0, z], sat_ref[1, z]
        so = 1.0 - sw - sg
        total = so * so * 0.5 + sw * sw + sg * sg * 5.0
        rows = pl.ds(pl.multiple_of(z * CX, CX), CX)
        for n, part in enumerate(split(total) + split(p_ref[z])):
            fields[rows, n * CY:(n + 1) * CY] = part

    sub256 = lax.broadcasted_iota(jnp.int32, (CY, 256), 0)

    def picked(count, dst):
        for j in range(SLOTS // 256):
            chunk = slice(j * 256, (j + 1) * 256)
            g = lax.dot_general(fields[...], onehot[:, chunk], CONTRACT_FIRST, preferred_element_type=F32)
            mask = sub256 == (pc_ref[0:1, chunk] & 127)
            for n in range(count):
                both = g[2 * n * CY:(2 * n + 1) * CY] + g[(2 * n + 1) * CY:(2 * n + 2) * CY]
                slotv[dst + n:dst + n + 1, chunk] = jnp.sum(jnp.where(mask, both, 0.0), axis=0, keepdims=True)

    def scattered(value_row):
        total = None
        for j in range(SLOTS // 256):
            chunk = slice(j * 256, (j + 1) * 256)
            high, low = split(slotv[value_row:value_row + 1, chunk])
            spread = jnp.concatenate([clane[:, chunk] * high, clane[:, chunk] * low], axis=0)
            part = lax.dot_general(onehot[:, chunk], spread, CONTRACT_LAST, preferred_element_type=F32)
            total = part if total is None else total + part
        return total[:, 0:CY] + total[:, CY:2 * CY]

    def well_sums(value_rows):
        for n, value_row in enumerate(value_rows):
            high, low = split(slotv[value_row:value_row + 1, :])
            wpart[64 * n:64 * n + 32, :] = wrow[...] * high
            wpart[64 * n + 32:64 * n + 64, :] = wrow[...] * low
        both = lax.dot_general(wpart[0:64 * len(value_rows), :], wlane[...], CONTRACT_LAST, preferred_element_type=F32)
        return [(both[64 * n:64 * n + 32] + both[64 * n + 32:64 * n + 64]).reshape(2, 16, CY) for n in range(len(value_rows))]

    picked(2, 4)
    factor = slotv[0:1, :] * slotv[4:5, :]
    slotv[1:2, :] = factor
    slotv[2:3, :] = factor * slotv[5:6, :]
    for n, sums in enumerate(well_sums((2, 1))):
        table0[:, 16 * n:16 * n + 16, :] = sums

    loaded(2)
    loaded(5)
    pair_lane = lax.broadcasted_iota(jnp.int32, (2, CY), 1)
    pair_row = lax.broadcasted_iota(jnp.int32, (2, CY), 0)
    target4 = jnp.broadcast_to(jnp.concatenate([wt_ref[...]] * 4, axis=1), (2, CY))
    mode4 = jnp.broadcast_to(jnp.concatenate([wm_ref[...].astype(F32)] * 4, axis=1), (2, CY))
    both = jnp.where((pair_lane // 32) % 2 == 0, target4, mode4)
    pair_src[...] = jnp.where((pair_row == chip_x // 2) & (pair_lane // 64 == lax.rem(chip_x, 2)), both, 0.0)

    pl.semaphore_wait(barrier, NGX + NGY - 2)

    def exchange(t):
        rs[t].arrive()
        part = table[t][core]
        for n in range(NGY - 1):
            part = part + rs_recv[t][n]
        xs_src[t][...] = part
        xs[t].send()

    def finish_sums(t):
        xs[t].arrive()
        total = xs_src[t][...]
        for n in range(NGX - 1):
            total = total + xs_recv[t][n]
        return total

    pair.send()
    rs[0].send()

    loaded(3)
    for z in range(NZ):
        for side, edge in enumerate((0, CX - 1)):
            at = slice(edge, edge + 1)
            rim = (p_ref[z, at, :], sat_ref[0, z, at, :], sat_ref[1, z, at, :], perm_ref[0, z, at, :], dep_ref[z, at, :],
                   (flag_ref[z, at, :] & 1).astype(F32))
            for n, f in enumerate(rim):
                hx_send[side, n, z:z + 1, :] = f
    halo1[0].send()

    @pl.loop(0, NZ)
    def _(z):
        rim = (p_ref[z], sat_ref[0, z], sat_ref[1, z], perm_ref[1, z], dep_ref[z], ((flag_ref[z] >> 1) & 1).astype(F32))
        packed = jnp.zeros((CX, CY), F32)
        for n, f in enumerate(rim):
            packed = jnp.where(lane == n, pltpu.roll(f, (n + 1) % CY, 1), packed)
            packed = jnp.where(lane == 8 + n, pltpu.roll(f, 8 + n, 1), packed)
        halo_y[z] = packed

    turned = halo_y[...].reshape(ROWS, CY).T
    hy_send[1] = turned[0:8, :]
    hy_send[0] = turned[8:16, :]
    halo1[1].send()

    @pl.loop(0, NZ)
    def _(z):
        p, sw, sg = p_ref[z], sat_ref[0, z], sat_ref[1, z]
        for c, m in enumerate(phase_mobility(p, sw, sg)):
            mob[c, z] = m

    cells = jnp.broadcast_to(pc_ref[...].astype(F32), (CY, SLOTS)).T
    for j in range(SLOTS // CY):
        chunk = slice(j * CY, (j + 1) * CY)
        same[:, chunk] = jnp.where(cells == pc_ref[0:1, chunk].astype(F32), 1.0, 0.0).astype(BF16)

    wacc[...] = scattered(1)
    pair.arrive()
    tm_all[ix] = pair_src[...] + pair_recv[0] + pair_recv[1] + pair_recv[2]
    tm.send()
    exchange(0)

    loaded(4)
    halo1[0].arrive()
    for side in range(2):
        for c, m in enumerate(phase_mobility(hx_recv[side, 0], hx_recv[side, 1], hx_recv[side, 2])):
            hx_mob[side, c] = m
        got = hy_recv[side]
        beside = phase_mobility(got[0:1], got[1:2], got[2:3]) + (got[3:4], got[4:5], got[5:6], got[0:1], got[7:8])
        for n, f in enumerate(beside):
            hy_rows[8 * side + n:8 * side + n + 1, :] = f
    stacked = jnp.concatenate([hy_rows[...], jnp.zeros((CY - 16, ROWS), F32)], axis=0)
    halo_y[...] = stacked.T.reshape(NZ, CX, CY)

    def face(w, m, n, k, kn, up, drop):
        trans = 2.0 * k * kn / (k + kn)
        c = jnp.zeros((CX, CY), F32)
        g = jnp.zeros((CX, CY), F32)
        for i in range(3):
            flux = w[i] * jnp.where(up, m[i], n[i])
            c = c + flux
            g = g + GAMMA[i] * flux
        c = c * trans
        return c, g * (trans * drop)

    @pl.loop(0, NZ)
    def _(z):
        p, sw, sg = p_ref[z], sat_ref[0, z], sat_ref[1, z]
        so, bo, bw = phase_state(p, sw, sg)
        w = (1.0 / bo, 1.0 / bw, 1.0 / p)
        m = (mob[0, z], mob[1, z], mob[2, z])
        dep = dep_ref[z]
        flags = flag_ref[z]
        storage = pv_ref[z] * (so * 0.2 * w[0] + sw * 0.05 * w[1] + sg * w[2])
        lift = jnp.zeros((CX, CY), F32)
        faces = jnp.zeros((CX, CY), F32)
        beside = jnp.zeros((CX, CY), F32)

        def add(n, lift, faces, beside, c, g, pn):
            coup[n, z] = c
            return lift + g, faces + c, beside + c * pn

        for side in range(2):
            here = pl.ds(z, 1)
            halo = [hx_mob[side, c, here, :] for c in range(3)] + [hx_recv[side, n, here, :] for n in (3, 4, 5, 0)]
            edge = 0 if side == 0 else CX - 1
            inside = (ix > 0) if side == 0 else (ix < NGX - 1)

            def shifted(f, n):
                return jnp.where(row == edge, jnp.broadcast_to(halo[n], (CX, CY)), pltpu.roll(f, 1 if side == 0 else CX - 1, 0))
            k = perm_ref[0, z]
            kn = shifted(k, 3)
            kn = jnp.where((row == edge) & jnp.logical_not(inside), 0.0, kn)
            if side == 0:
                up = shifted((flags & 1).astype(F32), 5) < 0.5
            else:
                up = (flags & 1) == 1
            c, g = face(w, m, tuple(shifted(m[i], i) for i in range(3)), k, kn, up, dep - shifted(dep, 4))
            lift, faces, beside = add(side, lift, faces, beside, c, g, shifted(p, 6))

        pack = halo_y[z]
        for side in range(2):
            edge = 0 if side == 0 else CY - 1
            inside = (iy > 0) if side == 0 else (iy < NGY - 1)

            def shifted(f, n):
                moved = pltpu.roll(pack, (CY - n) % CY if side == 0 else CY - 1 - 8 - n, 1)
                return jnp.where(lane == edge, moved, pltpu.roll(f, 1 if side == 0 else CY - 1, 1))
            k = perm_ref[1, z]
            kn = shifted(k, 3)
            kn = jnp.where((lane == edge) & jnp.logical_not(inside), 0.0, kn)
            if side == 0:
                up = shifted(((flags >> 1) & 1).astype(F32), 5) < 0.5
            else:
                up = ((flags >> 1) & 1) == 1
            c, g = face(w, m, tuple(shifted(m[i], i) for i in range(3)), k, kn, up, dep - shifted(dep, 4))
            lift, faces, beside = add(2 + side, lift, faces, beside, c, g, shifted(p, 6))

        for side in range(2):
            zn = jnp.maximum(z - 1, 0) if side == 0 else jnp.minimum(z + 1, NZ - 1)
            inside = (z > 0) if side == 0 else (z < NZ - 1)
            k = perm_ref[2, z]
            kn = jnp.where(inside, perm_ref[2, zn], 0.0)
            if side == 0:
                up = (flag_ref[zn] >> 2) == 0
            else:
                up = (flags >> 2) == 1
            c, g = face(w, m, (mob[0, zn], mob[1, zn], mob[2, zn]), k, kn, up, dep - dep_ref[zn])
            lift, faces, beside = add(4 + side, lift, faces, beside, c, g, p_ref[zn])

        combined = w[0] * res_ref[0, z] + w[1] * res_ref[1, z] + w[2] * res_ref[2, z]
        b = storage * p - combined + lift
        rows = pl.ds(pl.multiple_of(z * CX, CX), CX)
        damp = 0.8 / (storage + faces + wacc[rows, :])
        rhs[z] = b
        inv[z] = damp
        first = 0.2 * p + damp * (b + beside)
        pre[z] = first
        for n, part in enumerate(split(first) + split(damp)):
            fields[rows, n * CY:(n + 1) * CY] = part

    picked(2, 4)

    tm.arrive()
    for n in range(NGX):
        ctl[0, n:n + 1, :] = tm_all[n, 0:1, :]
        ctl[1, n:n + 1, :] = tm_all[n, 1:2, :]
    quarter = lax.broadcasted_iota(jnp.int32, (4, CY), 1) // 32
    quads = [[ctl[h, pl.ds(n, 4, stride=4), :] for n in range(4)] for h in range(2)]

    def placed(start):
        blocks = []
        for x in range(4):
            rows = jnp.zeros((4, CY), F32)
            for n in range(4):
                rows = jnp.where(quarter == n, pltpu.roll(quads[x // 2][n], (32 * n - start - 64 * (x % 2)) % CY, 1), rows)
            blocks.append(rows)
        return jnp.concatenate(blocks, axis=0)

    target, mode = placed(0), placed(32)

    def bhp_of(sums, base):
        return jnp.where(mode < 0.5, target, (sums - target) / base)

    def slot_flow(t):
        bh[t].arrive()
        wells = ball[t].reshape(32, CY)
        high, low = split(wells)
        g = jnp.dot(jnp.concatenate([high, low], axis=0), wlane[...], preferred_element_type=F32)
        slot_bhp = jnp.sum(jnp.where(well_rows, g[0:32] + g[32:64], 0.0), axis=0, keepdims=True)
        slotv[2:3, :] = slotv[1:2, :] * slot_bhp

    sums = finish_sums(0)
    base = sums[16:32]
    ball[0, core] = bhp_of(sums[0:16], base)
    bh[0].send()
    slot_flow(0)
    high, low = split(slotv[2:3, :])
    flow = jnp.concatenate([jnp.broadcast_to(high, (16, SLOTS)), jnp.broadcast_to(low, (16, SLOTS))], axis=0)
    met = jnp.dot(flow, same[...], preferred_element_type=F32)
    slotv[6:7, :] = slotv[1:2, :] * (slotv[4:5, :] + slotv[5:6, :] * (met[0:1, :] + met[16:17, :]))
    table1[...] = well_sums((6,))[0]
    rs[1].send()

    wacc[...] = scattered(2)

    @pl.loop(0, NZ)
    def _(z):
        rows = pl.ds(pl.multiple_of(z * CX, CX), CX)
        c = pre[z] + inv[z] * wacc[rows, :]
        cur[z] = c
        hx2_send[0, z] = c[0:1, :]
        hx2_send[1, z] = c[CX - 1:CX, :]
        packed = jnp.where(lane == 0, pltpu.roll(c, 1, 1), 0.0)
        halo_y[z] = jnp.where(lane == 8, pltpu.roll(c, 8, 1), packed)

    turned = halo_y[...].reshape(ROWS, CY).T
    hy2_send[1] = turned[0:8, :]
    hy2_send[0] = turned[8:16, :]
    for group in halo2:
        group.send()
    exchange(1)

    halo2[0].arrive()
    stacked = jnp.concatenate([hy2_recv[0], hy2_recv[1], jnp.zeros((CY - 16, ROWS), F32)], axis=0)
    halo_y[...] = stacked.T.reshape(NZ, CX, CY)

    @pl.loop(0, NZ)
    def _(z):
        c = cur[z]
        pack = halo_y[z]
        up_x = jnp.where(row == 0, jnp.broadcast_to(hx2_recv[0, z], (CX, CY)), pltpu.roll(c, 1, 0))
        down_x = jnp.where(row == CX - 1, jnp.broadcast_to(hx2_recv[1, z], (CX, CY)), pltpu.roll(c, CX - 1, 0))
        up_y = jnp.where(lane == 0, pack, pltpu.roll(c, 1, 1))
        down_y = jnp.where(lane == CY - 1, pltpu.roll(pack, CY - 9, 1), pltpu.roll(c, CY - 1, 1))
        up_z, down_z = cur[jnp.maximum(z - 1, 0)], cur[jnp.minimum(z + 1, NZ - 1)]
        total = rhs[z]
        for n, value in enumerate((up_x, down_x, up_y, down_y, up_z, down_z)):
            total = total + coup[n, z] * value
        pre[z] = 0.2 * c + inv[z] * total

    ball[1, core] = bhp_of(finish_sums(1), base)
    bh[1].send()
    slot_flow(1)
    out_ref[...] = pre[...] + inv[...] * scattered(2).reshape(NZ, CX, CY)

    line = lax.broadcasted_iota(jnp.int32, (16, CY), 0)
    wide = lax.broadcasted_iota(jnp.int32, (16, CY), 1)
    own = (line == chip_x * 4 + chip_y) & (wide // 32 == chip_z)
    mine = jnp.broadcast_to(jnp.sum(jnp.where(own, ball[1, core], 0.0), axis=0, keepdims=True), (8, CY))
    mine = mine + pltpu.roll(mine, 32, 1) + pltpu.roll(mine, 64, 1) + pltpu.roll(mine, 96, 1)
    bhp_ref[...] = mine[0:1, 0:32]

    remote(sent, sent, send_sem, recv_sem.at[0], partner).wait_send()


def hand_over(p_src, bhp_src, p_dst, bhp_dst, sem):
    copies = (pltpu.make_async_copy(p_src, p_dst, sem.at[0]), pltpu.make_async_copy(bhp_src, bhp_dst, sem.at[1]))
    for copy in copies:
        copy.start()
    for copy in copies:
        copy.wait()


def body(pressure, saturation, permeability, pore_volume, cell_depth, residual, upstream_flags,
         perf_cell, perf_well, perf_index, well_mode, well_target):
    grid = (NZ, CX, CY)
    vmem = pl.BlockSpec(memory_space=pltpu.VMEM)
    dma = pltpu.SemaphoreType.DMA
    new_pressure, well_bhp = pl.pallas_call(
        kernel,
        out_shape=(pltpu.VMEM(grid, F32), pltpu.VMEM((1, 32), F32)),
        in_specs=[pl.BlockSpec(memory_space=pl.ANY)] * 12,
        out_specs=(vmem, vmem),
        scratch_shapes=[
            pltpu.VMEM(grid, F32),
            pltpu.VMEM((2,) + grid, F32),
            pltpu.VMEM((3,) + grid, F32),
            pltpu.VMEM(grid, F32),
            pltpu.VMEM(grid, F32),
            pltpu.VMEM((3,) + grid, F32),
            pltpu.VMEM(grid, jnp.int32),
            pltpu.VMEM((1, SLOTS), jnp.int32),
            pltpu.VMEM((1, SLOTS), jnp.int32),
            pltpu.VMEM((1, SLOTS), F32),
            pltpu.VMEM((1, 32), jnp.int32),
            pltpu.VMEM((1, 32), F32),
            pltpu.VMEM((3,) + grid, F32),
            pltpu.VMEM((ROWS, SLOTS), BF16),
            pltpu.VMEM((ROWS, 4 * CY), BF16),
            pltpu.VMEM((CY, SLOTS), BF16),
            pltpu.VMEM((CY, SLOTS), BF16),
            pltpu.VMEM((32, SLOTS), BF16),
            pltpu.VMEM((128, SLOTS), BF16),
            pltpu.VMEM((SLOTS, SLOTS), BF16),
            pltpu.VMEM((6,) + grid, F32),
            pltpu.VMEM(grid, F32),
            pltpu.VMEM(grid, F32),
            pltpu.VMEM(grid, F32),
            pltpu.VMEM(grid, F32),
            pltpu.VMEM((ROWS, CY), F32),
            pltpu.VMEM((8, SLOTS), F32),
            pltpu.VMEM((2, 32, CY), F32),
            pltpu.VMEM((2, 16, CY), F32),
            pltpu.VMEM((NGY - 1, 32, CY), F32),
            pltpu.VMEM((NGY - 1, 16, CY), F32),
            pltpu.VMEM((32, CY), F32),
            pltpu.VMEM((16, CY), F32),
            pltpu.VMEM((NGX - 1, 32, CY), F32),
            pltpu.VMEM((NGX - 1, 16, CY), F32),
            pltpu.VMEM((2, CY), F32),
            pltpu.VMEM((3, 2, CY), F32),
            pltpu.VMEM((NGX, 2, CY), F32),
            pltpu.VMEM((2, NGX, CY), F32),
            pltpu.VMEM((2, 2, 16, CY), F32),
            pltpu.VMEM((2, 6, NZ, CY), F32),
            pltpu.VMEM((2, 6, NZ, CY), F32),
            pltpu.VMEM((2, 3, NZ, CY), F32),
            pltpu.VMEM((2, 8, ROWS), F32),
            pltpu.VMEM((2, 8, ROWS), F32),
            pltpu.VMEM((16, ROWS), F32),
            pltpu.VMEM(grid, F32),
            pltpu.VMEM((2, NZ, 1, CY), F32),
            pltpu.VMEM((2, NZ, 1, CY), F32),
            pltpu.VMEM((2, 8, ROWS), F32),
            pltpu.VMEM((2, 8, ROWS), F32),
            pltpu.VMEM((SENT_ROWS, 1, CY), F32),
            dma((6,)),
            dma,
            dma((10,)),
        ],
        compiler_params=pltpu.CompilerParams(collective_id=0, has_side_effects=True),
        name="cpr_step",
    )(pressure, saturation, permeability, pore_volume, cell_depth, residual, upstream_flags,
      perf_cell, perf_well, perf_index, well_mode.reshape(1, 32), well_target.reshape(1, 32))
    anywhere = pl.BlockSpec(memory_space=pl.ANY)
    new_pressure, well_bhp = pl.pallas_call(
        hand_over,
        out_shape=(jax.ShapeDtypeStruct(grid, F32), jax.ShapeDtypeStruct((1, 32), F32)),
        in_specs=[vmem] * 2,
        out_specs=(anywhere, anywhere),
        scratch_shapes=[dma((2,))],
        name="hand_over",
    )(pltpu.with_memory_space_constraint(new_pressure, pltpu.VMEM), pltpu.with_memory_space_constraint(well_bhp, pltpu.VMEM))
    return new_pressure, well_bhp.reshape(32)


def solution(mesh):
    areal, stacked, owned = P(None, "gx", "gy"), P(None, None, "gx", "gy"), P(("gx", "gy"))
    slots = P(("gx", "gy"), None)
    return jax.shard_map(
        body,
        mesh=mesh,
        in_specs=(areal, stacked, stacked, areal, areal, stacked, areal, slots, slots, slots, owned, owned),
        out_specs=(areal, owned),
        check_vma=False,
    )
```

```python
import jax
import jax.numpy as jnp
from jax import lax
from jax.experimental import pallas as pl
from jax.experimental.pallas import tpu as pltpu
from jax.sharding import PartitionSpec as P

MESH = pl.DeviceIdType.MESH
NZ, CX, CY = 12, 32, 128
ROWS = NZ * CX
SENT_ROWS = 7 * (32 + 16) + 15 * (32 + 16) + 2 * 16 + (3 + 15) * 2 + 2 * (6 * NZ + 24) + 2 * (NZ + 24)
SLOTS = 1024
NGX, NGY = 16, 8
GAMMA = (0.4, 0.5, 0.08)
F32, BF16 = jnp.float32, jnp.bfloat16
CONTRACT_LAST = (((1,), (1,)), ((), ()))
CONTRACT_FIRST = (((0,), (0,)), ((), ()))


def split(x):
    high = x.astype(BF16)
    return high, (x - high.astype(F32)).astype(BF16)


def phase_state(p, sw, sg):
    so = 1.0 - sw - sg
    bo = 1.0 + 0.2 * (p - 1.0)
    bw = 1.0 + 0.05 * (p - 1.0)
    return so, bo, bw


def phase_mobility(p, sw, sg):
    so, bo, bw = phase_state(p, sw, sg)
    return so * so * 0.5 * bo, sw * sw * bw, sg * sg * 5.0 * p


def hops(offset, size):
    return min(offset, size - offset)


GX_OFFSETS = sorted(((a, b) for a in range(4) for b in range(4) if a or b), key=lambda o: -hops(o[0], 4) - hops(o[1], 4))
GY_OFFSETS = sorted(((a, b) for a in range(4) for b in range(2) if a or b), key=lambda o: -2 * hops(o[0], 4) - o[1])


def kernel(
    p_hbm, sat_hbm, perm_hbm, pv_hbm, dep_hbm, res_hbm, flag_hbm, pc_hbm, pw_hbm, pi_hbm, wm_hbm, wt_hbm,
    out_ref, bhp_ref,
    p_ref, sat_ref, perm_ref, pv_ref, dep_ref, res_ref, flag_ref, pc_ref, pw_ref, pi_ref, wm_ref, wt_ref,
    mob, onehot, fields, wlane, clane, wrow, wpart, same, coup, pre, inv, rhs, cur, wacc, slotv,
    table0, table1, rs_recv0, rs_recv1, xs_src0, xs_src1, xs_recv0, xs_recv1, pair_src, pair_recv, tm_all, ctl, ball,
    hx_send, hx_recv, hx_mob, hy_send, hy_recv, hy_rows, halo_y, hx2_send, hx2_recv, hy2_send, hy2_recv, sent,
    in_sem, send_sem, recv_sem,
):
    ix, iy = lax.axis_index("gx"), lax.axis_index("gy")
    chip_y, chip_z = ix // 4, lax.rem(ix, 4)
    chip_x, core = iy // 2, lax.rem(iy, 2)

    def gx_of(a, b):
        return lax.rem(chip_y + a, 4) * 4 + lax.rem(chip_z + b, 4)

    def gy_of(a, b):
        return lax.rem(chip_x + a, 4) * 2 + lax.rem(core + b, 2)

    loads = (
        ((pc_hbm, pc_ref), (pw_hbm, pw_ref), (pi_hbm, pi_ref)),
        ((sat_hbm.at[0], sat_ref.at[0]), (sat_hbm.at[1], sat_ref.at[1]), (p_hbm, p_ref)),
        ((wm_hbm, wm_ref),),
        ((perm_hbm, perm_ref), (dep_hbm, dep_ref), (flag_hbm, flag_ref)),
        ((pv_hbm, pv_ref), (res_hbm, res_ref)),
        ((wt_hbm, wt_ref),),
    )
    sizes = (slotv.at[0:3], perm_ref, wm_ref, coup.at[0:5], coup.at[0:4], wt_ref)

    def load(n):
        for src, dst in loads[n]:
            pltpu.make_async_copy(src, dst, in_sem.at[n]).start()

    def loaded(n):
        pltpu.make_async_copy(sizes[n], sizes[n], in_sem.at[n]).wait()

    load(0)
    load(1)

    barrier = pltpu.get_barrier_semaphore()
    for a, b in GX_OFFSETS:
        pl.semaphore_signal(barrier, inc=1, device_id=(gx_of(a, b), iy), device_id_type=MESH)
    for a, b in GY_OFFSETS:
        pl.semaphore_signal(barrier, inc=1, device_id=(ix, gy_of(a, b)), device_id_type=MESH)

    for n in (2, 5, 3, 4):
        load(n)

    lane = lax.broadcasted_iota(jnp.int32, (CX, CY), 1)
    row = lax.broadcasted_iota(jnp.int32, (CX, CY), 0)

    def remote(src, dst, ss, rs, dev):
        return pltpu.make_async_remote_copy(src_ref=src, dst_ref=dst, send_sem=ss, recv_sem=rs,
                                            device_id=dev, device_id_type=MESH)

    table, rs_recv = (table0, table1), (rs_recv0, rs_recv1)
    xs_src, xs_recv = (xs_src0, xs_src1), (xs_recv0, xs_recv1)

    partner = (ix, gy_of(0, 1))
    x_peers = ((2, 0), (1, 0), (3, 0))

    class Group:
        def __init__(self, sem, copies, whole):
            self.copies = [remote(src, dst, send_sem, recv_sem.at[sem], dev) for src, dst, dev in copies]
            self.whole = (whole, whole, send_sem, recv_sem.at[sem], copies[0][2])

        def send(self):
            for copy in self.copies:
                copy.start()

        def arrive(self):
            remote(*self.whole).wait_recv()

    rs = [Group(t, [(table[t].at[lax.rem(core + b, 2)], rs_recv[t].at[n], (ix, gy_of(a, b))) for n, (a, b) in enumerate(GY_OFFSETS)],
                rs_recv[t]) for t in range(2)]
    xs = [Group(2 + t, [(xs_src[t], xs_recv[t].at[n], (gx_of(a, b), iy)) for n, (a, b) in enumerate(GX_OFFSETS)],
                xs_recv[t]) for t in range(2)]
    bh = [Group(4 + t, [(ball.at[t, core], ball.at[t, core], partner)], ball.at[t, 1 - core])
          for t in range(2)]
    pair = Group(6, [(pair_src, pair_recv.at[n], (ix, gy_of(a, b))) for n, (a, b) in enumerate(x_peers)], pair_recv)
    tm = Group(7, [(tm_all.at[ix], tm_all.at[ix], (gx_of(a, b), iy)) for a, b in GX_OFFSETS], tm_all.at[0:NGX - 1])

    def halo_groups(sem, xs, xr, ys, yr, size):
        after, before = (lax.rem(ix + 1, NGX), iy), (lax.rem(ix + NGX - 1, NGX), iy)
        right, left = (ix, lax.rem(iy + 1, NGY)), (ix, lax.rem(iy + NGY - 1, NGY))
        return (Group(sem, [(xs.at[1], xr.at[0], after), (xs.at[0], xr.at[1], before)], size),
                Group(sem, [(ys.at[1], yr.at[0], right), (ys.at[0], yr.at[1], left)], size))

    halo1 = halo_groups(8, hx_send, hx_recv, hy_send, hy_recv, coup.at[0, 0:6])
    halo2 = halo_groups(9, hx2_send, hx2_recv, hy2_send, hy2_recv, hx_mob)

    loaded(0)
    cell = pc_ref[...]
    cell_row = cell >> 7
    live = pw_ref[...] >= 0
    well = jnp.where(live, pw_ref[...], 0)
    owner = well >> 5
    well_row = (owner & 1) * 16 + ((owner >> 1) & 3) * 4 + (owner >> 5)
    well_lane = ((owner >> 3) & 3) * 32 + (well & 31)
    well_rows = lax.broadcasted_iota(jnp.int32, (32, SLOTS), 0) == well_row
    wrow[...] = jnp.where(well_rows, 1.0, 0.0).astype(BF16)
    slotv[0:1, :] = jnp.where(live, pi_ref[...], 0.0)

    @pl.loop(0, NZ)
    def _(z):
        ids = lax.broadcasted_iota(jnp.int32, (CX, SLOTS), 0) + z * CX
        onehot[pl.ds(pl.multiple_of(z * CX, CX), CX), :] = jnp.where(ids == cell_row, 1.0, 0.0).astype(BF16)

    wlane[...] = jnp.where(lax.broadcasted_iota(jnp.int32, (CY, SLOTS), 0) == well_lane, 1.0, 0.0).astype(BF16)

    clane[...] = jnp.where(lax.broadcasted_iota(jnp.int32, (CY, SLOTS), 0) == (cell & 127), 1.0, 0.0).astype(BF16)

    loaded(1)

    @pl.loop(0, NZ)
    def _(z):
        sw, sg = sat_ref[0, z], sat_ref[1, z]
        so = 1.0 - sw - sg
        total = so * so * 0.5 + sw * sw + sg * sg * 5.0
        rows = pl.ds(pl.multiple_of(z * CX, CX), CX)
        for n, part in enumerate(split(total) + split(p_ref[z])):
            fields[rows, n * CY:(n + 1) * CY] = part

    sub256 = lax.broadcasted_iota(jnp.int32, (CY, 256), 0)

    def picked(count, dst):
        for j in range(SLOTS // 256):
            chunk = slice(j * 256, (j + 1) * 256)
            g = lax.dot_general(fields[...], onehot[:, chunk], CONTRACT_FIRST, preferred_element_type=F32)
            mask = sub256 == (pc_ref[0:1, chunk] & 127)
            for n in range(count):
                both = g[2 * n * CY:(2 * n + 1) * CY] + g[(2 * n + 1) * CY:(2 * n + 2) * CY]
                slotv[dst + n:dst + n + 1, chunk] = jnp.sum(jnp.where(mask, both, 0.0), axis=0, keepdims=True)

    def scattered(value_row):
        total = None
        for j in range(SLOTS // 256):
            chunk = slice(j * 256, (j + 1) * 256)
            high, low = split(slotv[value_row:value_row + 1, chunk])
            spread = jnp.concatenate([clane[:, chunk] * high, clane[:, chunk] * low], axis=0)
            part = lax.dot_general(onehot[:, chunk], spread, CONTRACT_LAST, preferred_element_type=F32)
            total = part if total is None else total + part
        return total[:, 0:CY] + total[:, CY:2 * CY]

    def well_sums(value_rows):
        for n, value_row in enumerate(value_rows):
            high, low = split(slotv[value_row:value_row + 1, :])
            wpart[64 * n:64 * n + 32, :] = wrow[...] * high
            wpart[64 * n + 32:64 * n + 64, :] = wrow[...] * low
        both = lax.dot_general(wpart[0:64 * len(value_rows), :], wlane[...], CONTRACT_LAST, preferred_element_type=F32)
        return [(both[64 * n:64 * n + 32] + both[64 * n + 32:64 * n + 64]).reshape(2, 16, CY) for n in range(len(value_rows))]

    picked(2, 4)
    factor = slotv[0:1, :] * slotv[4:5, :]
    slotv[1:2, :] = factor
    slotv[2:3, :] = factor * slotv[5:6, :]
    for n, sums in enumerate(well_sums((2, 1))):
        table0[:, 16 * n:16 * n + 16, :] = sums

    loaded(2)
    loaded(5)
    pair_lane = lax.broadcasted_iota(jnp.int32, (2, CY), 1)
    pair_row = lax.broadcasted_iota(jnp.int32, (2, CY), 0)
    target4 = jnp.broadcast_to(jnp.concatenate([wt_ref[...]] * 4, axis=1), (2, CY))
    mode4 = jnp.broadcast_to(jnp.concatenate([wm_ref[...].astype(F32)] * 4, axis=1), (2, CY))
    both = jnp.where((pair_lane // 32) % 2 == 0, target4, mode4)
    pair_src[...] = jnp.where((pair_row == chip_x // 2) & (pair_lane // 64 == lax.rem(chip_x, 2)), both, 0.0)

    pl.semaphore_wait(barrier, NGX + NGY - 2)

    def exchange(t):
        rs[t].arrive()
        part = table[t][core]
        for n in range(NGY - 1):
            part = part + rs_recv[t][n]
        xs_src[t][...] = part
        xs[t].send()

    def finish_sums(t):
        xs[t].arrive()
        total = xs_src[t][...]
        for n in range(NGX - 1):
            total = total + xs_recv[t][n]
        return total

    pair.send()
    rs[0].send()

    loaded(3)
    for z in range(NZ):
        for side, edge in enumerate((0, CX - 1)):
            at = slice(edge, edge + 1)
            rim = (p_ref[z, at, :], sat_ref[0, z, at, :], sat_ref[1, z, at, :], perm_ref[0, z, at, :], dep_ref[z, at, :],
                   (flag_ref[z, at, :] & 1).astype(F32))
            for n, f in enumerate(rim):
                hx_send[side, n, z:z + 1, :] = f
    halo1[0].send()

    @pl.loop(0, NZ)
    def _(z):
        rim = (p_ref[z], sat_ref[0, z], sat_ref[1, z], perm_ref[1, z], dep_ref[z], ((flag_ref[z] >> 1) & 1).astype(F32))
        packed = jnp.zeros((CX, CY), F32)
        for n, f in enumerate(rim):
            packed = jnp.where(lane == n, pltpu.roll(f, (n + 1) % CY, 1), packed)
            packed = jnp.where(lane == 8 + n, pltpu.roll(f, 8 + n, 1), packed)
        halo_y[z] = packed

    turned = halo_y[...].reshape(ROWS, CY).T
    hy_send[1] = turned[0:8, :]
    hy_send[0] = turned[8:16, :]
    halo1[1].send()

    @pl.loop(0, NZ)
    def _(z):
        p, sw, sg = p_ref[z], sat_ref[0, z], sat_ref[1, z]
        for c, m in enumerate(phase_mobility(p, sw, sg)):
            mob[c, z] = m

    cells = jnp.broadcast_to(pc_ref[...].astype(F32), (CY, SLOTS)).T
    for j in range(SLOTS // CY):
        chunk = slice(j * CY, (j + 1) * CY)
        same[:, chunk] = jnp.where(cells == pc_ref[0:1, chunk].astype(F32), 1.0, 0.0).astype(BF16)

    wacc[...] = scattered(1)
    pair.arrive()
    tm_all[ix] = pair_src[...] + pair_recv[0] + pair_recv[1] + pair_recv[2]
    tm.send()
    exchange(0)

    loaded(4)
    halo1[0].arrive()
    for side in range(2):
        for c, m in enumerate(phase_mobility(hx_recv[side, 0], hx_recv[side, 1], hx_recv[side, 2])):
            hx_mob[side, c] = m
        got = hy_recv[side]
        beside = phase_mobility(got[0:1], got[1:2], got[2:3]) + (got[3:4], got[4:5], got[5:6], got[0:1], got[7:8])
        for n, f in enumerate(beside):
            hy_rows[8 * side + n:8 * side + n + 1, :] = f
    stacked = jnp.concatenate([hy_rows[...], jnp.zeros((CY - 16, ROWS), F32)], axis=0)
    halo_y[...] = stacked.T.reshape(NZ, CX, CY)

    def face(w, m, n, k, kn, up, drop):
        trans = 2.0 * k * kn / (k + kn)
        c = jnp.zeros((CX, CY), F32)
        g = jnp.zeros((CX, CY), F32)
        for i in range(3):
            flux = w[i] * jnp.where(up, m[i], n[i])
            c = c + flux
            g = g + GAMMA[i] * flux
        c = c * trans
        return c, g * (trans * drop)

    @pl.loop(0, NZ)
    def _(z):
        p, sw, sg = p_ref[z], sat_ref[0, z], sat_ref[1, z]
        so, bo, bw = phase_state(p, sw, sg)
        w = (1.0 / bo, 1.0 / bw, 1.0 / p)
        m = (mob[0, z], mob[1, z], mob[2, z])
        dep = dep_ref[z]
        flags = flag_ref[z]
        storage = pv_ref[z] * (so * 0.2 * w[0] + sw * 0.05 * w[1] + sg * w[2])
        lift = jnp.zeros((CX, CY), F32)
        faces = jnp.zeros((CX, CY), F32)
        beside = jnp.zeros((CX, CY), F32)

        def add(n, lift, faces, beside, c, g, pn):
            coup[n, z] = c
            return lift + g, faces + c, beside + c * pn

        for side in range(2):
            here = pl.ds(z, 1)
            halo = [hx_mob[side, c, here, :] for c in range(3)] + [hx_recv[side, n, here, :] for n in (3, 4, 5, 0)]
            edge = 0 if side == 0 else CX - 1
            inside = (ix > 0) if side == 0 else (ix < NGX - 1)

            def shifted(f, n):
                return jnp.where(row == edge, jnp.broadcast_to(halo[n], (CX, CY)), pltpu.roll(f, 1 if side == 0 else CX - 1, 0))
            k = perm_ref[0, z]
            kn = shifted(k, 3)
            kn = jnp.where((row == edge) & jnp.logical_not(inside), 0.0, kn)
            if side == 0:
                up = shifted((flags & 1).astype(F32), 5) < 0.5
            else:
                up = (flags & 1) == 1
            c, g = face(w, m, tuple(shifted(m[i], i) for i in range(3)), k, kn, up, dep - shifted(dep, 4))
            lift, faces, beside = add(side, lift, faces, beside, c, g, shifted(p, 6))

        pack = halo_y[z]
        for side in range(2):
            edge = 0 if side == 0 else CY - 1
            inside = (iy > 0) if side == 0 else (iy < NGY - 1)

            def shifted(f, n):
                moved = pltpu.roll(pack, (CY - n) % CY if side == 0 else CY - 1 - 8 - n, 1)
                return jnp.where(lane == edge, moved, pltpu.roll(f, 1 if side == 0 else CY - 1, 1))
            k = perm_ref[1, z]
            kn = shifted(k, 3)
            kn = jnp.where((lane == edge) & jnp.logical_not(inside), 0.0, kn)
            if side == 0:
                up = shifted(((flags >> 1) & 1).astype(F32), 5) < 0.5
            else:
                up = ((flags >> 1) & 1) == 1
            c, g = face(w, m, tuple(shifted(m[i], i) for i in range(3)), k, kn, up, dep - shifted(dep, 4))
            lift, faces, beside = add(2 + side, lift, faces, beside, c, g, shifted(p, 6))

        for side in range(2):
            zn = jnp.maximum(z - 1, 0) if side == 0 else jnp.minimum(z + 1, NZ - 1)
            inside = (z > 0) if side == 0 else (z < NZ - 1)
            k = perm_ref[2, z]
            kn = jnp.where(inside, perm_ref[2, zn], 0.0)
            if side == 0:
                up = (flag_ref[zn] >> 2) == 0
            else:
                up = (flags >> 2) == 1
            c, g = face(w, m, (mob[0, zn], mob[1, zn], mob[2, zn]), k, kn, up, dep - dep_ref[zn])
            lift, faces, beside = add(4 + side, lift, faces, beside, c, g, p_ref[zn])

        combined = w[0] * res_ref[0, z] + w[1] * res_ref[1, z] + w[2] * res_ref[2, z]
        b = storage * p - combined + lift
        rows = pl.ds(pl.multiple_of(z * CX, CX), CX)
        damp = 0.8 / (storage + faces + wacc[rows, :])
        rhs[z] = b
        inv[z] = damp
        first = 0.2 * p + damp * (b + beside)
        pre[z] = first
        for n, part in enumerate(split(first) + split(damp)):
            fields[rows, n * CY:(n + 1) * CY] = part

    picked(2, 4)

    tm.arrive()
    for n in range(NGX):
        ctl[0, n:n + 1, :] = tm_all[n, 0:1, :]
        ctl[1, n:n + 1, :] = tm_all[n, 1:2, :]
    quarter = lax.broadcasted_iota(jnp.int32, (4, CY), 1) // 32
    quads = [[ctl[h, pl.ds(n, 4, stride=4), :] for n in range(4)] for h in range(2)]

    def placed(start):
        blocks = []
        for x in range(4):
            rows = jnp.zeros((4, CY), F32)
            for n in range(4):
                rows = jnp.where(quarter == n, pltpu.roll(quads[x // 2][n], (32 * n - start - 64 * (x % 2)) % CY, 1), rows)
            blocks.append(rows)
        return jnp.concatenate(blocks, axis=0)

    target, mode = placed(0), placed(32)

    def bhp_of(sums, base):
        return jnp.where(mode < 0.5, target, (sums - target) / base)

    def slot_flow(t):
        bh[t].arrive()
        wells = ball[t].reshape(32, CY)
        high, low = split(wells)
        both = jnp.concatenate([high, low], axis=0)
        for j in range(SLOTS // 256):
            chunk = slice(j * 256, (j + 1) * 256)
            g = jnp.dot(both, wlane[:, chunk], preferred_element_type=F32)
            slot_bhp = jnp.sum(jnp.where(well_rows[:, chunk], g[0:32] + g[32:64], 0.0), axis=0, keepdims=True)
            slotv[2:3, chunk] = slotv[1:2, chunk] * slot_bhp

    sums = finish_sums(0)
    base = sums[16:32]
    ball[0, core] = bhp_of(sums[0:16], base)
    bh[0].send()
    slot_flow(0)
    high, low = split(slotv[2:3, :])
    upper = lax.broadcasted_iota(jnp.int32, (16, SLOTS), 0) < 8
    flow = jnp.where(upper, high.astype(F32), low.astype(F32)).astype(BF16)
    met = jnp.dot(flow, same[...], preferred_element_type=F32)
    slotv[6:7, :] = slotv[1:2, :] * (slotv[4:5, :] + slotv[5:6, :] * (met[0:1, :] + met[8:9, :]))
    table1[...] = well_sums((6,))[0]
    rs[1].send()

    wacc[...] = scattered(2)

    @pl.loop(0, NZ)
    def _(z):
        rows = pl.ds(pl.multiple_of(z * CX, CX), CX)
        c = pre[z] + inv[z] * wacc[rows, :]
        cur[z] = c
        hx2_send[0, z] = c[0:1, :]
        hx2_send[1, z] = c[CX - 1:CX, :]
        packed = jnp.where(lane == 0, pltpu.roll(c, 1, 1), 0.0)
        halo_y[z] = jnp.where(lane == 8, pltpu.roll(c, 8, 1), packed)

    turned = halo_y[...].reshape(ROWS, CY).T
    hy2_send[1] = turned[0:8, :]
    hy2_send[0] = turned[8:16, :]
    for group in halo2:
        group.send()
    exchange(1)

    halo2[0].arrive()
    stacked = jnp.concatenate([hy2_recv[0], hy2_recv[1], jnp.zeros((CY - 16, ROWS), F32)], axis=0)
    halo_y[...] = stacked.T.reshape(NZ, CX, CY)

    @pl.loop(0, NZ)
    def _(z):
        c = cur[z]
        pack = halo_y[z]
        up_x = jnp.where(row == 0, jnp.broadcast_to(hx2_recv[0, z], (CX, CY)), pltpu.roll(c, 1, 0))
        down_x = jnp.where(row == CX - 1, jnp.broadcast_to(hx2_recv[1, z], (CX, CY)), pltpu.roll(c, CX - 1, 0))
        up_y = jnp.where(lane == 0, pack, pltpu.roll(c, 1, 1))
        down_y = jnp.where(lane == CY - 1, pltpu.roll(pack, CY - 9, 1), pltpu.roll(c, CY - 1, 1))
        up_z, down_z = cur[jnp.maximum(z - 1, 0)], cur[jnp.minimum(z + 1, NZ - 1)]
        total = rhs[z]
        for n, value in enumerate((up_x, down_x, up_y, down_y, up_z, down_z)):
            total = total + coup[n, z] * value
        pre[z] = 0.2 * c + inv[z] * total

    ball[1, core] = bhp_of(finish_sums(1), base)
    bh[1].send()
    slot_flow(1)
    out_ref[...] = pre[...] + inv[...] * scattered(2).reshape(NZ, CX, CY)

    line = lax.broadcasted_iota(jnp.int32, (16, CY), 0)
    wide = lax.broadcasted_iota(jnp.int32, (16, CY), 1)
    own = (line == chip_x * 4 + chip_y) & (wide // 32 == chip_z)
    mine = jnp.broadcast_to(jnp.sum(jnp.where(own, ball[1, core], 0.0), axis=0, keepdims=True), (8, CY))
    mine = mine + pltpu.roll(mine, 32, 1) + pltpu.roll(mine, 64, 1) + pltpu.roll(mine, 96, 1)
    bhp_ref[...] = mine[0:1, 0:32]

    remote(sent, sent, send_sem, recv_sem.at[0], partner).wait_send()


def hand_over(p_src, bhp_src, p_dst, bhp_dst, sem):
    copies = (pltpu.make_async_copy(p_src, p_dst, sem.at[0]), pltpu.make_async_copy(bhp_src, bhp_dst, sem.at[1]))
    for copy in copies:
        copy.start()
    for copy in copies:
        copy.wait()


def body(pressure, saturation, permeability, pore_volume, cell_depth, residual, upstream_flags,
         perf_cell, perf_well, perf_index, well_mode, well_target):
    grid = (NZ, CX, CY)
    vmem = pl.BlockSpec(memory_space=pltpu.VMEM)
    dma = pltpu.SemaphoreType.DMA
    new_pressure, well_bhp = pl.pallas_call(
        kernel,
        out_shape=(pltpu.VMEM(grid, F32), pltpu.VMEM((1, 32), F32)),
        in_specs=[pl.BlockSpec(memory_space=pl.ANY)] * 12,
        out_specs=(vmem, vmem),
        scratch_shapes=[
            pltpu.VMEM(grid, F32),
            pltpu.VMEM((2,) + grid, F32),
            pltpu.VMEM((3,) + grid, F32),
            pltpu.VMEM(grid, F32),
            pltpu.VMEM(grid, F32),
            pltpu.VMEM((3,) + grid, F32),
            pltpu.VMEM(grid, jnp.int32),
            pltpu.VMEM((1, SLOTS), jnp.int32),
            pltpu.VMEM((1, SLOTS), jnp.int32),
            pltpu.VMEM((1, SLOTS), F32),
            pltpu.VMEM((1, 32), jnp.int32),
            pltpu.VMEM((1, 32), F32),
            pltpu.VMEM((3,) + grid, F32),
            pltpu.VMEM((ROWS, SLOTS), BF16),
            pltpu.VMEM((ROWS, 4 * CY), BF16),
            pltpu.VMEM((CY, SLOTS), BF16),
            pltpu.VMEM((CY, SLOTS), BF16),
            pltpu.VMEM((32, SLOTS), BF16),
            pltpu.VMEM((128, SLOTS), BF16),
            pltpu.VMEM((SLOTS, SLOTS), BF16),
            pltpu.VMEM((6,) + grid, F32),
            pltpu.VMEM(grid, F32),
            pltpu.VMEM(grid, F32),
            pltpu.VMEM(grid, F32),
            pltpu.VMEM(grid, F32),
            pltpu.VMEM((ROWS, CY), F32),
            pltpu.VMEM((8, SLOTS), F32),
            pltpu.VMEM((2, 32, CY), F32),
            pltpu.VMEM((2, 16, CY), F32),
            pltpu.VMEM((NGY - 1, 32, CY), F32),
            pltpu.VMEM((NGY - 1, 16, CY), F32),
            pltpu.VMEM((32, CY), F32),
            pltpu.VMEM((16, CY), F32),
            pltpu.VMEM((NGX - 1, 32, CY), F32),
            pltpu.VMEM((NGX - 1, 16, CY), F32),
            pltpu.VMEM((2, CY), F32),
            pltpu.VMEM((3, 2, CY), F32),
            pltpu.VMEM((NGX, 2, CY), F32),
            pltpu.VMEM((2, NGX, CY), F32),
            pltpu.VMEM((2, 2, 16, CY), F32),
            pltpu.VMEM((2, 6, NZ, CY), F32),
            pltpu.VMEM((2, 6, NZ, CY), F32),
            pltpu.VMEM((2, 3, NZ, CY), F32),
            pltpu.VMEM((2, 8, ROWS), F32),
            pltpu.VMEM((2, 8, ROWS), F32),
            pltpu.VMEM((16, ROWS), F32),
            pltpu.VMEM(grid, F32),
            pltpu.VMEM((2, NZ, 1, CY), F32),
            pltpu.VMEM((2, NZ, 1, CY), F32),
            pltpu.VMEM((2, 8, ROWS), F32),
            pltpu.VMEM((2, 8, ROWS), F32),
            pltpu.VMEM((SENT_ROWS, 1, CY), F32),
            dma((6,)),
            dma,
            dma((10,)),
        ],
        compiler_params=pltpu.CompilerParams(collective_id=0, has_side_effects=True),
        name="cpr_step",
    )(pressure, saturation, permeability, pore_volume, cell_depth, residual, upstream_flags,
      perf_cell, perf_well, perf_index, well_mode.reshape(1, 32), well_target.reshape(1, 32))
    anywhere = pl.BlockSpec(memory_space=pl.ANY)
    new_pressure, well_bhp = pl.pallas_call(
        hand_over,
        out_shape=(jax.ShapeDtypeStruct(grid, F32), jax.ShapeDtypeStruct((1, 32), F32)),
        in_specs=[vmem] * 2,
        out_specs=(anywhere, anywhere),
        scratch_shapes=[dma((2,))],
        name="hand_over",
    )(pltpu.with_memory_space_constraint(new_pressure, pltpu.VMEM), pltpu.with_memory_space_constraint(well_bhp, pltpu.VMEM))
    return new_pressure, well_bhp.reshape(32)


def solution(mesh):
    areal, stacked, owned = P(None, "gx", "gy"), P(None, None, "gx", "gy"), P(("gx", "gy"))
    slots = P(("gx", "gy"), None)
    return jax.shard_map(
        body,
        mesh=mesh,
        in_specs=(areal, stacked, stacked, areal, areal, stacked, areal, slots, slots, slots, owned, owned),
        out_specs=(areal, owned),
        check_vma=False,
    )
```
